256 devices in a mesh: seq: 4 (over x), ctx: 64 (over z, y, core).
Axes of the slice: x: 4, y: 4, z: 8, core: 2. Of those that a mesh axis runs over, the one named last changes fastest.
Arguments:
- queries: bfloat16 [32768, 2048], P(('seq', 'ctx')), parts along dimension 0, may hold values from -1 to 1
- keys_in: bfloat16 [32768, 2048], P(('seq', 'ctx')), parts along dimension 0, may hold values from -1 to 1
- value_input: bfloat16 [32768, 2048], P(('seq', 'ctx')), parts along dimension 0, may hold values from -1 to 1
- level_gain: float32 [14, 16, 32768], P(None, None, ('seq', 'ctx')), parts along dimension 2, may hold values from 0.2 to 2
- decay_log: float32 [16, 32768], P(None, ('seq', 'ctx')), parts along dimension 1, may hold values from -0.7 to 0, as said below
- out_grad: bfloat16 [32768, 2048], P(('seq', 'ctx')), parts along dimension 0, may hold values from -1 to 1
Outputs:
- mixed_out: bfloat16 [32768, 2048], P(('seq', 'ctx')), parts along dimension 0
- query_gradient: bfloat16 [32768, 2048], P(('seq', 'ctx')), parts along dimension 0
- grad_keys: bfloat16 [32768, 2048], P(('seq', 'ctx')), parts along dimension 0
- grad_values: bfloat16 [32768, 2048], P(('seq', 'ctx')), parts along dimension 0
- grad_gain: float32 [14, 16, 32768], P(None, None, ('seq', 'ctx')), parts along dimension 2
- grad_decay: float32 [16, 32768], P(None, ('seq', 'ctx')), parts along dimension 1
The draws below stay inside these ranges and needn't reach their ends.
There are 4 independent parts, one for each index of `seq`. The reference program is written for one: setup_inputs(seed, part) draws one part's arguments, and reference() takes and returns one part's arrays. A program takes and returns all parts, laid end to end along the dimension named above; each array names one. Nothing has to cross between parts.
Inputs may be any that keep to these rules, and one draw needn't show every extreme that they name: `decay_log`: every entry is negative.
All inputs are finite; a program needn't handle non-finite values.
Results may differ from the reference program's by a relative error of at most 0.001.
Values sent between devices are 32-bit elements; how exact they have to be, the bound alone decides.
A program may use at most 128 MiB of HBM per device.

```python
import math
import jax
import jax.numpy as jnp
from jax import lax

H = 16
HEAD = 128
TOK_DEV = 128
LEN = 8192
XLEV = 6
LEVELS = 14
N_CTX = 64


def draw_decay_log(key, part):
    pieces = jax.random.split(key, 8)
    log_high = jnp.log(jnp.float32(1.0 / 30.0))
    log_low = jnp.log(jnp.float32(0.01 / LEN))
    order = jax.random.permutation(pieces[0], H).astype(jnp.float32)
    place = (order + jax.random.uniform(pieces[1], (H,), jnp.float32)) / H
    rate = jnp.exp(log_low + place * (log_high - log_low))
    blocks = LEN // TOK_DEV
    block_factor = jnp.repeat(jax.random.uniform(pieces[3], (H, blocks), jnp.float32, 0.5, 1.5), TOK_DEV, axis=1)
    token_factor = jax.random.uniform(pieces[4], (H, LEN), jnp.float32, 0.5, 1.5)
    base = -rate[:, None] * block_factor * token_factor
    first_spot = jax.random.randint(pieces[5], (H,), 0, LEN)
    second_location = (first_spot + 1 + jax.random.randint(pieces[6], (H,), 0, LEN - 1)) % LEN
    loss_share = jax.random.uniform(pieces[7], (H, 2), jnp.float32, 0.2, 0.5)
    places = jnp.arange(LEN)
    first_hit = places[None, :] == first_spot[:, None]
    second_hit = places[None, :] == second_location[:, None]
    with_first = jnp.where(first_hit, jnp.log1p(-loss_share[:, 0])[:, None], base)
    return jnp.where(second_hit, jnp.log1p(-loss_share[:, 1])[:, None], with_first)


def steps_of(rng, shape, cuts, least, top_value):
    def one(position, parts):
        heights = jax.random.uniform(jax.random.fold_in(jax.random.fold_in(rng, 6), position), (parts,), jnp.float32, least / len(cuts), top_value / len(cuts))
        return jnp.repeat(jnp.exp(heights), shape[position] // parts).reshape((-1,) + (1,) * (len(shape) - position - 1))

    factor_of = one(*cuts[0])
    for cut in cuts[1:]:
        factor_of = factor_of * one(*cut)
    return factor_of


def scatter_about(rng, shape, width, most, cuts=(), kind=jnp.bfloat16):
    values = jax.random.normal(rng, shape, jnp.float32) * width
    if len(cuts) > 0:
        values = steps_of(rng, shape, cuts, -0.22, 0.18) * values
    return jnp.clip(values, min=-most, max=most).astype(kind)


def setup_inputs(seed: int = 0, part: int = 0) -> dict:
    arg_keys = jax.random.split(jax.random.key(seed), 7)
    part_splits = jax.random.split(jax.random.fold_in(arg_keys[6], part), 7)
    return {
        "queries": scatter_about(part_splits[0], (LEN, H * HEAD), 0.18, 1.0, ((0, 64),)),
        "keys_in": scatter_about(part_splits[1], (LEN, H * HEAD), 0.18, 1.0, ((0, 64),)),
        "value_input": scatter_about(part_splits[2], (LEN, H * HEAD), 0.18, 1.0, ((0, 64),)),
        "level_gain": jnp.clip(jnp.exp(math.log(2.0) - 2.3025851 * jax.random.uniform(part_splits[3], (LEVELS, H, LEN), jnp.float32) ** steps_of(part_splits[3], (LEVELS, H, LEN), ((2, 64),), -0.2, 0.2)), 0.2, 2.0),
        "decay_log": draw_decay_log(jax.random.fold_in(jax.random.fold_in(arg_keys[6], part), 71), part),
        "out_grad": scatter_about(part_splits[5], (LEN, H * HEAD), 0.18, 1.0, ((0, 64),)),
    }


TOP_ACCURACY = lax.Precision.HIGHEST

def level_table(tok, lvl_in):
    places = jnp.arange(tok, dtype=jnp.int32)
    mixing = jnp.bitwise_xor(places[:, None], places[None, :])
    table = jnp.zeros((tok, tok), jnp.int32)
    for power in range(lvl_in):
        table = table + (mixing >= 2 ** power).astype(jnp.int32)
    return table

def block_front(keys_h, value_rows_head, decay):
    running = jnp.cumsum(decay, axis=1)
    total_sum = running[:, -1]
    scaled_result = keys_h * jnp.exp(total_sum[:, None] - running)[:, :, None]
    return (jnp.einsum('ybu,ybe->yue', scaled_result, value_rows_head, precision=TOP_ACCURACY), total_sum)

def block_output(queries_h, keys_h, value_rows_head, gain, decay, buckets):
    tok = queries_h.shape[1]
    lvl_in = tok.bit_length() - 1
    running = jnp.cumsum(decay, axis=1)
    places = jnp.arange(tok, dtype=jnp.int32)
    causal = places[:, None] >= places[None, :]
    spread_gap = jnp.where(causal[None], running[:, :, None] - running[:, None, :], 0.0)
    fading = jnp.where(causal[None], jnp.exp(spread_gap), 0.0)
    table = level_table(tok, lvl_in)
    picks = (table[None] == jnp.arange(lvl_in + 1, dtype=jnp.int32)[:, None, None]).astype(jnp.float32)
    weighting = jnp.einsum('lij,lhi->hij', picks, gain[:lvl_in + 1], precision=TOP_ACCURACY)
    scores = jnp.einsum('hik,hjk->hij', queries_h, keys_h, precision=TOP_ACCURACY)
    result = jnp.einsum('hij,hjv->hiv', scores * weighting * fading, value_rows_head, precision=TOP_ACCURACY)
    lifted = queries_h * jnp.exp(running)[:, :, None]
    reach = gain[lvl_in + 1:][:, :, :, None] * lifted[None]
    return result + jnp.einsum('jhik,jhkv->hiv', reach, buckets, precision=TOP_ACCURACY)

def membership(count, depth):
    blocks = jnp.arange(count, dtype=jnp.int32)
    powers = jnp.arange(depth, dtype=jnp.int32)
    high_bits = jnp.right_shift(blocks[:, None], powers[None, :] + 1)
    own_bit = jnp.right_shift(blocks[:, None], powers[None, :]) % 2
    return (own_bit[:, :, None] == 1) & (high_bits[:, :, None] == high_bits.T[None]) & (own_bit.T[None] == 0)

def between_mask(count):
    blocks = jnp.arange(count, dtype=jnp.int32)
    inside = (blocks[None, None, :] > blocks[None, :, None]) & (blocks[None, None, :] < blocks[:, None, None])
    return inside.astype(jnp.float32)

def forward(query_full, key_full, value_full, gain, decay):
    count = N_CTX
    heads_q = query_full.reshape(count, TOK_DEV, H, HEAD).transpose(0, 2, 1, 3)
    heads_k = key_full.reshape(count, TOK_DEV, H, HEAD).transpose(0, 2, 1, 3)
    heads_v = value_full.reshape(count, TOK_DEV, H, HEAD).transpose(0, 2, 1, 3)
    decay_blocks = decay.reshape(H, count, TOK_DEV).transpose(1, 0, 2)
    gain_blocks = gain.reshape(LEVELS, H, count, TOK_DEV).transpose(2, 0, 1, 3)
    states, totals = lax.map(lambda items: block_front(items[0], items[1], items[2]), (heads_k, heads_v, decay_blocks))
    gaps = jnp.einsum('cdm,mh->cdh', between_mask(count), totals, precision=TOP_ACCURACY)
    member = membership(count, XLEV).astype(jnp.float32)

    def one_block(items):
        query_b, key_b, value_b, gain_b, decay_b, gap_b, member_b = items
        weights = member_b[:, :, None] * jnp.exp(gap_b)[None]
        buckets = jnp.einsum('jdh,dhkv->jhkv', weights, states, precision=TOP_ACCURACY)
        return block_output(query_b, key_b, value_b, gain_b, decay_b, buckets)
    outputs = lax.map(one_block, (heads_q, heads_k, heads_v, gain_blocks, decay_blocks, gaps, member))
    return outputs.transpose(0, 2, 1, 3).reshape(LEN, H * HEAD)

def reference(queries, keys_in, value_input, level_gain, decay_log, out_grad):
    mixed, back_fn = jax.vjp(forward, queries.astype(jnp.float32), keys_in.astype(jnp.float32), value_input.astype(jnp.float32), level_gain, decay_log)
    grads = back_fn(out_grad.astype(jnp.float32))
    return (mixed.astype(jnp.bfloat16), grads[0].astype(jnp.bfloat16), grads[1].astype(jnp.bfloat16), grads[2].astype(jnp.bfloat16), grads[3], grads[4])
```

```python
import jax
import jax.numpy as jnp
from jax import lax
from jax.experimental import pallas as pl
from jax.experimental.pallas import tpu as pltpu
from jax.sharding import PartitionSpec as P

MESH = pl.DeviceIdType.MESH
F32 = jnp.float32
BF16 = jnp.bfloat16
H = 16
HH = 8
N = 128
NR = 136
LVL_IN = 8
XLEV = 6
GRAN = 2

NN = (((1,), (0,)), ((), ()))
NT = (((1,), (1,)), ((), ()))


def mm(a, b, dims=NN):
    return lax.dot_general(a, b, dims, preferred_element_type=F32)


def split(x):
    hi = x.astype(BF16)
    lo = (x - hi.astype(F32)).astype(BF16)
    return hi, lo


def wide(x):
    hi, lo = split(x)
    return jnp.concatenate([hi, lo], axis=1)


def tall(x):
    hi, lo = split(x)
    return jnp.concatenate([hi, lo], axis=0)


def flip(x):
    return jnp.transpose(x.astype(F32)).astype(BF16)


def running_sums(decay):
    r = lax.broadcasted_iota(jnp.int32, (N, N), 0)
    t = lax.broadcasted_iota(jnp.int32, (N, N), 1)
    upper = (r <= t).astype(F32)
    run = lax.dot_general(decay, upper, NN, precision=lax.Precision.HIGHEST, preferred_element_type=F32)
    tot = lax.dot_general(decay, jnp.ones((N, N), F32), NN, precision=lax.Precision.HIGHEST, preferred_element_type=F32)
    return run, tot


def front_kernel(q_ref, k_ref, v_ref, g_ref, gain_ref, decay_ref, s_ref, big_ref, run_sc, tot_sc):
    h = pl.program_id(0)

    @pl.when(h == 0)
    def _():
        run, tot = running_sums(decay_ref[...])
        run_sc[...] = run
        tot_sc[...] = tot

    run = run_sc[pl.ds(h, 1), :]
    tot = tot_sc[pl.ds(h, 1), :]
    v = v_ref[...]
    g = g_ref[...]
    kt = jnp.transpose(k_ref[...].astype(F32))
    qt = jnp.transpose(q_ref[...].astype(F32))
    vv = jnp.concatenate([v, v], axis=0)
    gg = jnp.concatenate([g, g], axis=0)
    s_ref[0, 0:N, :] = mm(wide(kt * jnp.exp(tot - run)), vv)
    s_ref[0, N:NR, :] = jnp.broadcast_to(tot, (NR - N, N))
    lift = jnp.exp(run)
    for j in range(XLEV):
        row = gain_ref[LVL_IN + j, pl.ds(h, 1), :] * lift
        big_ref[j, 0] = mm(wide(qt * row), gg)


def front(q, k, v, g, gain, decay):
    col = pl.BlockSpec((N, N), lambda h: (0, h))
    return pl.pallas_call(
        front_kernel,
        grid=(H,),
        in_specs=[col, col, col, col,
                  pl.BlockSpec((LVL_IN + XLEV, H, N), lambda h: (0, 0, 0)),
                  pl.BlockSpec((H, N), lambda h: (0, 0))],
        out_specs=[pl.BlockSpec((1, NR, N), lambda h: (h, 0, 0)),
                   pl.BlockSpec((XLEV, 1, N, N), lambda h: (0, h, 0, 0))],
        out_shape=[jax.ShapeDtypeStruct((H, NR, N), F32),
                   jax.ShapeDtypeStruct((XLEV, H, N, N), F32)],
        scratch_shapes=[pltpu.VMEM((H, N), F32), pltpu.VMEM((H, N), F32)],
        name="front",
    )(q, k, v, g, gain, decay)


def coords():
    c = lax.axis_index("ctx")
    return c, lax.rem(c, 2), lax.rem(c // 2, 4), c // 8


def comm_kernel(s_ref, g_ref, b0_ref, bk_ref, ds_ref,
                rg, cbuf, mbuf, rbuf, pbuf, qbuf, ebuf, fbuf, abuf, bbuf, ybuf, xbuf,
                ssem, rx1, rx2, ry1, ry2, rz, re, ra, rb, rlate):
    seq = lax.axis_index("seq")
    c, b, y, z = coords()
    mine = b * HH
    theirs = (1 - b) * HH
    part = c + 1 - 2 * b
    yn = c + 2 - 4 * lax.rem(y, 2)
    ym = c + 2 * (3 - 2 * y)
    up = c + 8
    dn = c - 8
    yodd = lax.rem(y, 2) == 1
    yhi = y >= 2
    zb = [lax.rem(z, 2) == 1, lax.rem(z // 2, 2) == 1, z >= 4]

    barrier = pltpu.get_barrier_semaphore()

    def greet(who):
        pl.semaphore_signal(barrier, inc=1, device_id=(seq, who), device_id_type=MESH)

    greet(part)
    greet(yn)
    greet(ym)

    @pl.when(z < 7)
    def _():
        greet(up)

    @pl.when(z > 0)
    def _():
        greet(dn)

    pl.semaphore_wait(barrier, 3 + jnp.minimum(z, 1) + jnp.minimum(7 - z, 1))

    def copy(src, dst, send, recv, who):
        return pltpu.make_async_remote_copy(src_ref=src, dst_ref=dst, send_sem=send, recv_sem=recv,
                                            device_id=(seq, who), device_id_type=MESH)

    def x1(h):
        return copy(s_ref.at[theirs + h], b0_ref.at[theirs + h], ssem.at[0], rx1.at[h], part)

    def x1b(h):
        return copy(s_ref.at[h], b0_ref.at[h], ssem.at[1], rlate.at[5], part)

    def x2(j, h):
        return copy(g_ref.at[j, theirs + h], rg.at[j, h], ssem.at[2 + j], rx2.at[j, h], part)

    def x4(j, h):
        return copy(bk_ref.at[j, mine + h], bk_ref.at[j, mine + h], ssem.at[8 + j], rlate.at[j], part)

    def x5(h):
        return copy(xbuf.at[h], ds_ref.at[mine + h], ssem.at[13], rlate.at[6], part)

    def y1(h):
        return copy(cbuf.at[h], bk_ref.at[0, mine + h], ssem.at[14], ry1.at[h], yn)

    def y2(h):
        return copy(mbuf.at[h], bk_ref.at[1, mine + h], ssem.at[15], ry2.at[h], ym)

    def zmsg(j, src, h):
        return copy(src, bk_ref.at[2 + j, mine + h], ssem.at[16 + j], rz.at[j, h], up)

    def emsg(j, h):
        return copy(fbuf.at[j, h], ebuf.at[j, h], ssem.at[19 + j], re.at[j, h], dn)

    def amsg(h):
        return copy(abuf.at[h], ybuf.at[0, h], ssem.at[22], ra.at[h], ym)

    def bmsg(h):
        return copy(bbuf.at[h], ybuf.at[1, h], ssem.at[23], rb.at[h], yn)

    setbits = [None, yodd, yhi, zb[0], zb[1], zb[2]]

    def tot(ref):
        return ref[N:N + 1, :]

    def each(fn):
        def body(h, carry):
            fn(h)
            return carry
        lax.fori_loop(0, HH, body, 0)

    each(lambda h: x1(h).start())

    def send_g(h):
        for j in (5, 4, 3, 2, 1):
            @pl.when(setbits[j])
            def _(j=j):
                x2(j, h).start()
    each(send_g)

    @pl.when(b == 0)
    def _():
        each(lambda h: x1b(h).start())

    @pl.when(b == 1)
    def _():
        each(lambda h: x2(0, h).start())

    @pl.when(z == 7)
    def _():
        def zero(h):
            ebuf[2, h] = jnp.zeros((N, N), F32)
        each(zero)

    def merge(out, low, high, ht):
        out[0:N, :] = jnp.exp(ht) * low[0:N, :] + high[0:N, :]
        out[N:NR, :] = low[N:NR, :] + high[N:NR, :]

    def f1(h):
        x1(h).wait_recv()

        @pl.when(b == 0)
        def _():
            merge(cbuf.at[h], s_ref.at[mine + h], b0_ref.at[mine + h], tot(b0_ref.at[mine + h]))

        @pl.when(b == 1)
        def _():
            merge(cbuf.at[h], b0_ref.at[mine + h], s_ref.at[mine + h], tot(s_ref.at[mine + h]))

        y1(h).start()

    def f2(h):
        y1(h).wait_recv()
        other = bk_ref.at[0, mine + h]

        @pl.when(yodd)
        def _():
            merge(mbuf.at[h], other, cbuf.at[h], tot(cbuf.at[h]))
            x4(0, h).start()

        @pl.when(jnp.logical_not(yodd))
        def _():
            merge(mbuf.at[h], cbuf.at[h], other, tot(other))

        y2(h).start()

    def f3(h):
        y2(h).wait_recv()
        other = bk_ref.at[1, mine + h]

        @pl.when(yhi)
        def _():
            merge(rbuf.at[h], other, mbuf.at[h], tot(mbuf.at[h]))
            x4(1, h).start()

        @pl.when(jnp.logical_not(yhi))
        def _():
            merge(rbuf.at[h], mbuf.at[h], other, tot(other))

        @pl.when(jnp.logical_not(zb[0]))
        def _():
            zmsg(0, rbuf.at[h], h).start()

    def f4(h):
        zmsg(0, rbuf.at[h], h).wait_recv()
        x4(2, h).start()
        merge(pbuf.at[h], bk_ref.at[2, mine + h], rbuf.at[h], tot(rbuf.at[h]))

        @pl.when(jnp.logical_not(zb[1]))
        def _():
            zmsg(1, pbuf.at[h], h).start()

    def f5(h):
        here = bk_ref.at[3, mine + h]
        zmsg(1, here, h).wait_recv()

        @pl.when(jnp.logical_not(zb[0]))
        def _():
            zmsg(1, here, h).start()

        x4(3, h).start()

        @pl.when(z == 3)
        def _():
            merge(qbuf.at[h], here, pbuf.at[h], tot(pbuf.at[h]))
            zmsg(2, qbuf.at[h], h).start()

    def f7(h):
        here = bk_ref.at[4, mine + h]
        zmsg(2, here, h).wait_recv()

        @pl.when(z < 7)
        def _():
            zmsg(2, here, h).start()

        x4(4, h).start()

    def base_tot(h):
        own = tot(s_ref.at[mine + h])
        other = tot(b0_ref.at[mine + h])
        return jnp.where(b == 0, own, other)

    def chip_grad(j, h, off):
        e0 = jnp.exp(base_tot(h))
        own = g_ref[j, mine + h]
        other = rg[j, h]
        low = jnp.where(b == 0, jnp.exp(off), e0 * jnp.exp(off))
        high = jnp.where(b == 0, e0 * jnp.exp(off), jnp.exp(off))
        return low * own + high * other

    def row_off(h):
        t1 = tot(bk_ref.at[0, mine + h])
        t2 = tot(bk_ref.at[1, mine + h])
        return jnp.where(yodd, t1, 0.0) + jnp.where(yhi, t2, 0.0)

    in_slot = [jnp.where(zb[1], 2, 1), jnp.where(zb[0], 2, 1), 2]
    d_slot = jnp.where(zb[0], jnp.where(zb[1], 2, 1), 0)

    def back(h):
        @pl.when(jnp.logical_not(zb[0]))
        def _():
            emsg(0, h).wait_recv()

        @pl.when(zb[0] != zb[1])
        def _():
            emsg(1, h).wait_recv()

        @pl.when(jnp.logical_and(z >= 3, z < 7))
        def _():
            emsg(2, h).wait_recv()

        off = row_off(h)
        ez = jnp.exp(tot(rbuf.at[h]))
        for j in (2, 1, 0):
            @pl.when(zb[j])
            def _(j=j):
                x2(3 + j, h).wait_recv()
                fbuf[j, h] = ez * ebuf[in_slot[j], h] + chip_grad(3 + j, h, off)
                emsg(j, h).start()

        @pl.when(yhi)
        def _():
            x2(2, h).wait_recv()
            e23 = jnp.exp(tot(mbuf.at[h]))
            off2 = jnp.where(yodd, tot(bk_ref.at[0, mine + h]), 0.0)
            abuf[h] = e23 * ebuf[d_slot, h] + chip_grad(2, h, off2)

        @pl.when(jnp.logical_not(yhi))
        def _():
            abuf[h] = ebuf[d_slot, h]

        amsg(h).start()

    def ya(h):
        amsg(h).wait_recv()
        e23 = jnp.where(yhi, 1.0, jnp.exp(tot(bk_ref.at[1, mine + h])))
        yv = e23 * ebuf[d_slot, h] + ybuf[0, h]
        ybuf[2, h] = yv

        @pl.when(yodd)
        def _():
            x2(1, h).wait_recv()
            bbuf[h] = jnp.exp(tot(cbuf.at[h])) * yv + chip_grad(1, h, jnp.zeros((1, N), F32))

        @pl.when(jnp.logical_not(yodd))
        def _():
            bbuf[h] = yv

        bmsg(h).start()

    def yb(h):
        bmsg(h).wait_recv()
        e1 = jnp.where(yodd, 1.0, jnp.exp(tot(bk_ref.at[0, mine + h])))
        dc = e1 * ybuf[2, h] + ybuf[1, h]

        @pl.when(b == 0)
        def _():
            x2(0, h).wait_recv()
            ds_ref[mine + h] = jnp.exp(tot(b0_ref.at[mine + h])) * dc + rg[0, h]
            xbuf[h] = dc

        @pl.when(b == 1)
        def _():
            ds_ref[mine + h] = dc
            xbuf[h] = jnp.exp(tot(s_ref.at[mine + h])) * dc + g_ref[0, mine + h]

        x5(h).start()

    d = GRAN
    back0 = 2 * d

    def tick(t, carry):
        def stage(fn, lag, cond=None):
            h = t - lag
            ok = jnp.logical_and(h >= 0, h < HH)
            if cond is not None:
                ok = jnp.logical_and(ok, cond)

            @pl.when(ok)
            def _():
                fn(h)

        stage(f1, 0)
        stage(f2, d)
        stage(f3, 2 * d)
        stage(back, back0 + (7 - z) * d)
        stage(f4, 3 * d, zb[0])
        stage(f5, 4 * d + jnp.where(zb[0], d, 0), zb[1])
        stage(f7, 6 * d + (z - 4) * d, zb[2])
        stage(ya, back0 + (8 - z) * d)
        stage(yb, back0 + (9 - z) * d)
        return carry

    lax.fori_loop(0, HH + back0 + 9 * d, tick, 0)

    def all_of(src, dst, send, recv):
        return copy(src, dst, send, recv, part)

    half = pl.ds(0, HH)
    for j in range(5):
        def late(j=j):
            all_of(bk_ref.at[j, half], bk_ref.at[j, half], ssem.at[8 + j], rlate.at[j]).wait()
        pl.when(setbits[j + 1])(late)
        def sent(j=j):
            all_of(rg.at[j, half], rg.at[j, half], ssem.at[3 + j], rlate.at[j]).wait_send()
        pl.when(setbits[j + 1])(sent)

    @pl.when(b == 0)
    def _():
        all_of(s_ref.at[half], s_ref.at[half], ssem.at[1], rlate.at[5]).wait_send()

    @pl.when(b == 1)
    def _():
        all_of(s_ref.at[half], s_ref.at[half], ssem.at[1], rlate.at[5]).wait_recv()
        all_of(rg.at[0, half], rg.at[0, half], ssem.at[2], rlate.at[5]).wait_send()

    all_of(xbuf.at[half], xbuf.at[half], ssem.at[13], rlate.at[6]).wait()
    all_of(s_ref.at[half], s_ref.at[half], ssem.at[0], rlate.at[5]).wait_send()
    all_of(cbuf.at[half], cbuf.at[half], ssem.at[14], rlate.at[5]).wait_send()
    all_of(mbuf.at[half], mbuf.at[half], ssem.at[15], rlate.at[5]).wait_send()
    all_of(abuf.at[half], abuf.at[half], ssem.at[22], rlate.at[5]).wait_send()
    all_of(bbuf.at[half], bbuf.at[half], ssem.at[23], rlate.at[5]).wait_send()
    out_cond = [jnp.logical_not(zb[0]), zb[0] != zb[1], jnp.logical_and(z >= 3, z < 7)]
    for j in range(3):
        def zsent(j=j):
            all_of(cbuf.at[half], cbuf.at[half], ssem.at[16 + j], rlate.at[5]).wait_send()
        pl.when(out_cond[j])(zsent)
        def esent(j=j):
            all_of(fbuf.at[j, half], fbuf.at[j, half], ssem.at[19 + j], rlate.at[5]).wait_send()
        pl.when(zb[j])(esent)


def comm(s, big):
    vm = pl.BlockSpec(memory_space=pltpu.VMEM)
    st = lambda *lead: pltpu.VMEM(lead + (NR, N), F32)
    sg = lambda *lead: pltpu.VMEM(lead + (N, N), F32)
    dma = pltpu.SemaphoreType.DMA
    return pl.pallas_call(
        comm_kernel,
        in_specs=[vm, vm],
        out_specs=[vm, vm, vm],
        out_shape=[jax.ShapeDtypeStruct((H, NR, N), F32),
                   jax.ShapeDtypeStruct((XLEV - 1, H, NR, N), F32),
                   jax.ShapeDtypeStruct((H, N, N), F32)],
        scratch_shapes=[sg(6, HH), st(HH), st(HH), st(HH), st(HH), st(HH),
                        sg(3, HH), sg(3, HH), sg(HH), sg(HH), sg(3, HH), sg(HH),
                        dma((24,)), dma((HH,)), dma((6, HH)), dma((HH,)), dma((HH,)),
                        dma((3, HH)), dma((3, HH)), dma((HH,)), dma((HH,)), dma((7,))],
        compiler_params=pltpu.CompilerParams(collective_id=0, has_side_effects=True,
                                             vmem_limit_bytes=62 * 1024 * 1024),
        name="states",
    )(s, big)


def final_kernel(q_ref, k_ref, v_ref, g_ref, gain_ref, decay_ref, b0_ref, bk_ref, ds_ref,
                 o_ref, dq_ref, dk_ref, dv_ref, dgain_ref, rev_ref, tot_ref,
                 run_sc, tot_sc, row_sc, col_sc):
    h = pl.program_id(0)
    c = lax.axis_index("ctx")

    @pl.when(h == 0)
    def _():
        run, tot = running_sums(decay_ref[...])
        run_sc[...] = run
        tot_sc[...] = tot
        col_sc[...] = jnp.zeros((N, N), F32)

    run = run_sc[pl.ds(h, 1), :]
    tot = tot_sc[pl.ds(h, 1), :]
    q, k, v, g = q_ref[...], k_ref[...], v_ref[...], g_ref[...]
    qt32 = jnp.transpose(q.astype(F32))
    qt = qt32.astype(BF16)
    gt, kt, vt = flip(g), flip(k), flip(v)

    bits = [lax.rem(c // (1 << j), 2) == 1 for j in range(XLEV)]
    rows = []
    lifts = []
    off = run
    buckets = []
    for j in range(XLEV):
        src = b0_ref.at[0] if j == 0 else bk_ref.at[j - 1, 0]
        buckets.append(jnp.where(bits[j], src[0:N, :], 0.0))
        lift = jnp.where(bits[j], jnp.exp(off), 0.0)
        lifts.append(lift)
        rows.append(gain_ref[LVL_IN + j, pl.ds(h, 1), :] * lift)
        off = off + jnp.where(bits[j], src[N:N + 1, :], 0.0)
    rows += [run, jnp.exp(tot - run)]
    cols = jnp.transpose(jnp.concatenate(rows + [jnp.zeros((N - 8, N), F32)], axis=0))
    run_col = cols[:, 6:7]
    tail_col = cols[:, 7:8]

    s_i = lax.broadcasted_iota(jnp.int32, (N, N), 0)
    t_i = lax.broadcasted_iota(jnp.int32, (N, N), 1)
    causal = s_i <= t_i
    mixing = jnp.bitwise_xor(s_i, t_i)
    fade = jnp.where(causal, jnp.exp(jnp.where(causal, run - run_col, 0.0)), 0.0)
    weight = jnp.broadcast_to(gain_ref[0, pl.ds(h, 1), :], (N, N))
    for lev in range(1, LVL_IN):
        weight = jnp.where(mixing >= (1 << (lev - 1)), gain_ref[lev, pl.ds(h, 1), :], weight)
    sc = mm(k, qt)
    gv = mm(v, gt)
    wd = weight * fade
    wt = sc * wd
    xt = gv * wd
    pair = sc * gv * fade
    above = [jnp.sum(pair, axis=0, keepdims=True)]
    for lev in range(1, LVL_IN):
        above.append(jnp.sum(jnp.where(mixing >= (1 << (lev - 1)), pair, 0.0), axis=0, keepdims=True))
    above.append(jnp.zeros((1, N), F32))
    for lev in range(LVL_IN):
        dgain_ref[lev, pl.ds(h, 1), :] = above[lev] - above[lev + 1]

    vt2 = jnp.concatenate([vt, vt], axis=1)
    kt2 = jnp.concatenate([kt, kt], axis=1)
    gt2 = jnp.concatenate([gt, gt], axis=0)
    q2 = jnp.concatenate([q, q], axis=1)
    o = jnp.transpose(mm(vt2, tall(wt)))
    dqt = mm(kt2, tall(xt))
    for j in range(XLEV):
        m_hi, m_lo = split(buckets[j])
        o = o + cols[:, j:j + 1] * mm(q2, jnp.concatenate([m_hi, m_lo], axis=0))
        dt = mm(jnp.concatenate([m_hi, m_lo], axis=1), gt2)
        dqt = dqt + rows[j] * dt
        dgain_ref[LVL_IN + j, pl.ds(h, 1), :] = lifts[j] * jnp.sum(dt * qt32, axis=0, keepdims=True)
    o_ref[...] = o.astype(BF16)
    dq_ref[...] = jnp.transpose(dqt).astype(BF16)
    row_sc[pl.ds(h, 1), :] = jnp.sum(dqt * qt32, axis=0, keepdims=True)

    d_hi, d_lo = split(ds_ref[0])
    k2 = jnp.concatenate([k, k], axis=1)
    v2 = jnp.concatenate([v, v], axis=1)
    dv = mm(wide(wt), jnp.concatenate([g, g], axis=0))
    dv = dv + tail_col * mm(k2, jnp.concatenate([d_hi, d_lo], axis=0))
    dk = mm(wide(xt), jnp.concatenate([q, q], axis=0))
    dk = dk + tail_col * mm(v2, jnp.concatenate([d_hi, d_lo], axis=1), NT)
    dk_ref[...] = dk.astype(BF16)
    dv_ref[...] = dv.astype(BF16)
    col = jnp.sum(v.astype(F32) * dv, axis=1, keepdims=True)
    col_sc[...] = jnp.where(t_i == h, col, col_sc[...])

    @pl.when(h == H - 1)
    def _():
        da = row_sc[...] - jnp.transpose(col_sc[...])[0:H, :]
        lower = (s_i >= t_i).astype(F32)
        rev_ref[...] = lax.dot_general(da, lower, NN, precision=lax.Precision.HIGHEST, preferred_element_type=F32)
        tot_ref[...] = lax.dot_general(da, jnp.ones((N, N), F32), NN, precision=lax.Precision.HIGHEST,
                                       preferred_element_type=F32)


def final(q, k, v, g, gain, decay, b0, bk, ds):
    col = pl.BlockSpec((N, N), lambda h: (0, h))
    whole3 = pl.BlockSpec((LVL_IN + XLEV, H, N), lambda h: (0, 0, 0))
    whole2 = pl.BlockSpec((H, N), lambda h: (0, 0))
    wide_out = jax.ShapeDtypeStruct((N, H * N), BF16)
    return pl.pallas_call(
        final_kernel,
        grid=(H,),
        in_specs=[col, col, col, col, whole3, whole2,
                  pl.BlockSpec((1, NR, N), lambda h: (h, 0, 0)),
                  pl.BlockSpec((XLEV - 1, 1, NR, N), lambda h: (0, h, 0, 0)),
                  pl.BlockSpec((1, N, N), lambda h: (h, 0, 0))],
        out_specs=[col, col, col, col, whole3, whole2, whole2],
        out_shape=[wide_out, wide_out, wide_out, wide_out,
                   jax.ShapeDtypeStruct((LVL_IN + XLEV, H, N), F32),
                   jax.ShapeDtypeStruct((H, N), F32), jax.ShapeDtypeStruct((H, N), F32)],
        scratch_shapes=[pltpu.VMEM((H, N), F32), pltpu.VMEM((H, N), F32),
                        pltpu.VMEM((H, N), F32), pltpu.VMEM((N, N), F32)],
        name="final",
    )(q, k, v, g, gain, decay, b0, bk, ds)


def suffix_kernel(rev_ref, tot_ref, out_ref, rowin, zin, sendbuf, ssem, rsem, zssem, zrsem):
    seq = lax.axis_index("seq")
    c, _, _, z = coords()
    r = lax.rem(c, 8)
    barrier = pltpu.get_barrier_semaphore()
    for i in range(1, 8):
        pl.semaphore_signal(barrier, inc=1, device_id=(seq, z * 8 + lax.rem(r + i, 8)), device_id_type=MESH)
        pl.semaphore_signal(barrier, inc=1, device_id=(seq, lax.rem(z + i, 8) * 8 + r), device_id_type=MESH)
    pl.semaphore_wait(barrier, 14)

    def rcopy(i):
        return pltpu.make_async_remote_copy(
            src_ref=tot_ref, dst_ref=rowin.at[i], send_sem=ssem.at[i], recv_sem=rsem.at[i],
            device_id=(seq, z * 8 + lax.rem(r + i, 8)), device_id_type=MESH)

    def zcopy(i):
        return pltpu.make_async_remote_copy(
            src_ref=sendbuf, dst_ref=zin.at[i], send_sem=zssem.at[i], recv_sem=zrsem.at[i],
            device_id=(seq, lax.rem(z + i, 8) * 8 + r), device_id_type=MESH)

    for i in range(1, 8):
        rcopy(i).start()
    total = tot_ref[...]
    after = jnp.zeros((H, N), F32)
    for i in range(1, 8):
        rcopy(i).wait_recv()
        val = rowin[i]
        total = total + val
        after = after + jnp.where(r - i < 0, val, 0.0)
    sendbuf[...] = total
    for i in range(1, 8):
        zcopy(i).start()
    acc = rev_ref[...] + after
    for i in range(1, 8):
        zcopy(i).wait_recv()
        acc = acc + jnp.where(z - i < 0, zin[i], 0.0)
    out_ref[...] = acc
    for i in range(1, 8):
        rcopy(i).wait_send()
        zcopy(i).wait_send()


def suffix(rev, tot):
    vm = pl.BlockSpec(memory_space=pltpu.VMEM)
    dma = pltpu.SemaphoreType.DMA
    return pl.pallas_call(
        suffix_kernel,
        in_specs=[vm, vm],
        out_specs=vm,
        out_shape=jax.ShapeDtypeStruct((H, N), F32),
        scratch_shapes=[pltpu.VMEM((8, H, N), F32), pltpu.VMEM((8, H, N), F32), pltpu.VMEM((H, N), F32),
                        dma((8,)), dma((8,)), dma((8,)), dma((8,))],
        compiler_params=pltpu.CompilerParams(collective_id=1, has_side_effects=True),
        name="suffix",
    )(rev, tot)


def per_device(queries, keys_in, value_input, level_gain, decay_log, out_grad):
    s, big = front(queries, keys_in, value_input, out_grad, level_gain, decay_log)
    b0, bk, ds = comm(s, big)
    o, dq, dk, dv, dgain, rev, tot = final(queries, keys_in, value_input, out_grad, level_gain, decay_log, b0, bk, ds)
    return o, dq, dk, dv, dgain, suffix(rev, tot)


def solution(mesh):
    tokens = P(("seq", "ctx"), None)
    gains = P(None, None, ("seq", "ctx"))
    decays = P(None, ("seq", "ctx"))
    return jax.shard_map(
        per_device,
        mesh=mesh,
        in_specs=(tokens, tokens, tokens, gains, decays, tokens),
        out_specs=(tokens, tokens, tokens, tokens, gains, decays),
        check_vma=False,
    )
```

```python
import jax
import jax.numpy as jnp
from jax import lax
from jax.experimental import pallas as pl
from jax.experimental.pallas import tpu as pltpu
from jax.sharding import PartitionSpec as P

MESH = pl.DeviceIdType.MESH
F32 = jnp.float32
BF16 = jnp.bfloat16
H = 16
HH = 8
N = 128
LVL_IN = 8
XLEV = 6
GRAN = 2

NN = (((1,), (0,)), ((), ()))
NT = (((1,), (1,)), ((), ()))


def mm(a, b, dims=NN):
    return lax.dot_general(a, b, dims, preferred_element_type=F32)


def split(x):
    hi = x.astype(BF16)
    lo = (x - hi.astype(F32)).astype(BF16)
    return hi, lo


def wide(x):
    hi, lo = split(x)
    return jnp.concatenate([hi, lo], axis=1)


def tall(x):
    hi, lo = split(x)
    return jnp.concatenate([hi, lo], axis=0)


def flip(x):
    return jnp.transpose(x.astype(F32)).astype(BF16)


def running_sums(decay):
    r = lax.broadcasted_iota(jnp.int32, (N, N), 0)
    t = lax.broadcasted_iota(jnp.int32, (N, N), 1)
    upper = (r <= t).astype(F32)
    run = lax.dot_general(decay, upper, NN, precision=lax.Precision.HIGHEST, preferred_element_type=F32)
    tot = lax.dot_general(decay, jnp.ones((N, N), F32), NN, precision=lax.Precision.HIGHEST, preferred_element_type=F32)
    return run, tot


def front_kernel(q_ref, k_ref, v_ref, g_ref, gain_ref, decay_ref, s_ref, big_ref, own_ref, run_sc, tot_sc):
    h = pl.program_id(0)

    @pl.when(h == 0)
    def _():
        run, tot = running_sums(decay_ref[...])
        run_sc[...] = run
        tot_sc[...] = tot
        own_ref[...] = tot

    run = run_sc[pl.ds(h, 1), :]
    tot = tot_sc[pl.ds(h, 1), :]
    v = v_ref[...]
    g = g_ref[...]
    kt = jnp.transpose(k_ref[...].astype(F32))
    qt = jnp.transpose(q_ref[...].astype(F32))
    vv = jnp.concatenate([v, v], axis=0)
    gg = jnp.concatenate([g, g], axis=0)
    s_ref[0] = mm(wide(kt * jnp.exp(tot - run)), vv)
    lift = jnp.exp(run)
    for j in range(XLEV):
        row = gain_ref[LVL_IN + j, pl.ds(h, 1), :] * lift
        big_ref[j, 0] = mm(wide(qt * row), gg)


def front(q, k, v, g, gain, decay):
    col = pl.BlockSpec((N, N), lambda h: (0, h))
    return pl.pallas_call(
        front_kernel,
        grid=(H,),
        in_specs=[col, col, col, col,
                  pl.BlockSpec((LVL_IN + XLEV, H, N), lambda h: (0, 0, 0)),
                  pl.BlockSpec((H, N), lambda h: (0, 0))],
        out_specs=[pl.BlockSpec((1, N, N), lambda h: (h, 0, 0)),
                   pl.BlockSpec((XLEV, 1, N, N), lambda h: (0, h, 0, 0)),
                   pl.BlockSpec((H, N), lambda h: (0, 0))],
        out_shape=[jax.ShapeDtypeStruct((H, N, N), F32),
                   jax.ShapeDtypeStruct((XLEV, H, N, N), F32),
                   jax.ShapeDtypeStruct((H, N), F32)],
        scratch_shapes=[pltpu.VMEM((H, N), F32), pltpu.VMEM((H, N), F32)],
        name="front",
    )(q, k, v, g, gain, decay)


def coords():
    c = lax.axis_index("ctx")
    return c, lax.rem(c, 2), lax.rem(c // 2, 4), c // 8


def pick(parts, cond):
    acc = jnp.zeros((H, N), F32)
    for i in range(8):
        acc = acc + jnp.where(cond(i), parts[i], 0.0)
    return acc


def comm_kernel(s_ref, g_ref, own_ref, b0_ref, bk_ref, ds_ref, off_ref,
                rg, cbuf, mbuf, rbuf, pbuf, qbuf, ebuf, fbuf, abuf, bbuf, ybuf, xbuf, tt, rowt, zt, rsum,
                ssem, rx1, rx2, ry1, ry2, rz, re, ra, rb, rlate, trs, trr, tzs, tzr):
    seq = lax.axis_index("seq")
    c, b, y, z = coords()
    r = lax.rem(c, 8)
    mine = b * HH
    theirs = (1 - b) * HH
    part = c + 1 - 2 * b
    yn = c + 2 - 4 * lax.rem(y, 2)
    ym = c + 2 * (3 - 2 * y)
    up = c + 8
    dn = c - 8
    yodd = lax.rem(y, 2) == 1
    yhi = y >= 2
    zb = [lax.rem(z, 2) == 1, lax.rem(z // 2, 2) == 1, z >= 4]
    row_peer = [z * 8 + lax.rem(r + i, 8) for i in range(8)]
    z_peer = [lax.rem(z + i, 8) * 8 + r for i in range(8)]
    row_from = [lax.rem(r - i + 8, 8) for i in range(8)]
    z_from = [lax.rem(z - i + 8, 8) for i in range(8)]

    barrier = pltpu.get_barrier_semaphore()
    for i in range(1, 8):
        pl.semaphore_signal(barrier, inc=1, device_id=(seq, row_peer[i]), device_id_type=MESH)
        pl.semaphore_signal(barrier, inc=1, device_id=(seq, z_peer[i]), device_id_type=MESH)
    pl.semaphore_wait(barrier, 14)

    def copy(src, dst, send, recv, who):
        return pltpu.make_async_remote_copy(src_ref=src, dst_ref=dst, send_sem=send, recv_sem=recv,
                                            device_id=(seq, who), device_id_type=MESH)

    def x1(h):
        return copy(s_ref.at[theirs + h], b0_ref.at[theirs + h], ssem.at[0], rx1.at[h], part)

    def x1b(h):
        return copy(s_ref.at[h], b0_ref.at[h], ssem.at[1], rlate.at[5], part)

    def x2(j, h):
        return copy(g_ref.at[j, theirs + h], rg.at[j, h], ssem.at[2 + j], rx2.at[j, h], part)

    def x4(j, h):
        return copy(bk_ref.at[j, mine + h], bk_ref.at[j, mine + h], ssem.at[8 + j], rlate.at[j], part)

    def x5(h):
        return copy(xbuf.at[h], ds_ref.at[mine + h], ssem.at[13], rlate.at[6], part)

    def y1(h):
        return copy(cbuf.at[h], bk_ref.at[0, mine + h], ssem.at[14], ry1.at[h], yn)

    def y2(h):
        return copy(mbuf.at[h], bk_ref.at[1, mine + h], ssem.at[15], ry2.at[h], ym)

    def zmsg(j, src, h):
        return copy(src, bk_ref.at[2 + j, mine + h], ssem.at[16 + j], rz.at[j, h], up)

    def emsg(j, h):
        return copy(fbuf.at[j, h], ebuf.at[j, h], ssem.at[19 + j], re.at[j, h], dn)

    def amsg(h):
        return copy(abuf.at[h], ybuf.at[0, h], ssem.at[22], ra.at[h], ym)

    def bmsg(h):
        return copy(bbuf.at[h], ybuf.at[1, h], ssem.at[23], rb.at[h], yn)

    def rtot(i):
        return copy(own_ref, rowt.at[i], trs.at[i], trr.at[i], row_peer[i])

    def ztot(i):
        return copy(rsum, zt.at[i], tzs.at[i], tzr.at[i], z_peer[i])

    setbits = [None, yodd, yhi, zb[0], zb[1], zb[2]]

    def each(fn):
        def body(h, carry):
            fn(h)
            return carry
        lax.fori_loop(0, HH, body, 0)

    for i in range(1, 8):
        rtot(i).start()
    each(lambda h: x1(h).start())
    for j in (5, 4, 3, 2, 1):
        @pl.when(setbits[j])
        def _(j=j):
            each(lambda h: x2(j, h).start())

    @pl.when(b == 0)
    def _():
        each(lambda h: x1b(h).start())

    @pl.when(b == 1)
    def _():
        each(lambda h: x2(0, h).start())

    @pl.when(z == 7)
    def _():
        def zero(h):
            ebuf[2, h] = jnp.zeros((N, N), F32)
        each(zero)

    for i in range(1, 8):
        rtot(i).wait_recv()
    parts = [own_ref[...]] + [rowt[i] for i in range(1, 8)]
    rows = pick(parts, lambda i: row_from[i] >= 0)
    rsum[...] = rows
    for i in range(1, 8):
        ztot(i).start()
    core0 = pick(parts, lambda i: row_from[i] == 2 * y)
    core1 = pick(parts, lambda i: row_from[i] == 2 * y + 1)
    tt[0] = core0
    tt[1] = core1
    tt[2] = pick(parts, lambda i: row_from[i] // 2 == 2 * (y // 2) + 1)
    tt[3] = pick(parts, lambda i: row_from[i] >= 4)
    tt[4] = rows
    tt[5] = pick(parts, lambda i: row_from[i] < 2 * y)
    tt[6] = pick(parts, lambda i: jnp.logical_and(row_from[i] >= 4, row_from[i] < 2 * y))
    tt[7] = jnp.zeros((H, N), F32)
    off_ref[0] = jnp.zeros((H, N), F32)
    off_ref[1] = jnp.where(b == 1, core0, 0.0)
    off_ref[2] = pick(parts, lambda i: jnp.logical_and(row_from[i] >= 4 * (y // 2), row_from[i] < r))         if False else jnp.where(b == 1, core0, 0.0) + pick(
            parts, lambda i: jnp.logical_and(row_from[i] // 2 == y - 1, yodd))
    off3 = pick(parts, lambda i: row_from[i] < r)
    off_ref[3] = off3

    def z_tables():
        for i in range(1, 8):
            ztot(i).wait_recv()
        zp = [tt[4]] + [zt[i] for i in range(1, 8)]
        tt[8] = pick(zp, lambda i: jnp.logical_and(z_from[i] >= z - 1, z_from[i] <= z))
        off_ref[4] = off_ref[3] + pick(zp, lambda i: jnp.logical_and(z_from[i] >= 2 * (z // 2), z_from[i] < z))
        off_ref[5] = off_ref[3] + pick(zp, lambda i: jnp.logical_and(z_from[i] >= 4 * (z // 4), z_from[i] < z))

    def tb(k, h):
        return tt[k, pl.ds(mine + h, 1), :]

    def merge(out, low, high, k, h):
        out[...] = jnp.exp(tb(k, h)) * low[...] + high[...]

    def f1(h):
        x1(h).wait_recv()

        @pl.when(b == 0)
        def _():
            merge(cbuf.at[h], s_ref.at[mine + h], b0_ref.at[mine + h], 1, h)

        @pl.when(b == 1)
        def _():
            merge(cbuf.at[h], b0_ref.at[mine + h], s_ref.at[mine + h], 1, h)

        y1(h).start()

    def f2(h):
        y1(h).wait_recv()
        other = bk_ref.at[0, mine + h]

        @pl.when(yodd)
        def _():
            merge(mbuf.at[h], other, cbuf.at[h], 2, h)
            x4(0, h).start()

        @pl.when(jnp.logical_not(yodd))
        def _():
            merge(mbuf.at[h], cbuf.at[h], other, 2, h)

        y2(h).start()

    def f3(h):
        y2(h).wait_recv()
        other = bk_ref.at[1, mine + h]

        @pl.when(yhi)
        def _():
            merge(rbuf.at[h], other, mbuf.at[h], 3, h)
            x4(1, h).start()

        @pl.when(jnp.logical_not(yhi))
        def _():
            merge(rbuf.at[h], mbuf.at[h], other, 3, h)

        @pl.when(jnp.logical_not(zb[0]))
        def _():
            zmsg(0, rbuf.at[h], h).start()

    def f4(h):
        zmsg(0, rbuf.at[h], h).wait_recv()
        x4(2, h).start()
        merge(pbuf.at[h], bk_ref.at[2, mine + h], rbuf.at[h], 4, h)

        @pl.when(jnp.logical_not(zb[1]))
        def _():
            zmsg(1, pbuf.at[h], h).start()

    def f5(h):
        here = bk_ref.at[3, mine + h]
        zmsg(1, here, h).wait_recv()

        @pl.when(jnp.logical_not(zb[0]))
        def _():
            zmsg(1, here, h).start()

        x4(3, h).start()

        @pl.when(z == 3)
        def _():
            merge(qbuf.at[h], here, pbuf.at[h], 8, h)
            zmsg(2, qbuf.at[h], h).start()

    def f7(h):
        here = bk_ref.at[4, mine + h]
        zmsg(2, here, h).wait_recv()

        @pl.when(z < 7)
        def _():
            zmsg(2, here, h).start()

        x4(4, h).start()

    def chip_grad(j, h, k):
        x2(j, h).wait_recv()
        e0 = jnp.exp(tb(0, h))
        off = jnp.exp(tb(k, h))
        low = jnp.where(b == 0, off, e0 * off)
        high = jnp.where(b == 0, e0 * off, off)
        return low * g_ref[j, mine + h] + high * rg[j, h]

    in_slot = [jnp.where(zb[1], 2, 1), jnp.where(zb[0], 2, 1), 2]
    d_slot = jnp.where(zb[0], jnp.where(zb[1], 2, 1), 0)
    in_cond = [jnp.logical_not(zb[0]), zb[0] != zb[1], jnp.logical_and(z >= 3, z < 7)]

    def e_send(j):
        def go(h):
            fbuf[j, h] = jnp.exp(tb(4, h)) * ebuf[in_slot[j], h] + chip_grad(3 + j, h, 5)
            emsg(j, h).start()
        return go

    def e_wait(j):
        return lambda h: emsg(j, h).wait_recv()

    def a_send(h):
        @pl.when(yhi)
        def _():
            abuf[h] = jnp.exp(tb(3, h)) * ebuf[d_slot, h] + chip_grad(2, h, 6)

        @pl.when(jnp.logical_not(yhi))
        def _():
            abuf[h] = ebuf[d_slot, h]

        amsg(h).start()

    def ya(h):
        amsg(h).wait_recv()
        e23 = jnp.where(yhi, 1.0, jnp.exp(tb(3, h)))
        yv = e23 * ebuf[d_slot, h] + ybuf[0, h]
        ybuf[2, h] = yv

        @pl.when(yodd)
        def _():
            bbuf[h] = jnp.exp(tb(2, h)) * yv + chip_grad(1, h, 7)

        @pl.when(jnp.logical_not(yodd))
        def _():
            bbuf[h] = yv

        bmsg(h).start()

    def yb(h):
        bmsg(h).wait_recv()
        e1 = jnp.where(yodd, 1.0, jnp.exp(tb(2, h)))
        dc = e1 * ybuf[2, h] + ybuf[1, h]

        @pl.when(b == 0)
        def _():
            x2(0, h).wait_recv()
            ds_ref[mine + h] = jnp.exp(tb(1, h)) * dc + rg[0, h]
            xbuf[h] = dc

        @pl.when(b == 1)
        def _():
            ds_ref[mine + h] = dc
            xbuf[h] = jnp.exp(tb(1, h)) * dc + g_ref[0, mine + h]

        x5(h).start()

    d = GRAN
    e5_lag = (7 - z) * d
    low_half = z < 4
    e4_lag = jnp.where(low_half, (7 - z) * d, HH + (7 - z) * d)
    e3_lag = jnp.where(z == 7, 2 * HH, jnp.where(z == 5, HH + 2 * d, jnp.where(z == 3, HH + 4 * d, 6 * d)))
    d_lag = jnp.where(z == 7, 0, jnp.where(z == 6, 2 * HH + d, jnp.where(z == 5, HH + 2 * d, jnp.where(
        z == 4, HH + 3 * d, jnp.where(z == 3, 4 * d, jnp.where(z == 2, HH + 5 * d, jnp.where(z == 1, 6 * d, 7 * d)))))))
    B0 = 1

    def tick(t, carry):
        def stage(fn, lag, cond=None):
            h = t - lag
            ok = jnp.logical_and(h >= 0, h < HH)
            if cond is not None:
                ok = jnp.logical_and(ok, cond)

            @pl.when(ok)
            def _():
                fn(h)

        @pl.when(t == 3)
        def _():
            z_tables()

        stage(f1, 0)
        stage(e_wait(2), B0 + e5_lag, in_cond[2])
        stage(e_send(2), B0 + e5_lag, zb[2])
        stage(e_wait(1), B0 + e4_lag, in_cond[1])
        stage(e_send(1), B0 + e4_lag, zb[1])
        stage(f2, d)
        stage(f3, 2 * d)
        stage(f4, 3 * d, zb[0])
        stage(f5, 4 * d + jnp.where(zb[0], d, 0), zb[1])
        stage(f7, 6 * d + (z - 4) * d, zb[2])
        stage(e_send(0), B0 + e3_lag, zb[0])
        stage(e_wait(0), B0 + d_lag, in_cond[0])
        stage(a_send, B0 + d_lag)
        stage(ya, B0 + d_lag + d)
        stage(yb, B0 + d_lag + 2 * d)
        return carry

    lax.fori_loop(0, B0 + 3 * HH + 3 * d, tick, 0)

    def all_of(src, dst, send, recv):
        return copy(src, dst, send, recv, part)

    half = pl.ds(0, HH)
    for j in range(5):
        def late(j=j):
            all_of(bk_ref.at[j, half], bk_ref.at[j, half], ssem.at[8 + j], rlate.at[j]).wait()
            all_of(rg.at[j, half], rg.at[j, half], ssem.at[3 + j], rlate.at[j]).wait_send()
        pl.when(setbits[j + 1])(late)

    def sent(k, buf):
        all_of(buf.at[half], buf.at[half], ssem.at[k], rlate.at[5]).wait_send()

    @pl.when(b == 0)
    def _():
        sent(1, s_ref)

    @pl.when(b == 1)
    def _():
        all_of(s_ref.at[half], s_ref.at[half], ssem.at[1], rlate.at[5]).wait_recv()
        sent(2, cbuf)

    all_of(xbuf.at[half], xbuf.at[half], ssem.at[13], rlate.at[6]).wait()
    sent(0, cbuf)
    for k in (14, 15, 22, 23):
        sent(k, cbuf)
    for j in range(3):
        def zsent(j=j):
            sent(16 + j, cbuf)
        pl.when(in_cond[j])(zsent)
        def esent(j=j):
            sent(19 + j, cbuf)
        pl.when(zb[j])(esent)
    for i in range(1, 8):
        rtot(i).wait_send()
        ztot(i).wait_send()


def comm(s, big, own):
    vm = pl.BlockSpec(memory_space=pltpu.VMEM)
    sg = lambda *lead: pltpu.VMEM(lead + (N, N), F32)
    tv = lambda *lead: pltpu.VMEM(lead + (H, N), F32)
    dma = pltpu.SemaphoreType.DMA
    return pl.pallas_call(
        comm_kernel,
        in_specs=[vm, vm, vm],
        out_specs=[vm, vm, vm, vm],
        out_shape=[jax.ShapeDtypeStruct((H, N, N), F32),
                   jax.ShapeDtypeStruct((XLEV - 1, H, N, N), F32),
                   jax.ShapeDtypeStruct((H, N, N), F32),
                   jax.ShapeDtypeStruct((XLEV, H, N), F32)],
        scratch_shapes=[sg(6, HH), sg(HH), sg(HH), sg(HH), sg(HH), sg(HH),
                        sg(3, HH), sg(3, HH), sg(HH), sg(HH), sg(3, HH), sg(HH),
                        tv(9), tv(8), tv(8), tv(),
                        dma((24,)), dma((HH,)), dma((6, HH)), dma((HH,)), dma((HH,)),
                        dma((3, HH)), dma((3, HH)), dma((HH,)), dma((HH,)), dma((7,)),
                        dma((8,)), dma((8,)), dma((8,)), dma((8,))],
        compiler_params=pltpu.CompilerParams(collective_id=0, has_side_effects=True,
                                             vmem_limit_bytes=62 * 1024 * 1024),
        name="states",
    )(s, big, own)


def final_kernel(q_ref, k_ref, v_ref, g_ref, gain_ref, decay_ref, b0_ref, bk_ref, ds_ref, off_ref,
                 o_ref, dq_ref, dk_ref, dv_ref, dgain_ref, rev_ref, tot_ref,
                 run_sc, tot_sc, row_sc, col_sc):
    h = pl.program_id(0)
    c = lax.axis_index("ctx")

    @pl.when(h == 0)
    def _():
        run, tot = running_sums(decay_ref[...])
        run_sc[...] = run
        tot_sc[...] = tot
        col_sc[...] = jnp.zeros((N, N), F32)

    run = run_sc[pl.ds(h, 1), :]
    tot = tot_sc[pl.ds(h, 1), :]
    q, k, v, g = q_ref[...], k_ref[...], v_ref[...], g_ref[...]
    qt32 = jnp.transpose(q.astype(F32))
    qt = qt32.astype(BF16)
    gt, kt, vt = flip(g), flip(k), flip(v)

    bits = [lax.rem(c // (1 << j), 2) == 1 for j in range(XLEV)]
    rows = []
    lifts = []
    buckets = []
    for j in range(XLEV):
        src = b0_ref.at[0] if j == 0 else bk_ref.at[j - 1, 0]
        buckets.append(jnp.where(bits[j], src[...], 0.0))
        lift = jnp.where(bits[j], jnp.exp(run + off_ref[j, pl.ds(h, 1), :]), 0.0)
        lifts.append(lift)
        rows.append(gain_ref[LVL_IN + j, pl.ds(h, 1), :] * lift)
    rows += [run, jnp.exp(tot - run)]
    cols = jnp.transpose(jnp.concatenate(rows + [jnp.zeros((N - 8, N), F32)], axis=0))
    run_col = cols[:, 6:7]
    tail_col = cols[:, 7:8]

    s_i = lax.broadcasted_iota(jnp.int32, (N, N), 0)
    t_i = lax.broadcasted_iota(jnp.int32, (N, N), 1)
    causal = s_i <= t_i
    mixing = jnp.bitwise_xor(s_i, t_i)
    fade = jnp.where(causal, jnp.exp(jnp.where(causal, run - run_col, 0.0)), 0.0)
    weight = jnp.broadcast_to(gain_ref[0, pl.ds(h, 1), :], (N, N))
    for lev in range(1, LVL_IN):
        weight = jnp.where(mixing >= (1 << (lev - 1)), gain_ref[lev, pl.ds(h, 1), :], weight)
    sc = mm(k, qt)
    gv = mm(v, gt)
    wd = weight * fade
    wt = sc * wd
    xt = gv * wd
    pair = sc * gv * fade
    above = [jnp.sum(pair, axis=0, keepdims=True)]
    for lev in range(1, LVL_IN):
        above.append(jnp.sum(jnp.where(mixing >= (1 << (lev - 1)), pair, 0.0), axis=0, keepdims=True))
    above.append(jnp.zeros((1, N), F32))
    for lev in range(LVL_IN):
        dgain_ref[lev, pl.ds(h, 1), :] = above[lev] - above[lev + 1]

    vt2 = jnp.concatenate([vt, vt], axis=1)
    kt2 = jnp.concatenate([kt, kt], axis=1)
    gt2 = jnp.concatenate([gt, gt], axis=0)
    q2 = jnp.concatenate([q, q], axis=1)
    o = jnp.transpose(mm(vt2, tall(wt)))
    dqt = mm(kt2, tall(xt))
    for j in range(XLEV):
        m_hi, m_lo = split(buckets[j])
        o = o + cols[:, j:j + 1] * mm(q2, jnp.concatenate([m_hi, m_lo], axis=0))
        dt = mm(jnp.concatenate([m_hi, m_lo], axis=1), gt2)
        dqt = dqt + rows[j] * dt
        dgain_ref[LVL_IN + j, pl.ds(h, 1), :] = lifts[j] * jnp.sum(dt * qt32, axis=0, keepdims=True)
    o_ref[...] = o.astype(BF16)
    dq_ref[...] = jnp.transpose(dqt).astype(BF16)
    row_sc[pl.ds(h, 1), :] = jnp.sum(dqt * qt32, axis=0, keepdims=True)

    d_hi, d_lo = split(ds_ref[0])
    k2 = jnp.concatenate([k, k], axis=1)
    v2 = jnp.concatenate([v, v], axis=1)
    dv = mm(wide(wt), jnp.concatenate([g, g], axis=0))
    dv = dv + tail_col * mm(k2, jnp.concatenate([d_hi, d_lo], axis=0))
    dk = mm(wide(xt), jnp.concatenate([q, q], axis=0))
    dk = dk + tail_col * mm(v2, jnp.concatenate([d_hi, d_lo], axis=1), NT)
    dk_ref[...] = dk.astype(BF16)
    dv_ref[...] = dv.astype(BF16)
    col = jnp.sum(v.astype(F32) * dv, axis=1, keepdims=True)
    col_sc[...] = jnp.where(t_i == h, col, col_sc[...])

    @pl.when(h == H - 1)
    def _():
        da = row_sc[...] - jnp.transpose(col_sc[...])[0:H, :]
        lower = (s_i >= t_i).astype(F32)
        rev_ref[...] = lax.dot_general(da, lower, NN, precision=lax.Precision.HIGHEST, preferred_element_type=F32)
        tot_ref[...] = lax.dot_general(da, jnp.ones((N, N), F32), NN, precision=lax.Precision.HIGHEST,
                                       preferred_element_type=F32)


def final(q, k, v, g, gain, decay, b0, bk, ds, off):
    col = pl.BlockSpec((N, N), lambda h: (0, h))
    whole3 = pl.BlockSpec((LVL_IN + XLEV, H, N), lambda h: (0, 0, 0))
    whole2 = pl.BlockSpec((H, N), lambda h: (0, 0))
    wide_out = jax.ShapeDtypeStruct((N, H * N), BF16)
    return pl.pallas_call(
        final_kernel,
        grid=(H,),
        in_specs=[col, col, col, col, whole3, whole2,
                  pl.BlockSpec((1, N, N), lambda h: (h, 0, 0)),
                  pl.BlockSpec((XLEV - 1, 1, N, N), lambda h: (0, h, 0, 0)),
                  pl.BlockSpec((1, N, N), lambda h: (h, 0, 0)),
                  pl.BlockSpec((XLEV, H, N), lambda h: (0, 0, 0))],
        out_specs=[col, col, col, col, whole3, whole2, whole2],
        out_shape=[wide_out, wide_out, wide_out, wide_out,
                   jax.ShapeDtypeStruct((LVL_IN + XLEV, H, N), F32),
                   jax.ShapeDtypeStruct((H, N), F32), jax.ShapeDtypeStruct((H, N), F32)],
        scratch_shapes=[pltpu.VMEM((H, N), F32), pltpu.VMEM((H, N), F32),
                        pltpu.VMEM((H, N), F32), pltpu.VMEM((N, N), F32)],
        name="final",
    )(q, k, v, g, gain, decay, b0, bk, ds, off)


def suffix_kernel(rev_ref, tot_ref, out_ref, rowin, zin, sendbuf, ssem, rsem, zssem, zrsem):
    seq = lax.axis_index("seq")
    c, _, _, z = coords()
    r = lax.rem(c, 8)
    barrier = pltpu.get_barrier_semaphore()
    for i in range(1, 8):
        pl.semaphore_signal(barrier, inc=1, device_id=(seq, z * 8 + lax.rem(r + i, 8)), device_id_type=MESH)
        pl.semaphore_signal(barrier, inc=1, device_id=(seq, lax.rem(z + i, 8) * 8 + r), device_id_type=MESH)
    pl.semaphore_wait(barrier, 14)

    def rcopy(i):
        return pltpu.make_async_remote_copy(
            src_ref=tot_ref, dst_ref=rowin.at[i], send_sem=ssem.at[i], recv_sem=rsem.at[i],
            device_id=(seq, z * 8 + lax.rem(r + i, 8)), device_id_type=MESH)

    def zcopy(i):
        return pltpu.make_async_remote_copy(
            src_ref=sendbuf, dst_ref=zin.at[i], send_sem=zssem.at[i], recv_sem=zrsem.at[i],
            device_id=(seq, lax.rem(z + i, 8) * 8 + r), device_id_type=MESH)

    for i in range(1, 8):
        rcopy(i).start()
    total = tot_ref[...]
    after = jnp.zeros((H, N), F32)
    for i in range(1, 8):
        rcopy(i).wait_recv()
        val = rowin[i]
        total = total + val
        after = after + jnp.where(r - i < 0, val, 0.0)
    sendbuf[...] = total
    for i in range(1, 8):
        zcopy(i).start()
    acc = rev_ref[...] + after
    for i in range(1, 8):
        zcopy(i).wait_recv()
        acc = acc + jnp.where(z - i < 0, zin[i], 0.0)
    out_ref[...] = acc
    for i in range(1, 8):
        rcopy(i).wait_send()
        zcopy(i).wait_send()


def suffix(rev, tot):
    vm = pl.BlockSpec(memory_space=pltpu.VMEM)
    dma = pltpu.SemaphoreType.DMA
    return pl.pallas_call(
        suffix_kernel,
        in_specs=[vm, vm],
        out_specs=vm,
        out_shape=jax.ShapeDtypeStruct((H, N), F32),
        scratch_shapes=[pltpu.VMEM((8, H, N), F32), pltpu.VMEM((8, H, N), F32), pltpu.VMEM((H, N), F32),
                        dma((8,)), dma((8,)), dma((8,)), dma((8,))],
        compiler_params=pltpu.CompilerParams(collective_id=1, has_side_effects=True),
        name="suffix",
    )(rev, tot)


def per_device(queries, keys_in, value_input, level_gain, decay_log, out_grad):
    s, big, own = front(queries, keys_in, value_input, out_grad, level_gain, decay_log)
    b0, bk, ds, off = comm(s, big, own)
    o, dq, dk, dv, dgain, rev, tot = final(queries, keys_in, value_input, out_grad, level_gain, decay_log,
                                           b0, bk, ds, off)
    return o, dq, dk, dv, dgain, suffix(rev, tot)


def solution(mesh):
    tokens = P(("seq", "ctx"), None)
    gains = P(None, None, ("seq", "ctx"))
    decays = P(None, ("seq", "ctx"))
    return jax.shard_map(
        per_device,
        mesh=mesh,
        in_specs=(tokens, tokens, tokens, gains, decays, tokens),
        out_specs=(tokens, tokens, tokens, tokens, gains, decays),
        check_vma=False,
    )
```

```python
import jax
import jax.numpy as jnp
from jax import lax
from jax.experimental import pallas as pl
from jax.experimental.pallas import tpu as pltpu
from jax.sharding import PartitionSpec as P

MESH = pl.DeviceIdType.MESH
F32 = jnp.float32
BF16 = jnp.bfloat16
H = 16
HH = 8
N = 128
LVL_IN = 8
XLEV = 6

NN = (((1,), (0,)), ((), ()))
NT = (((1,), (1,)), ((), ()))


def mm(a, b, dims=NN):
    return lax.dot_general(a, b, dims, preferred_element_type=F32)


def split(x):
    hi = x.astype(BF16)
    lo = (x - hi.astype(F32)).astype(BF16)
    return hi, lo


def wide(x):
    hi, lo = split(x)
    return jnp.concatenate([hi, lo], axis=1)


def tall(x):
    hi, lo = split(x)
    return jnp.concatenate([hi, lo], axis=0)


def flip(x):
    return jnp.transpose(x.astype(F32)).astype(BF16)


def running_sums(decay):
    r = lax.broadcasted_iota(jnp.int32, (N, N), 0)
    t = lax.broadcasted_iota(jnp.int32, (N, N), 1)
    upper = (r <= t).astype(F32)
    run = lax.dot_general(decay, upper, NN, precision=lax.Precision.HIGHEST, preferred_element_type=F32)
    tot = lax.dot_general(decay, jnp.ones((N, N), F32), NN, precision=lax.Precision.HIGHEST, preferred_element_type=F32)
    return run, tot


def front_kernel(q_ref, k_ref, v_ref, g_ref, gain_ref, decay_ref, s_ref, big_ref, own_ref, run_sc, tot_sc):
    h = pl.program_id(0)

    @pl.when(h == 0)
    def _():
        run, tot = running_sums(decay_ref[...])
        run_sc[...] = run
        tot_sc[...] = tot
        own_ref[...] = tot

    run = run_sc[pl.ds(h, 1), :]
    tot = tot_sc[pl.ds(h, 1), :]
    v = v_ref[...]
    g = g_ref[...]
    kt = jnp.transpose(k_ref[...].astype(F32))
    qt = jnp.transpose(q_ref[...].astype(F32))
    vv = jnp.concatenate([v, v], axis=0)
    gg = jnp.concatenate([g, g], axis=0)
    s_ref[0] = mm(wide(kt * jnp.exp(tot - run)), vv)
    lift = jnp.exp(run)
    for j in range(XLEV):
        row = gain_ref[LVL_IN + j, pl.ds(h, 1), :] * lift
        big_ref[j, 0] = mm(wide(qt * row), gg)


def front(q, k, v, g, gain, decay):
    col = pl.BlockSpec((N, N), lambda h: (0, h))
    return pl.pallas_call(
        front_kernel,
        grid=(H,),
        in_specs=[col, col, col, col,
                  pl.BlockSpec((LVL_IN + XLEV, H, N), lambda h: (0, 0, 0)),
                  pl.BlockSpec((H, N), lambda h: (0, 0))],
        out_specs=[pl.BlockSpec((1, N, N), lambda h: (h, 0, 0)),
                   pl.BlockSpec((XLEV, 1, N, N), lambda h: (0, h, 0, 0)),
                   pl.BlockSpec((H, N), lambda h: (0, 0))],
        out_shape=[jax.ShapeDtypeStruct((H, N, N), F32),
                   jax.ShapeDtypeStruct((XLEV, H, N, N), F32),
                   jax.ShapeDtypeStruct((H, N), F32)],
        scratch_shapes=[pltpu.VMEM((H, N), F32), pltpu.VMEM((H, N), F32)],
        name="front",
    )(q, k, v, g, gain, decay)


def coords():
    c = lax.axis_index("ctx")
    return c, lax.rem(c, 2), lax.rem(c // 2, 4), c // 8


def pick(parts, cond):
    acc = jnp.zeros((H, N), F32)
    for i in range(8):
        acc = acc + jnp.where(cond(i), parts[i], 0.0)
    return acc


def comm_kernel(s_ref, g_ref, own_ref, b0_ref, bk_ref, ds_ref, off_ref,
                rg, cbuf, mbuf, rbuf, pbuf, qbuf, ebuf, fbuf, abuf, bbuf, ybuf, xbuf, tt, rowt, zt, rsum,
                ssem, rx1, rx2, ry1, ry2, rz, re, ra, rb, rlate, trs, trr, tzs, tzr):
    seq = lax.axis_index("seq")
    c, b, y, z = coords()
    r = lax.rem(c, 8)
    mine = b * HH
    theirs = (1 - b) * HH
    part = c + 1 - 2 * b
    yn = c + 2 - 4 * lax.rem(y, 2)
    ym = c + 2 * (3 - 2 * y)
    up = c + 8
    dn = c - 8
    yodd = lax.rem(y, 2) == 1
    yhi = y >= 2
    zb = [lax.rem(z, 2) == 1, lax.rem(z // 2, 2) == 1, z >= 4]
    row_peer = [z * 8 + lax.rem(r + i, 8) for i in range(8)]
    z_peer = [lax.rem(z + i, 8) * 8 + r for i in range(8)]
    row_from = [lax.rem(r - i + 8, 8) for i in range(8)]
    z_from = [lax.rem(z - i + 8, 8) for i in range(8)]

    barrier = pltpu.get_barrier_semaphore()
    for i in range(1, 8):
        pl.semaphore_signal(barrier, inc=1, device_id=(seq, row_peer[i]), device_id_type=MESH)
        pl.semaphore_signal(barrier, inc=1, device_id=(seq, z_peer[i]), device_id_type=MESH)
    pl.semaphore_wait(barrier, 14)

    def copy(src, dst, send, recv, who):
        return pltpu.make_async_remote_copy(src_ref=src, dst_ref=dst, send_sem=send, recv_sem=recv,
                                            device_id=(seq, who), device_id_type=MESH)

    def x1(h):
        return copy(s_ref.at[theirs + h], b0_ref.at[theirs + h], ssem.at[0], rx1.at[h], part)

    def x1b(h):
        return copy(s_ref.at[h], b0_ref.at[h], ssem.at[1], rlate.at[5], part)

    def x2(j, h):
        return copy(g_ref.at[j, theirs + h], rg.at[j, h], ssem.at[2 + j], rx2.at[j, h], part)

    def x4(j, h):
        return copy(bk_ref.at[j, mine + h], bk_ref.at[j, mine + h], ssem.at[8 + j], rlate.at[j], part)

    def x5(h):
        return copy(xbuf.at[h], ds_ref.at[mine + h], ssem.at[13], rlate.at[6], part)

    def y1(h):
        return copy(cbuf.at[h], bk_ref.at[0, mine + h], ssem.at[14], ry1.at[h], yn)

    def y2(h):
        return copy(mbuf.at[h], bk_ref.at[1, mine + h], ssem.at[15], ry2.at[h], ym)

    def zmsg(j, src, h):
        return copy(src, bk_ref.at[2 + j, mine + h], ssem.at[16 + j], rz.at[j, h], up)

    def emsg(j, h):
        return copy(fbuf.at[j, h], ebuf.at[j, h], ssem.at[19 + j], re.at[j, h], dn)

    def amsg(h):
        return copy(abuf.at[h], ybuf.at[0, h], ssem.at[22], ra.at[h], ym)

    def bmsg(h):
        return copy(bbuf.at[h], ybuf.at[1, h], ssem.at[23], rb.at[h], yn)

    def rtot(i):
        return copy(own_ref, rowt.at[i], trs.at[i], trr.at[i], row_peer[i])

    def ztot(i):
        return copy(rsum, zt.at[i], tzs.at[i], tzr.at[i], z_peer[i])

    setbits = [None, yodd, yhi, zb[0], zb[1], zb[2]]

    def each(fn):
        def body(h, carry):
            fn(h)
            return carry
        lax.fori_loop(0, HH, body, 0)

    for i in range(1, 8):
        rtot(i).start()
    each(lambda h: x1(h).start())
    for j in (5, 4, 3, 2, 1):
        @pl.when(setbits[j])
        def _(j=j):
            each(lambda h: x2(j, h).start())

    @pl.when(b == 0)
    def _():
        each(lambda h: x1b(h).start())

    @pl.when(b == 1)
    def _():
        each(lambda h: x2(0, h).start())

    @pl.when(z == 7)
    def _():
        def zero(h):
            ebuf[2, h] = jnp.zeros((N, N), F32)
        each(zero)

    for i in range(1, 8):
        rtot(i).wait_recv()
    parts = [own_ref[...]] + [rowt[i] for i in range(1, 8)]
    rows = pick(parts, lambda i: row_from[i] >= 0)
    rsum[...] = rows
    for i in range(1, 8):
        ztot(i).start()
    core0 = pick(parts, lambda i: row_from[i] == 2 * y)
    core1 = pick(parts, lambda i: row_from[i] == 2 * y + 1)
    tt[0] = core0
    tt[1] = core1
    tt[2] = pick(parts, lambda i: row_from[i] // 2 == 2 * (y // 2) + 1)
    tt[3] = pick(parts, lambda i: row_from[i] >= 4)
    tt[4] = rows
    tt[5] = pick(parts, lambda i: row_from[i] < 2 * y)
    tt[6] = pick(parts, lambda i: jnp.logical_and(row_from[i] >= 4, row_from[i] < 2 * y))
    tt[7] = jnp.zeros((H, N), F32)
    off_ref[0] = jnp.zeros((H, N), F32)
    off_ref[1] = jnp.where(b == 1, core0, 0.0)
    off_ref[2] = pick(parts, lambda i: jnp.logical_and(row_from[i] >= 4 * (y // 2), row_from[i] < r))         if False else jnp.where(b == 1, core0, 0.0) + pick(
            parts, lambda i: jnp.logical_and(row_from[i] // 2 == y - 1, yodd))
    off3 = pick(parts, lambda i: row_from[i] < r)
    off_ref[3] = off3

    def z_tables():
        for i in range(1, 8):
            ztot(i).wait_recv()
        zp = [tt[4]] + [zt[i] for i in range(1, 8)]
        tt[8] = pick(zp, lambda i: jnp.logical_and(z_from[i] >= z - 1, z_from[i] <= z))
        off_ref[4] = off_ref[3] + pick(zp, lambda i: jnp.logical_and(z_from[i] >= 2 * (z // 2), z_from[i] < z))
        off_ref[5] = off_ref[3] + pick(zp, lambda i: jnp.logical_and(z_from[i] >= 4 * (z // 4), z_from[i] < z))

    def tb(k, h):
        return tt[k, pl.ds(mine + h, 1), :]

    def merge(out, low, high, k, h):
        out[...] = jnp.exp(tb(k, h)) * low[...] + high[...]

    def f1(h):
        x1(h).wait_recv()

        @pl.when(b == 0)
        def _():
            merge(cbuf.at[h], s_ref.at[mine + h], b0_ref.at[mine + h], 1, h)

        @pl.when(b == 1)
        def _():
            merge(cbuf.at[h], b0_ref.at[mine + h], s_ref.at[mine + h], 1, h)

        y1(h).start()

    def f2(h):
        y1(h).wait_recv()
        other = bk_ref.at[0, mine + h]

        @pl.when(yodd)
        def _():
            merge(mbuf.at[h], other, cbuf.at[h], 2, h)
            x4(0, h).start()

        @pl.when(jnp.logical_not(yodd))
        def _():
            merge(mbuf.at[h], cbuf.at[h], other, 2, h)

        y2(h).start()

    def f3(h):
        y2(h).wait_recv()
        other = bk_ref.at[1, mine + h]

        @pl.when(yhi)
        def _():
            merge(rbuf.at[h], other, mbuf.at[h], 3, h)
            x4(1, h).start()

        @pl.when(jnp.logical_not(yhi))
        def _():
            merge(rbuf.at[h], mbuf.at[h], other, 3, h)

        @pl.when(jnp.logical_not(zb[0]))
        def _():
            zmsg(0, rbuf.at[h], h).start()

    def f4(h):
        zmsg(0, rbuf.at[h], h).wait_recv()
        x4(2, h).start()
        merge(pbuf.at[h], bk_ref.at[2, mine + h], rbuf.at[h], 4, h)

        @pl.when(jnp.logical_not(zb[1]))
        def _():
            zmsg(1, pbuf.at[h], h).start()

    def f5(h):
        here = bk_ref.at[3, mine + h]
        zmsg(1, here, h).wait_recv()

        @pl.when(jnp.logical_not(zb[0]))
        def _():
            zmsg(1, here, h).start()

        x4(3, h).start()

        @pl.when(z == 3)
        def _():
            merge(qbuf.at[h], here, pbuf.at[h], 8, h)
            zmsg(2, qbuf.at[h], h).start()

    def f7(h):
        here = bk_ref.at[4, mine + h]
        zmsg(2, here, h).wait_recv()

        @pl.when(z < 7)
        def _():
            zmsg(2, here, h).start()

        x4(4, h).start()

    def chip_grad(j, h, k, wait=True):
        if wait:
            x2(j, h).wait_recv()
        e0 = jnp.exp(tb(0, h))
        off = jnp.exp(tb(k, h))
        low = jnp.where(b == 0, off, e0 * off)
        high = jnp.where(b == 0, e0 * off, off)
        return low * g_ref[j, mine + h] + high * rg[j, h]

    in_slot = [jnp.where(zb[1], 2, 1), jnp.where(zb[0], 2, 1), 2]
    d_slot = jnp.where(zb[0], jnp.where(zb[1], 2, 1), 0)
    in_cond = [jnp.logical_not(zb[0]), zb[0] != zb[1], jnp.logical_and(z >= 3, z < 7)]

    def e_send(j):
        def go(h):
            if j == 1:
                @pl.when(z != 3)
                def _():
                    x2(4, h).wait_recv()
            else:
                x2(3 + j, h).wait_recv()
            fbuf[j, h] = jnp.exp(tb(4, h)) * ebuf[in_slot[j], h] + chip_grad(3 + j, h, 5, False)
            emsg(j, h).start()
        return go

    def e_wait(j):
        return lambda h: emsg(j, h).wait_recv()

    def a_send(h):
        @pl.when(yhi)
        def _():
            abuf[h] = jnp.exp(tb(3, h)) * ebuf[d_slot, h] + chip_grad(2, h, 6)

        @pl.when(jnp.logical_not(yhi))
        def _():
            abuf[h] = ebuf[d_slot, h]

        amsg(h).start()

    def ya(h):
        amsg(h).wait_recv()
        e23 = jnp.where(yhi, 1.0, jnp.exp(tb(3, h)))
        yv = e23 * ebuf[d_slot, h] + ybuf[0, h]
        ybuf[2, h] = yv

        @pl.when(yodd)
        def _():
            bbuf[h] = jnp.exp(tb(2, h)) * yv + chip_grad(1, h, 7)

        @pl.when(jnp.logical_not(yodd))
        def _():
            bbuf[h] = yv

        bmsg(h).start()

    def yb(h):
        bmsg(h).wait_recv()
        e1 = jnp.where(yodd, 1.0, jnp.exp(tb(2, h)))
        dc = e1 * ybuf[2, h] + ybuf[1, h]

        @pl.when(b == 0)
        def _():
            x2(0, h).wait_recv()
            ds_ref[mine + h] = jnp.exp(tb(1, h)) * dc + rg[0, h]
            xbuf[h] = dc

        @pl.when(b == 1)
        def _():
            ds_ref[mine + h] = dc
            xbuf[h] = jnp.exp(tb(1, h)) * dc + g_ref[0, mine + h]

        x5(h).start()

    def hop(n):
        return (5 * n + 1) // 2

    def by_z(vals):
        out = jnp.int32(vals[7])
        for i in range(7):
            out = jnp.where(z == i, vals[i], out)
        return out

    far = 1000
    e5_lag = by_z([far, far, far, hop(4), hop(3), hop(2), hop(1), far])
    e4_in = by_z([far, hop(6), hop(5), far, far, HH + hop(2), HH + hop(1), far])
    e4_out = by_z([far, far, hop(5), hop(4), far, far, HH + hop(1), far])
    e3_out = by_z([far, hop(6), far, 0, far, HH + hop(2), far, far])
    d_lag = by_z([hop(7), hop(6), hop(5), hop(4), HH + hop(3), HH + hop(2), 2 * HH + hop(1), 6])

    def d_ready(h):
        emsg(0, h).wait_recv()

        @pl.when(z == 2)
        def _():
            ebuf[0, h] = ebuf[0, h] + ebuf[1, h]

    def delta_send(h):
        fbuf[0, h] = chip_grad(3, h, 5) - chip_grad(4, h, 5)
        emsg(0, h).start()

    @pl.when(z == 7)
    def _():
        each(e_send(2))
        each(e_send(1))
        each(e_send(0))

    B0 = 2

    def tick(t, carry):
        def stage(fn, lag, cond=None):
            h = t - lag
            ok = jnp.logical_and(h >= 0, h < HH)
            if cond is not None:
                ok = jnp.logical_and(ok, cond)

            @pl.when(ok)
            def _():
                fn(h)

        @pl.when(t == 6)
        def _():
            z_tables()

        stage(f1, 0)
        stage(e_wait(2), B0 + e5_lag)
        stage(e_send(2), B0 + e5_lag, z > 3)
        stage(e_wait(1), B0 + e4_in)
        stage(e_send(1), B0 + e4_out)
        stage(f2, hop(1))
        stage(f3, hop(2))
        stage(f4, hop(3), zb[0])
        stage(f5, hop(4) + jnp.where(zb[0], hop(5) - hop(4), 0), zb[1])
        stage(f7, by_z([far, far, far, far, hop(6), hop(7), hop(8), hop(9)]))
        stage(delta_send, B0 + e3_out, z == 3)
        stage(e_send(0), B0 + e3_out, z != 3)
        stage(d_ready, B0 + d_lag, in_cond[0])
        stage(a_send, B0 + d_lag)
        stage(ya, B0 + d_lag + hop(1))
        stage(yb, B0 + d_lag + hop(2))
        return carry

    lax.fori_loop(0, B0 + 3 * HH + hop(3), tick, 0)

    def all_of(src, dst, send, recv):
        return copy(src, dst, send, recv, part)

    half = pl.ds(0, HH)
    for j in range(5):
        def late(j=j):
            all_of(bk_ref.at[j, half], bk_ref.at[j, half], ssem.at[8 + j], rlate.at[j]).wait()
            all_of(rg.at[j, half], rg.at[j, half], ssem.at[3 + j], rlate.at[j]).wait_send()
        pl.when(setbits[j + 1])(late)

    def sent(k, buf):
        all_of(buf.at[half], buf.at[half], ssem.at[k], rlate.at[5]).wait_send()

    @pl.when(b == 0)
    def _():
        sent(1, s_ref)

    @pl.when(b == 1)
    def _():
        all_of(s_ref.at[half], s_ref.at[half], ssem.at[1], rlate.at[5]).wait_recv()
        sent(2, cbuf)

    all_of(xbuf.at[half], xbuf.at[half], ssem.at[13], rlate.at[6]).wait()
    sent(0, cbuf)
    for k in (14, 15, 22, 23):
        sent(k, cbuf)
    for j in range(3):
        def zsent(j=j):
            sent(16 + j, cbuf)
        pl.when(in_cond[j])(zsent)
        def esent(j=j):
            sent(19 + j, cbuf)
        pl.when(zb[j])(esent)
    for i in range(1, 8):
        rtot(i).wait_send()
        ztot(i).wait_send()


def comm(s, big, own):
    vm = pl.BlockSpec(memory_space=pltpu.VMEM)
    sg = lambda *lead: pltpu.VMEM(lead + (N, N), F32)
    tv = lambda *lead: pltpu.VMEM(lead + (H, N), F32)
    dma = pltpu.SemaphoreType.DMA
    return pl.pallas_call(
        comm_kernel,
        in_specs=[vm, vm, vm],
        out_specs=[vm, vm, vm, vm],
        out_shape=[jax.ShapeDtypeStruct((H, N, N), F32),
                   jax.ShapeDtypeStruct((XLEV - 1, H, N, N), F32),
                   jax.ShapeDtypeStruct((H, N, N), F32),
                   jax.ShapeDtypeStruct((XLEV, H, N), F32)],
        scratch_shapes=[sg(6, HH), sg(HH), sg(HH), sg(HH), sg(HH), sg(HH),
                        sg(3, HH), sg(3, HH), sg(HH), sg(HH), sg(3, HH), sg(HH),
                        tv(9), tv(8), tv(8), tv(),
                        dma((24,)), dma((HH,)), dma((6, HH)), dma((HH,)), dma((HH,)),
                        dma((3, HH)), dma((3, HH)), dma((HH,)), dma((HH,)), dma((7,)),
                        dma((8,)), dma((8,)), dma((8,)), dma((8,))],
        compiler_params=pltpu.CompilerParams(collective_id=0, has_side_effects=True,
                                             vmem_limit_bytes=62 * 1024 * 1024),
        name="states",
    )(s, big, own)


def final_kernel(q_ref, k_ref, v_ref, g_ref, gain_ref, decay_ref, b0_ref, bk_ref, ds_ref, off_ref,
                 o_ref, dq_ref, dk_ref, dv_ref, dgain_ref, rev_ref, tot_ref,
                 run_sc, tot_sc, row_sc, col_sc):
    h = pl.program_id(0)
    c = lax.axis_index("ctx")

    @pl.when(h == 0)
    def _():
        run, tot = running_sums(decay_ref[...])
        run_sc[...] = run
        tot_sc[...] = tot
        col_sc[...] = jnp.zeros((N, N), F32)

    run = run_sc[pl.ds(h, 1), :]
    tot = tot_sc[pl.ds(h, 1), :]
    q, k, v, g = q_ref[...], k_ref[...], v_ref[...], g_ref[...]
    qt32 = jnp.transpose(q.astype(F32))
    qt = qt32.astype(BF16)
    gt, kt, vt = flip(g), flip(k), flip(v)

    bits = [lax.rem(c // (1 << j), 2) == 1 for j in range(XLEV)]
    rows = []
    lifts = []
    buckets = []
    for j in range(XLEV):
        src = b0_ref.at[0] if j == 0 else bk_ref.at[j - 1, 0]
        buckets.append(jnp.where(bits[j], src[...], 0.0))
        lift = jnp.where(bits[j], jnp.exp(run + off_ref[j, pl.ds(h, 1), :]), 0.0)
        lifts.append(lift)
        rows.append(gain_ref[LVL_IN + j, pl.ds(h, 1), :] * lift)
    rows += [run, jnp.exp(tot - run)]
    cols = jnp.transpose(jnp.concatenate(rows + [jnp.zeros((N - 8, N), F32)], axis=0))
    run_col = cols[:, 6:7]
    tail_col = cols[:, 7:8]

    s_i = lax.broadcasted_iota(jnp.int32, (N, N), 0)
    t_i = lax.broadcasted_iota(jnp.int32, (N, N), 1)
    causal = s_i <= t_i
    mixing = jnp.bitwise_xor(s_i, t_i)
    fade = jnp.where(causal, jnp.exp(jnp.where(causal, run - run_col, 0.0)), 0.0)
    weight = jnp.broadcast_to(gain_ref[0, pl.ds(h, 1), :], (N, N))
    for lev in range(1, LVL_IN):
        weight = jnp.where(mixing >= (1 << (lev - 1)), gain_ref[lev, pl.ds(h, 1), :], weight)
    sc = mm(k, qt)
    gv = mm(v, gt)
    wd = weight * fade
    wt = sc * wd
    xt = gv * wd
    pair = sc * gv * fade
    above = [jnp.sum(pair, axis=0, keepdims=True)]
    for lev in range(1, LVL_IN):
        above.append(jnp.sum(jnp.where(mixing >= (1 << (lev - 1)), pair, 0.0), axis=0, keepdims=True))
    above.append(jnp.zeros((1, N), F32))
    for lev in range(LVL_IN):
        dgain_ref[lev, pl.ds(h, 1), :] = above[lev] - above[lev + 1]

    vt2 = jnp.concatenate([vt, vt], axis=1)
    kt2 = jnp.concatenate([kt, kt], axis=1)
    gt2 = jnp.concatenate([gt, gt], axis=0)
    q2 = jnp.concatenate([q, q], axis=1)
    o = jnp.transpose(mm(vt2, tall(wt)))
    dqt = mm(kt2, tall(xt))
    for j in range(XLEV):
        m_hi, m_lo = split(buckets[j])
        o = o + cols[:, j:j + 1] * mm(q2, jnp.concatenate([m_hi, m_lo], axis=0))
        dt = mm(jnp.concatenate([m_hi, m_lo], axis=1), gt2)
        dqt = dqt + rows[j] * dt
        dgain_ref[LVL_IN + j, pl.ds(h, 1), :] = lifts[j] * jnp.sum(dt * qt32, axis=0, keepdims=True)
    o_ref[...] = o.astype(BF16)
    dq_ref[...] = jnp.transpose(dqt).astype(BF16)
    row_sc[pl.ds(h, 1), :] = jnp.sum(dqt * qt32, axis=0, keepdims=True)

    d_hi, d_lo = split(ds_ref[0])
    k2 = jnp.concatenate([k, k], axis=1)
    v2 = jnp.concatenate([v, v], axis=1)
    dv = mm(wide(wt), jnp.concatenate([g, g], axis=0))
    dv = dv + tail_col * mm(k2, jnp.concatenate([d_hi, d_lo], axis=0))
    dk = mm(wide(xt), jnp.concatenate([q, q], axis=0))
    dk = dk + tail_col * mm(v2, jnp.concatenate([d_hi, d_lo], axis=1), NT)
    dk_ref[...] = dk.astype(BF16)
    dv_ref[...] = dv.astype(BF16)
    col = jnp.sum(v.astype(F32) * dv, axis=1, keepdims=True)
    col_sc[...] = jnp.where(t_i == h, col, col_sc[...])

    @pl.when(h == H - 1)
    def _():
        da = row_sc[...] - jnp.transpose(col_sc[...])[0:H, :]
        lower = (s_i >= t_i).astype(F32)
        rev_ref[...] = lax.dot_general(da, lower, NN, precision=lax.Precision.HIGHEST, preferred_element_type=F32)
        tot_ref[...] = lax.dot_general(da, jnp.ones((N, N), F32), NN, precision=lax.Precision.HIGHEST,
                                       preferred_element_type=F32)


def final(q, k, v, g, gain, decay, b0, bk, ds, off):
    col = pl.BlockSpec((N, N), lambda h: (0, h))
    whole3 = pl.BlockSpec((LVL_IN + XLEV, H, N), lambda h: (0, 0, 0))
    whole2 = pl.BlockSpec((H, N), lambda h: (0, 0))
    wide_out = jax.ShapeDtypeStruct((N, H * N), BF16)
    return pl.pallas_call(
        final_kernel,
        grid=(H,),
        in_specs=[col, col, col, col, whole3, whole2,
                  pl.BlockSpec((1, N, N), lambda h: (h, 0, 0)),
                  pl.BlockSpec((XLEV - 1, 1, N, N), lambda h: (0, h, 0, 0)),
                  pl.BlockSpec((1, N, N), lambda h: (h, 0, 0)),
                  pl.BlockSpec((XLEV, H, N), lambda h: (0, 0, 0))],
        out_specs=[col, col, col, col, whole3, whole2, whole2],
        out_shape=[wide_out, wide_out, wide_out, wide_out,
                   jax.ShapeDtypeStruct((LVL_IN + XLEV, H, N), F32),
                   jax.ShapeDtypeStruct((H, N), F32), jax.ShapeDtypeStruct((H, N), F32)],
        scratch_shapes=[pltpu.VMEM((H, N), F32), pltpu.VMEM((H, N), F32),
                        pltpu.VMEM((H, N), F32), pltpu.VMEM((N, N), F32)],
        name="final",
    )(q, k, v, g, gain, decay, b0, bk, ds, off)


def suffix_kernel(rev_ref, tot_ref, out_ref, rowin, zin, sendbuf, ssem, rsem, zssem, zrsem):
    seq = lax.axis_index("seq")
    c, _, _, z = coords()
    r = lax.rem(c, 8)
    barrier = pltpu.get_barrier_semaphore()
    for i in range(1, 8):
        pl.semaphore_signal(barrier, inc=1, device_id=(seq, z * 8 + lax.rem(r + i, 8)), device_id_type=MESH)
        pl.semaphore_signal(barrier, inc=1, device_id=(seq, lax.rem(z + i, 8) * 8 + r), device_id_type=MESH)
    pl.semaphore_wait(barrier, 14)

    def rcopy(i):
        return pltpu.make_async_remote_copy(
            src_ref=tot_ref, dst_ref=rowin.at[i], send_sem=ssem.at[i], recv_sem=rsem.at[i],
            device_id=(seq, z * 8 + lax.rem(r + i, 8)), device_id_type=MESH)

    def zcopy(i):
        return pltpu.make_async_remote_copy(
            src_ref=sendbuf, dst_ref=zin.at[i], send_sem=zssem.at[i], recv_sem=zrsem.at[i],
            device_id=(seq, lax.rem(z + i, 8) * 8 + r), device_id_type=MESH)

    for i in range(1, 8):
        rcopy(i).start()
    total = tot_ref[...]
    after = jnp.zeros((H, N), F32)
    for i in range(1, 8):
        rcopy(i).wait_recv()
        val = rowin[i]
        total = total + val
        after = after + jnp.where(r - i < 0, val, 0.0)
    sendbuf[...] = total
    for i in range(1, 8):
        zcopy(i).start()
    acc = rev_ref[...] + after
    for i in range(1, 8):
        zcopy(i).wait_recv()
        acc = acc + jnp.where(z - i < 0, zin[i], 0.0)
    out_ref[...] = acc
    for i in range(1, 8):
        rcopy(i).wait_send()
        zcopy(i).wait_send()


def suffix(rev, tot):
    vm = pl.BlockSpec(memory_space=pltpu.VMEM)
    dma = pltpu.SemaphoreType.DMA
    return pl.pallas_call(
        suffix_kernel,
        in_specs=[vm, vm],
        out_specs=vm,
        out_shape=jax.ShapeDtypeStruct((H, N), F32),
        scratch_shapes=[pltpu.VMEM((8, H, N), F32), pltpu.VMEM((8, H, N), F32), pltpu.VMEM((H, N), F32),
                        dma((8,)), dma((8,)), dma((8,)), dma((8,))],
        compiler_params=pltpu.CompilerParams(collective_id=1, has_side_effects=True),
        name="suffix",
    )(rev, tot)


def per_device(queries, keys_in, value_input, level_gain, decay_log, out_grad):
    s, big, own = front(queries, keys_in, value_input, out_grad, level_gain, decay_log)
    b0, bk, ds, off = comm(s, big, own)
    o, dq, dk, dv, dgain, rev, tot = final(queries, keys_in, value_input, out_grad, level_gain, decay_log,
                                           b0, bk, ds, off)
    return o, dq, dk, dv, dgain, suffix(rev, tot)


def solution(mesh):
    tokens = P(("seq", "ctx"), None)
    gains = P(None, None, ("seq", "ctx"))
    decays = P(None, ("seq", "ctx"))
    return jax.shard_map(
        per_device,
        mesh=mesh,
        in_specs=(tokens, tokens, tokens, gains, decays, tokens),
        out_specs=(tokens, tokens, tokens, tokens, gains, decays),
        check_vma=False,
    )
```

```python
import jax
import jax.numpy as jnp
from jax import lax
from jax.experimental import pallas as pl
from jax.experimental.pallas import tpu as pltpu
from jax.sharding import PartitionSpec as P

MESH = pl.DeviceIdType.MESH
F32 = jnp.float32
BF16 = jnp.bfloat16
H = 16
HH = 8
N = 128
LVL_IN = 8
XLEV = 6

NN = (((1,), (0,)), ((), ()))
NT = (((1,), (1,)), ((), ()))


def mm(a, b, dims=NN):
    return lax.dot_general(a, b, dims, preferred_element_type=F32)


def split(x):
    hi = x.astype(BF16)
    lo = (x - hi.astype(F32)).astype(BF16)
    return hi, lo


def wide(x):
    hi, lo = split(x)
    return jnp.concatenate([hi, lo], axis=1)


def tall(x):
    hi, lo = split(x)
    return jnp.concatenate([hi, lo], axis=0)


def flip(x):
    return jnp.transpose(x.astype(F32)).astype(BF16)


def running_sums(decay):
    r = lax.broadcasted_iota(jnp.int32, (N, N), 0)
    t = lax.broadcasted_iota(jnp.int32, (N, N), 1)
    upper = (r <= t).astype(F32)
    run = lax.dot_general(decay, upper, NN, precision=lax.Precision.HIGHEST, preferred_element_type=F32)
    tot = lax.dot_general(decay, jnp.ones((N, N), F32), NN, precision=lax.Precision.HIGHEST, preferred_element_type=F32)
    return run, tot


def coords():
    c = lax.axis_index("ctx")
    return c, lax.rem(c, 2), lax.rem(c // 2, 4), c // 8


def pick(parts, cond):
    acc = jnp.zeros((H, N), F32)
    for i in range(8):
        acc = acc + jnp.where(cond(i), parts[i], 0.0)
    return acc


def fused_kernel(q_ref, k_ref, v_ref, g_ref, gain_ref, decay_ref,
                 o_ref, dq_ref, dk_ref, dv_ref, dgain_ref, ddecay_ref,
                 st, g_st, b0, bk, ds, oacc, dqacc, dkacc, dvacc, qt_sc, kt_sc, gt_sc,
                 rg, cbuf, mbuf, rbuf, pbuf, qbuf, ebuf, fbuf, abuf, bbuf, ybuf, xbuf,
                 tt, rowt, zt, rowf, zf, off, rsum, own, run_sc, row_sc, flux, zflux_sum, col_sc,
                 ssem, rx1, rx1b, rx2, rx4, rx5, ry1, ry2, rz, re, ra, rb,
                 trs, trr, tzs, tzr, frs, frr, fzs, fzr):
    seq = lax.axis_index("seq")
    c, b, y, z = coords()
    r = lax.rem(c, 8)
    mine = b * HH
    theirs = (1 - b) * HH
    part = c + 1 - 2 * b
    yn = c + 2 - 4 * lax.rem(y, 2)
    ym = c + 2 * (3 - 2 * y)
    up = c + 8
    dn = c - 8
    yodd = lax.rem(y, 2) == 1
    yhi = y >= 2
    zb = [lax.rem(z, 2) == 1, lax.rem(z // 2, 2) == 1, z >= 4]
    row_peer = [z * 8 + lax.rem(r + i, 8) for i in range(8)]
    z_peer = [lax.rem(z + i, 8) * 8 + r for i in range(8)]
    row_from = [lax.rem(r - i + 8, 8) for i in range(8)]
    z_from = [lax.rem(z - i + 8, 8) for i in range(8)]

    barrier = pltpu.get_barrier_semaphore()
    for i in range(1, 8):
        pl.semaphore_signal(barrier, inc=1, device_id=(seq, row_peer[i]), device_id_type=MESH)
        pl.semaphore_signal(barrier, inc=1, device_id=(seq, z_peer[i]), device_id_type=MESH)
    run, tot = running_sums(decay_ref[...])
    run_sc[...] = run
    own[...] = tot
    dgain_ref[...] = jnp.zeros((LVL_IN + XLEV, H, N), F32)
    pl.semaphore_wait(barrier, 14)

    def copy(src, dst, send, recv, who):
        return pltpu.make_async_remote_copy(src_ref=src, dst_ref=dst, send_sem=send, recv_sem=recv,
                                            device_id=(seq, who), device_id_type=MESH)

    def x1(h):
        return copy(st.at[theirs + h], b0.at[theirs + h], ssem.at[0], rx1.at[h], part)

    def x1b(h):
        return copy(st.at[h], b0.at[h], ssem.at[1], rx1b.at[h], part)

    def x2(j, h):
        return copy(g_st.at[j, theirs + h], rg.at[j, h], ssem.at[2 + j], rx2.at[j, h], part)

    def x4(j, h):
        return copy(bk.at[j, mine + h], bk.at[j, mine + h], ssem.at[8 + j], rx4.at[j, h], part)

    def x5(h):
        return copy(xbuf.at[h], ds.at[mine + h], ssem.at[13], rx5.at[h], part)

    def y1(h):
        return copy(cbuf.at[h], bk.at[0, mine + h], ssem.at[14], ry1.at[h], yn)

    def y2(h):
        return copy(mbuf.at[h], bk.at[1, mine + h], ssem.at[15], ry2.at[h], ym)

    def zmsg(j, src, h):
        return copy(src, bk.at[2 + j, mine + h], ssem.at[16 + j], rz.at[j, h], up)

    def emsg(j, h):
        return copy(fbuf.at[j, h], ebuf.at[j, h], ssem.at[19 + j], re.at[j, h], dn)

    def amsg(h):
        return copy(abuf.at[h], ybuf.at[0, h], ssem.at[22], ra.at[h], ym)

    def bmsg(h):
        return copy(bbuf.at[h], ybuf.at[1, h], ssem.at[23], rb.at[h], yn)

    def rtot(i):
        return copy(own, rowt.at[i], trs.at[i], trr.at[i], row_peer[i])

    def ztot(i):
        return copy(rsum, zt.at[i], tzs.at[i], tzr.at[i], z_peer[i])

    def rflux(i):
        return copy(flux, rowf.at[i], frs.at[i], frr.at[i], row_peer[i])

    def zflux(i):
        return copy(zflux_sum, zf.at[i], fzs.at[i], fzr.at[i], z_peer[i])

    setbits = [None, yodd, yhi, zb[0], zb[1], zb[2]]

    def each(fn):
        def body(h, carry):
            fn(h)
            return carry
        lax.fori_loop(0, HH, body, 0)

    for i in range(1, 8):
        rtot(i).start()

    def cols(h):
        return pl.ds(pl.multiple_of(h * N, N), N)

    def row(ref, h):
        return ref[pl.ds(h, 1), :]

    def make_state(h):
        kt = jnp.transpose(k_ref[:, cols(h)].astype(F32))
        kt_sc[h] = kt.astype(BF16)
        v = v_ref[:, cols(h)]
        st[h] = mm(wide(kt * jnp.exp(row(own, h) - row(run_sc, h))), jnp.concatenate([v, v], axis=0))

    def make_turned(h):
        qt_sc[h] = flip(q_ref[:, cols(h)])
        gt_sc[h] = flip(g_ref[:, cols(h)])

    def make_grad(j, h):
        g = g_ref[:, cols(h)]
        scale = gain_ref[LVL_IN + j, pl.ds(h, 1), :] * jnp.exp(row(run_sc, h))
        g_st[j, h] = mm(wide(qt_sc[h].astype(F32) * scale), jnp.concatenate([g, g], axis=0))

    def state_theirs(h):
        make_state(theirs + h)
        x1(h).start()

    def state_mine(h):
        make_state(mine + h)

        @pl.when(b == 0)
        def _():
            x1b(h).start()

    each(state_theirs)
    each(state_mine)

    @pl.when(z == 7)
    def _():
        def zero(h):
            ebuf[2, h] = jnp.zeros((N, N), F32)
        each(zero)

    for i in range(1, 8):
        rtot(i).wait_recv()
    parts = [own[...]] + [rowt[i] for i in range(1, 8)]
    rows = pick(parts, lambda i: row_from[i] >= 0)
    rsum[...] = rows
    for i in range(1, 8):
        ztot(i).start()
    core0 = pick(parts, lambda i: row_from[i] == 2 * y)
    core1 = pick(parts, lambda i: row_from[i] == 2 * y + 1)
    tt[0] = core0
    tt[1] = core1
    tt[2] = pick(parts, lambda i: row_from[i] // 2 == 2 * (y // 2) + 1)
    tt[3] = pick(parts, lambda i: row_from[i] >= 4)
    tt[4] = rows
    tt[5] = pick(parts, lambda i: row_from[i] < 2 * y)
    tt[6] = pick(parts, lambda i: jnp.logical_and(row_from[i] >= 4, row_from[i] < 2 * y))
    tt[7] = jnp.zeros((H, N), F32)
    off[0] = jnp.zeros((H, N), F32)
    off[1] = jnp.where(b == 1, core0, 0.0)
    off[2] = pick(parts, lambda i: jnp.logical_and(row_from[i] >= 4 * (y // 2), row_from[i] < r))         if False else jnp.where(b == 1, core0, 0.0) + pick(
            parts, lambda i: jnp.logical_and(row_from[i] // 2 == y - 1, yodd))
    off3 = pick(parts, lambda i: row_from[i] < r)
    off[3] = off3

    def z_tables():
        for i in range(1, 8):
            ztot(i).wait_recv()
        zp = [tt[4]] + [zt[i] for i in range(1, 8)]
        tt[8] = pick(zp, lambda i: jnp.logical_and(z_from[i] >= z - 1, z_from[i] <= z))
        off[4] = off[3] + pick(zp, lambda i: jnp.logical_and(z_from[i] >= 2 * (z // 2), z_from[i] < z))
        off[5] = off[3] + pick(zp, lambda i: jnp.logical_and(z_from[i] >= 4 * (z // 4), z_from[i] < z))

    def tb(k, h):
        return tt[k, pl.ds(mine + h, 1), :]

    def merge(out, low, high, k, h):
        out[...] = jnp.exp(tb(k, h)) * low[...] + high[...]

    def f1(h):
        x1(h).wait_recv()

        @pl.when(b == 0)
        def _():
            merge(cbuf.at[h], st.at[mine + h], b0.at[mine + h], 1, h)

        @pl.when(b == 1)
        def _():
            merge(cbuf.at[h], b0.at[mine + h], st.at[mine + h], 1, h)

        y1(h).start()

    def f2(h):
        y1(h).wait_recv()
        other = bk.at[0, mine + h]

        @pl.when(yodd)
        def _():
            merge(mbuf.at[h], other, cbuf.at[h], 2, h)
            x4(0, h).start()

        @pl.when(jnp.logical_not(yodd))
        def _():
            merge(mbuf.at[h], cbuf.at[h], other, 2, h)

        y2(h).start()

    def f3(h):
        y2(h).wait_recv()
        other = bk.at[1, mine + h]

        @pl.when(yhi)
        def _():
            merge(rbuf.at[h], other, mbuf.at[h], 3, h)
            x4(1, h).start()

        @pl.when(jnp.logical_not(yhi))
        def _():
            merge(rbuf.at[h], mbuf.at[h], other, 3, h)

        @pl.when(jnp.logical_not(zb[0]))
        def _():
            zmsg(0, rbuf.at[h], h).start()

    def f4(h):
        zmsg(0, rbuf.at[h], h).wait_recv()
        x4(2, h).start()
        merge(pbuf.at[h], bk.at[2, mine + h], rbuf.at[h], 4, h)

        @pl.when(jnp.logical_not(zb[1]))
        def _():
            zmsg(1, pbuf.at[h], h).start()

    def f5(h):
        here = bk.at[3, mine + h]
        zmsg(1, here, h).wait_recv()

        @pl.when(jnp.logical_not(zb[0]))
        def _():
            zmsg(1, here, h).start()

        x4(3, h).start()

        @pl.when(z == 3)
        def _():
            merge(qbuf.at[h], here, pbuf.at[h], 8, h)
            zmsg(2, qbuf.at[h], h).start()

    def f7(h):
        here = bk.at[4, mine + h]
        zmsg(2, here, h).wait_recv()

        @pl.when(z < 7)
        def _():
            zmsg(2, here, h).start()

        x4(4, h).start()

    def chip_grad(j, h, k, wait=True):
        if wait:
            x2(j, h).wait_recv()
        e0 = jnp.exp(tb(0, h))
        off = jnp.exp(tb(k, h))
        low = jnp.where(b == 0, off, e0 * off)
        high = jnp.where(b == 0, e0 * off, off)
        return low * g_st[j, mine + h] + high * rg[j, h]

    in_slot = [jnp.where(zb[1], 2, 1), jnp.where(zb[0], 2, 1), 2]
    d_slot = jnp.where(zb[0], jnp.where(zb[1], 2, 1), 0)
    in_cond = [jnp.logical_not(zb[0]), zb[0] != zb[1], jnp.logical_and(z >= 3, z < 7)]

    def e_send(j):
        def go(h):
            if j == 1:
                @pl.when(z != 3)
                def _():
                    x2(4, h).wait_recv()
            else:
                x2(3 + j, h).wait_recv()
            fbuf[j, h] = jnp.exp(tb(4, h)) * ebuf[in_slot[j], h] + chip_grad(3 + j, h, 5, False)
            emsg(j, h).start()
        return go

    def e_wait(j):
        return lambda h: emsg(j, h).wait_recv()

    def a_send(h):
        @pl.when(yhi)
        def _():
            abuf[h] = jnp.exp(tb(3, h)) * ebuf[d_slot, h] + chip_grad(2, h, 6)

        @pl.when(jnp.logical_not(yhi))
        def _():
            abuf[h] = ebuf[d_slot, h]

        amsg(h).start()

    def ya(h):
        amsg(h).wait_recv()
        e23 = jnp.where(yhi, 1.0, jnp.exp(tb(3, h)))
        yv = e23 * ebuf[d_slot, h] + ybuf[0, h]
        ybuf[2, h] = yv

        @pl.when(yodd)
        def _():
            bbuf[h] = jnp.exp(tb(2, h)) * yv + chip_grad(1, h, 7)

        @pl.when(jnp.logical_not(yodd))
        def _():
            bbuf[h] = yv

        bmsg(h).start()

    def yb(h):
        bmsg(h).wait_recv()
        e1 = jnp.where(yodd, 1.0, jnp.exp(tb(2, h)))
        dc = e1 * ybuf[2, h] + ybuf[1, h]

        @pl.when(b == 0)
        def _():
            x2(0, h).wait_recv()
            ds[mine + h] = jnp.exp(tb(1, h)) * dc + rg[0, h]
            xbuf[h] = dc

        @pl.when(b == 1)
        def _():
            ds[mine + h] = dc
            xbuf[h] = jnp.exp(tb(1, h)) * dc + g_st[0, mine + h]

        x5(h).start()

    def intra(h):
        run_h = row(run_sc, h)
        run_col = jnp.transpose(jnp.broadcast_to(run_h, (N, N)))
        q, k, v, g = (x[:, cols(h)] for x in (q_ref, k_ref, v_ref, g_ref))
        qt, gt, kt = qt_sc[h], gt_sc[h], kt_sc[h]
        vt = flip(v)
        s_i = lax.broadcasted_iota(jnp.int32, (N, N), 0)
        t_i = lax.broadcasted_iota(jnp.int32, (N, N), 1)
        causal = s_i <= t_i
        mixing = jnp.bitwise_xor(s_i, t_i)
        fade = jnp.where(causal, jnp.exp(jnp.where(causal, run_h - run_col, 0.0)), 0.0)
        weight = jnp.broadcast_to(gain_ref[0, pl.ds(h, 1), :], (N, N))
        for lev in range(1, LVL_IN):
            weight = jnp.where(mixing >= (1 << (lev - 1)), gain_ref[lev, pl.ds(h, 1), :], weight)
        sc = mm(k, qt)
        gv = mm(v, gt)
        wd = weight * fade
        wt = sc * wd
        xt = gv * wd
        pair = sc * gv * fade
        above = [jnp.sum(pair, axis=0, keepdims=True)]
        for lev in range(1, LVL_IN):
            above.append(jnp.sum(jnp.where(mixing >= (1 << (lev - 1)), pair, 0.0), axis=0, keepdims=True))
        above.append(jnp.zeros((1, N), F32))
        for lev in range(LVL_IN):
            dgain_ref[lev, pl.ds(h, 1), :] = above[lev] - above[lev + 1]
        oacc[h] = jnp.transpose(mm(jnp.concatenate([vt, vt], axis=1), tall(wt)))
        dqt = mm(jnp.concatenate([kt, kt], axis=1), tall(xt))
        dqacc[h] = dqt
        row_sc[pl.ds(h, 1), :] = jnp.sum(dqt * qt.astype(F32), axis=0, keepdims=True)
        dvacc[h] = mm(wide(wt), jnp.concatenate([g, g], axis=0))
        dkacc[h] = mm(wide(xt), jnp.concatenate([q, q], axis=0))

    def level(j, h):
        lift = jnp.exp(row(run_sc, h) + off[j, pl.ds(h, 1), :])
        scale = gain_ref[LVL_IN + j, pl.ds(h, 1), :] * lift
        q = q_ref[:, cols(h)]
        gt = gt_sc[h]
        m_hi, m_lo = split(b0[h] if j == 0 else bk[j - 1, h])
        part_o = mm(jnp.concatenate([q, q], axis=1), jnp.concatenate([m_hi, m_lo], axis=0))
        oacc[h] = oacc[h] + jnp.transpose(jnp.broadcast_to(scale, (N, N))) * part_o
        dt = mm(jnp.concatenate([m_hi, m_lo], axis=1), jnp.concatenate([gt, gt], axis=0))
        dqacc[h] = dqacc[h] + scale * dt
        sums = jnp.sum(dt * qt_sc[h].astype(F32), axis=0, keepdims=True)
        dgain_ref[LVL_IN + j, pl.ds(h, 1), :] = lift * sums
        row_sc[pl.ds(h, 1), :] = row_sc[pl.ds(h, 1), :] + scale * sums

    def level_own(j):
        return lambda h: level(j, mine + h)

    def level_other(j):
        def go(h):
            if j == 0:
                x1b(h).wait_recv()
            else:
                copy(bk.at[j - 1, theirs + h], bk.at[j - 1, theirs + h], ssem.at[7 + j], rx4.at[j - 1, h],
                     part).wait_recv()
            level(j, theirs + h)
        return go

    def tail_terms(h):
        tail = jnp.transpose(jnp.broadcast_to(jnp.exp(row(own, h) - row(run_sc, h)), (N, N)))
        k, v = k_ref[:, cols(h)], v_ref[:, cols(h)]
        d_hi, d_lo = split(ds[h])
        dv = dvacc[h] + tail * mm(jnp.concatenate([k, k], axis=1), jnp.concatenate([d_hi, d_lo], axis=0))
        dk = dkacc[h] + tail * mm(jnp.concatenate([v, v], axis=1), jnp.concatenate([d_hi, d_lo], axis=1), NT)
        dk_ref[:, cols(h)] = dk.astype(BF16)
        dv_ref[:, cols(h)] = dv.astype(BF16)
        t_i = lax.broadcasted_iota(jnp.int32, (N, N), 1)
        col_sc[...] = jnp.where(t_i == h, jnp.sum(v.astype(F32) * dv, axis=1, keepdims=True), col_sc[...])

    def tail_own(h):
        tail_terms(mine + h)

    def tail_other(h):
        copy(ds.at[theirs + h], ds.at[theirs + h], ssem.at[13], rx5.at[h], part).wait_recv()
        tail_terms(theirs + h)

    def grads_early(i):
        h = lax.rem(theirs + i, H)
        make_turned(h)

        for j in (5, 4, 3):
            @pl.when(setbits[j])
            def _(j=j):
                make_grad(j, h)

                @pl.when(i < HH)
                def _():
                    x2(j, i).start()

    def grads_late(i):
        h = lax.rem(theirs + i, H)
        for j in (2, 1, 0):
            @pl.when(b == 1 if j == 0 else setbits[j])
            def _(j=j):
                make_grad(j, h)

                @pl.when(i < HH)
                def _():
                    x2(j, i).start()

    def hop(n):
        return (5 * n + 1) // 2

    def by_z(vals):
        out = jnp.int32(vals[7])
        for i in range(7):
            out = jnp.where(z == i, vals[i], out)
        return out

    far = 1000
    e5_lag = by_z([far, far, far, hop(4), hop(3), hop(2), hop(1), far])
    e4_in = by_z([far, hop(6), hop(5), far, far, HH + hop(2), HH + hop(1), far])
    e4_out = by_z([far, far, hop(5), hop(4), far, far, HH + hop(1), far])
    e3_out = by_z([far, hop(6), far, 0, far, HH + hop(2), far, far])
    d_lag = by_z([hop(7), hop(6), hop(5), hop(4), HH + hop(3), HH + hop(2), 2 * HH + hop(1), 8])
    f7_lag = by_z([far, far, far, far, hop(6), hop(7), hop(8), hop(9)])

    def d_ready(h):
        emsg(0, h).wait_recv()

        @pl.when(z == 2)
        def _():
            ebuf[0, h] = ebuf[0, h] + ebuf[1, h]

    def delta_send(h):
        fbuf[0, h] = chip_grad(3, h, 5) - chip_grad(4, h, 5)
        emsg(0, h).start()

    def early(i, carry):
        grads_early(i)
        return carry

    col_sc[...] = jnp.zeros((N, N), F32)
    each(f1)
    lax.fori_loop(0, H, early, 0)

    @pl.when(z == 7)
    def _():
        each(e_send(2))
        each(e_send(1))
        each(e_send(0))

    B0 = 2

    def tick(t, carry):
        def stage(fn, lag, cond=None, count=HH):
            h = t - lag
            ok = jnp.logical_and(h >= 0, h < count)
            if cond is not None:
                ok = jnp.logical_and(ok, cond)

            @pl.when(ok)
            def _():
                fn(h)

        @pl.when(t == 5)
        def _():
            z_tables()

        stage(e_wait(2), B0 + e5_lag)
        stage(e_send(2), B0 + e5_lag, z > 3)
        stage(e_wait(1), B0 + e4_in)
        stage(e_send(1), B0 + e4_out)
        stage(f2, 0)
        stage(f3, hop(2) - hop(1))
        stage(f4, hop(3) - hop(1), zb[0])
        stage(f5, hop(4) - hop(1) + jnp.where(zb[0], hop(5) - hop(4), 0), zb[1])
        stage(f7, f7_lag - hop(1))
        stage(delta_send, B0 + e3_out, z == 3)
        stage(e_send(0), B0 + e3_out, z != 3)
        stage(grads_late, 0, count=H)
        stage(d_ready, B0 + d_lag, in_cond[0])
        stage(a_send, B0 + d_lag)
        stage(ya, B0 + d_lag + hop(1))
        stage(yb, B0 + d_lag + hop(2))
        stage(tail_own, B0 + d_lag + hop(2) + 1)
        stage(tail_other, B0 + d_lag + hop(2) + 2)
        stage(lambda i: intra(lax.rem(mine + i, H)), 0, count=H)
        stage(level_own(0), 2, b == 1)
        stage(level_own(1), 3, setbits[1])
        stage(level_own(2), 6, setbits[2])
        stage(level_own(3), 7, setbits[3])
        stage(level_own(4), 12, setbits[4])
        stage(level_own(5), f7_lag - hop(1) + 1, setbits[5])
        stage(level_other(0), 20, b == 1)
        stage(level_other(1), 15, setbits[1])
        stage(level_other(2), 17, setbits[2])
        stage(level_other(3), 13, setbits[3])
        stage(level_other(4), 14, setbits[4])
        stage(level_other(5), f7_lag - hop(1) + 2, setbits[5])
        return carry

    lax.fori_loop(0, B0 + 3 * HH + hop(4), tick, 0)

    da = row_sc[...] - jnp.transpose(col_sc[...])[0:H, :]
    s_i = lax.broadcasted_iota(jnp.int32, (N, N), 0)
    t_i = lax.broadcasted_iota(jnp.int32, (N, N), 1)
    flux[...] = lax.dot_general(da, jnp.ones((N, N), F32), NN, precision=lax.Precision.HIGHEST,
                                preferred_element_type=F32)
    for i in range(1, 8):
        rflux(i).start()

    def put_out(h):
        o_ref[:, cols(h)] = oacc[h].astype(BF16)
        dq_ref[:, cols(h)] = jnp.transpose(dqacc[h]).astype(BF16)

    def put(h, carry):
        put_out(h)
        return carry

    lax.fori_loop(0, HH, put, 0)
    total = flux[...]
    after = lax.dot_general(da, (s_i >= t_i).astype(F32), NN, precision=lax.Precision.HIGHEST,
                            preferred_element_type=F32)
    for i in range(1, 8):
        rflux(i).wait_recv()
        val = rowf[i]
        total = total + val
        after = after + jnp.where(row_from[i] > r, val, 0.0)
    zflux_sum[...] = total
    for i in range(1, 8):
        zflux(i).start()
    lax.fori_loop(HH, H, put, 0)
    for i in range(1, 8):
        zflux(i).wait_recv()
        after = after + jnp.where(z_from[i] > z, zf[i], 0.0)
    ddecay_ref[...] = after

    def all_of(src, dst, send, recv):
        return copy(src, dst, send, recv, part)

    half = pl.ds(0, HH)

    def sent(k, buf):
        all_of(buf.at[half], buf.at[half], ssem.at[k], rx1.at[0]).wait_send()

    for j in range(5):
        def late(j=j):
            sent(8 + j, cbuf)
            sent(3 + j, cbuf)
        pl.when(setbits[j + 1])(late)

    @pl.when(b == 0)
    def _():
        sent(1, cbuf)

    @pl.when(b == 1)
    def _():
        sent(2, cbuf)

    sent(0, cbuf)
    for k in (13, 14, 15, 22, 23):
        sent(k, cbuf)
    for j in range(3):
        def zsent(j=j):
            sent(16 + j, cbuf)
        pl.when(in_cond[j])(zsent)
        def esent(j=j):
            sent(19 + j, cbuf)
        pl.when(zb[j])(esent)
    for i in range(1, 8):
        rtot(i).wait_send()
        ztot(i).wait_send()
        rflux(i).wait_send()
        zflux(i).wait_send()


def fused(q, k, v, g, gain, decay):
    vm = pl.BlockSpec(memory_space=pltpu.VMEM)
    sg = lambda *lead: pltpu.VMEM(lead + (N, N), F32)
    sh = lambda *lead: pltpu.VMEM(lead + (N, N), BF16)
    tv = lambda *lead: pltpu.VMEM(lead + (H, N), F32)
    dma = pltpu.SemaphoreType.DMA
    wide_out = jax.ShapeDtypeStruct((N, H * N), BF16)
    return pl.pallas_call(
        fused_kernel,
        in_specs=[vm] * 6,
        out_specs=[vm] * 6,
        out_shape=[wide_out, wide_out, wide_out, wide_out,
                   jax.ShapeDtypeStruct((LVL_IN + XLEV, H, N), F32),
                   jax.ShapeDtypeStruct((H, N), F32)],
        scratch_shapes=[sg(H), sg(XLEV, H), sg(H), sg(XLEV - 1, H), sg(H), sg(H), sg(H), sg(H), sg(H),
                        sh(H), sh(H), sh(H),
                        sg(6, HH), sg(HH), sg(HH), sg(HH), sg(HH), sg(HH),
                        sg(3, HH), sg(3, HH), sg(HH), sg(HH), sg(3, HH), sg(HH),
                        tv(9), tv(8), tv(8), tv(8), tv(8), tv(XLEV), tv(), tv(), tv(), tv(), tv(), tv(), sg(),
                        dma((24,)), dma((HH,)), dma((HH,)), dma((6, HH)), dma((5, HH)), dma((HH,)),
                        dma((HH,)), dma((HH,)), dma((3, HH)), dma((3, HH)), dma((HH,)), dma((HH,))]
                       + [dma((8,))] * 8,
        compiler_params=pltpu.CompilerParams(collective_id=0, has_side_effects=True,
                                             vmem_limit_bytes=62 * 1024 * 1024),
        name="fused",
    )(q, k, v, g, gain, decay)


def per_device(queries, keys_in, value_input, level_gain, decay_log, out_grad):
    return tuple(fused(queries, keys_in, value_input, out_grad, level_gain, decay_log))


def solution(mesh):
    tokens = P(("seq", "ctx"), None)
    gains = P(None, None, ("seq", "ctx"))
    decays = P(None, ("seq", "ctx"))
    return jax.shard_map(
        per_device,
        mesh=mesh,
        in_specs=(tokens, tokens, tokens, gains, decays, tokens),
        out_specs=(tokens, tokens, tokens, tokens, gains, decays),
        check_vma=False,
    )
```

```python
import jax
import jax.numpy as jnp
from jax import lax
from jax.experimental import pallas as pl
from jax.experimental.pallas import tpu as pltpu
from jax.sharding import PartitionSpec as P

MESH = pl.DeviceIdType.MESH
F32 = jnp.float32
BF16 = jnp.bfloat16
H = 16
HH = 8
N = 128
LVL_IN = 8
XLEV = 6

NN = (((1,), (0,)), ((), ()))
NT = (((1,), (1,)), ((), ()))


def mm(a, b, dims=NN):
    return lax.dot_general(a, b, dims, preferred_element_type=F32)


def split(x):
    hi = x.astype(BF16)
    lo = (x - hi.astype(F32)).astype(BF16)
    return hi, lo


def wide(x):
    hi, lo = split(x)
    return jnp.concatenate([hi, lo], axis=1)


def tall(x):
    hi, lo = split(x)
    return jnp.concatenate([hi, lo], axis=0)


def flip(x):
    return jnp.transpose(x.astype(F32)).astype(BF16)


def running_sums(decay):
    r = lax.broadcasted_iota(jnp.int32, (N, N), 0)
    t = lax.broadcasted_iota(jnp.int32, (N, N), 1)
    upper = (r <= t).astype(F32)
    run = lax.dot_general(decay, upper, NN, precision=lax.Precision.HIGHEST, preferred_element_type=F32)
    tot = lax.dot_general(decay, jnp.ones((N, N), F32), NN, precision=lax.Precision.HIGHEST, preferred_element_type=F32)
    return run, tot


def coords():
    c = lax.axis_index("ctx")
    return c, lax.rem(c, 2), lax.rem(c // 2, 4), c // 8


def pick(parts, cond):
    acc = jnp.zeros((H, N), F32)
    for i in range(8):
        acc = acc + jnp.where(cond(i), parts[i], 0.0)
    return acc


def fused_kernel(q_in, k_in, v_in, g_in, gain_in, decay_in,
                 o_ref, dq_ref, dk_ref, dv_ref, dgain_ref, ddecay_ref,
                 st, g_st, b0, bk, ds, oacc, dqacc, dkacc, dvacc, qt_sc, kt_sc, gt_sc,
                 rg, cbuf, mbuf, rbuf, pbuf, qbuf, ebuf, fbuf, abuf, bbuf, ybuf, xbuf,
                 tt, rowt, zt, rowf, off, rsum, own, run_sc, row_sc, flux, flow_sc, col_sc,
                 ssem, rx1, rx1b, rx2, rx4, rx5, ry1, ry2, rz, re, ra, rb,
                 trs, trr, tzs, tzr, frs, frr,
                 q_ref, k_ref, v_ref, g_ref, gain_ref, decay_ref, insem):
    seq = lax.axis_index("seq")
    c, b, y, z = coords()
    r = lax.rem(c, 8)
    mine = b * HH
    theirs = (1 - b) * HH
    part = c + 1 - 2 * b
    yn = c + 2 - 4 * lax.rem(y, 2)
    ym = c + 2 * (3 - 2 * y)
    up = c + 8
    dn = c - 8
    yodd = lax.rem(y, 2) == 1
    yhi = y >= 2
    zb = [lax.rem(z, 2) == 1, lax.rem(z // 2, 2) == 1, z >= 4]
    row_peer = [z * 8 + lax.rem(r + i, 8) for i in range(8)]
    row_from = [lax.rem(r - i + 8, 8) for i in range(8)]

    loads = [pltpu.make_async_copy(src, dst, insem.at[i]) for i, (src, dst) in enumerate((
        (decay_in, decay_ref), (k_in, k_ref), (v_in, v_ref), (q_in, q_ref), (g_in, g_ref), (gain_in, gain_ref)))]
    for load in loads:
        load.start()
    barrier = pltpu.get_barrier_semaphore()
    for i in range(1, 8):
        pl.semaphore_signal(barrier, inc=1, device_id=(seq, row_peer[i]), device_id_type=MESH)

    @pl.when(z < 7)
    def _():
        pl.semaphore_signal(barrier, inc=1, device_id=(seq, up), device_id_type=MESH)

    @pl.when(z > 0)
    def _():
        pl.semaphore_signal(barrier, inc=1, device_id=(seq, dn), device_id_type=MESH)

    loads[0].wait()
    run, tot = running_sums(decay_ref[...])
    run_sc[...] = run
    own[...] = tot
    dgain_ref[...] = jnp.zeros((LVL_IN + XLEV, H, N), F32)
    col_sc[...] = jnp.zeros((N, N), F32)
    flow_sc[...] = jnp.zeros((H, N), F32)

    def cols(h):
        return pl.ds(pl.multiple_of(h * N, N), N)

    def row(ref, h):
        return ref[pl.ds(h, 1), :]

    def make_state(h):
        kt = jnp.transpose(k_ref[:, cols(h)].astype(F32))
        kt_sc[h] = kt.astype(BF16)
        v = v_ref[:, cols(h)]
        st[h] = mm(wide(kt * jnp.exp(row(own, h) - row(run_sc, h))), jnp.concatenate([v, v], axis=0))

    def states_first(h, carry):
        make_state(theirs + h)
        return carry

    loads[1].wait()
    loads[2].wait()
    lax.fori_loop(0, HH, states_first, 0)
    pl.semaphore_wait(barrier, 7 + jnp.minimum(z, 1) + jnp.minimum(7 - z, 1))

    def copy(src, dst, send, recv, who):
        return pltpu.make_async_remote_copy(src_ref=src, dst_ref=dst, send_sem=send, recv_sem=recv,
                                            device_id=(seq, who), device_id_type=MESH)

    def x1(h):
        return copy(st.at[theirs + h], b0.at[theirs + h], ssem.at[0], rx1.at[h], part)

    def x1b(h):
        return copy(st.at[h], b0.at[h], ssem.at[1], rx1b.at[h], part)

    def x2(j, h):
        return copy(g_st.at[j, theirs + h], rg.at[j, h], ssem.at[2 + j], rx2.at[j, h], part)

    def x4(j, h):
        return copy(bk.at[j, mine + h], bk.at[j, mine + h], ssem.at[8 + j], rx4.at[j, h], part)

    def x5(h):
        return copy(xbuf.at[h], ds.at[mine + h], ssem.at[13], rx5.at[h], part)

    def y1(h):
        return copy(cbuf.at[h], bk.at[0, mine + h], ssem.at[14], ry1.at[h], yn)

    def y2(h):
        return copy(mbuf.at[h], bk.at[1, mine + h], ssem.at[15], ry2.at[h], ym)

    def zmsg(j, src, h):
        return copy(src, bk.at[2 + j, mine + h], ssem.at[16 + j], rz.at[j, h], up)

    def emsg(j, h):
        return copy(fbuf.at[j, h], ebuf.at[j, h], ssem.at[19 + j], re.at[j, h], dn)

    def amsg(h):
        return copy(abuf.at[h], ybuf.at[0, h], ssem.at[22], ra.at[h], ym)

    def bmsg(h):
        return copy(bbuf.at[h], ybuf.at[1, h], ssem.at[23], rb.at[h], yn)

    def rtot(i):
        return copy(own, rowt.at[i], trs.at[i], trr.at[i], z * 8 + lax.rem(r + i, 8))

    def ztot():
        return copy(rsum, zt, tzs.at[0], tzr.at[0], up)

    def rflux(i):
        return copy(flux, rowf.at[i], frs.at[i], frr.at[i], row_peer[i])

    setbits = [None, yodd, yhi, zb[0], zb[1], zb[2]]

    def each(fn):
        def body(h, carry):
            fn(h)
            return carry
        lax.fori_loop(0, HH, body, 0)

    rtot(jnp.where(b == 0, 1, 7)).start()
    each(lambda h: x1(h).start())
    rtot(jnp.where(b == 0, 7, 1)).start()
    for i in range(2, 7):
        rtot(i).start()

    def make_turned(h):
        qt_sc[h] = flip(q_ref[:, cols(h)])
        gt_sc[h] = flip(g_ref[:, cols(h)])

    def make_grad(j, h):
        g = g_ref[:, cols(h)]
        scale = gain_ref[LVL_IN + j, pl.ds(h, 1), :] * jnp.exp(row(run_sc, h))
        g_st[j, h] = mm(wide(qt_sc[h].astype(F32) * scale), jnp.concatenate([g, g], axis=0))

    def state_mine(h):
        make_state(mine + h)

        @pl.when(b == 0)
        def _():
            x1b(h).start()

    each(state_mine)

    @pl.when(z == 7)
    def _():
        def zero(h):
            ebuf[2, h] = jnp.zeros((N, N), F32)
        each(zero)

    pair_slot = jnp.where(b == 0, 7, 1)
    rtot(pair_slot).wait_recv()
    tt[0] = jnp.where(b == 0, own[...], rowt[pair_slot])
    tt[1] = jnp.where(b == 0, rowt[pair_slot], own[...])

    def row_tables():
        rtot(8 - pair_slot).wait_recv()
        for i in range(2, 7):
            rtot(i).wait_recv()
        parts = [own[...]] + [rowt[i] for i in range(1, 8)]
        rows = pick(parts, lambda i: row_from[i] >= 0)
        rsum[1] = rows
        tt[2] = pick(parts, lambda i: row_from[i] // 2 == 2 * (y // 2) + 1)
        tt[3] = pick(parts, lambda i: row_from[i] >= 4)
        tt[4] = rows
        tt[5] = pick(parts, lambda i: row_from[i] < 2 * y)
        tt[6] = pick(parts, lambda i: jnp.logical_and(row_from[i] >= 4, row_from[i] < 2 * y))
        tt[7] = jnp.zeros((H, N), F32)
        off[0] = jnp.zeros((H, N), F32)
        off[1] = jnp.where(b == 1, tt[0], 0.0)
        off[2] = pick(parts, lambda i: jnp.logical_and(row_from[i] >= 4 * (y // 2), row_from[i] < r))
        off[3] = pick(parts, lambda i: row_from[i] < r)

    zq = lax.rem(z, 4)

    def z_tables():
        @pl.when(zq == 0)
        def _():
            zt[...] = jnp.zeros((2, H, N), F32)

        @pl.when(zq > 0)
        def _():
            ztot().wait_recv()

        below, last = zt[0], zt[1]
        tt[8] = tt[4] + last
        tt[9] = tt[4] + below
        off[4] = off[3] + jnp.where(zb[0], last, 0.0)
        off[5] = off[3] + below
        rsum[0] = tt[4] + below

        @pl.when(zq < 3)
        def _():
            ztot().start()

    def tb(k, h):
        return tt[k, pl.ds(mine + h, 1), :]

    def merge(out, low, high, k, h):
        out[...] = jnp.exp(tb(k, h)) * low[...] + high[...]

    def f1(h):
        x1(h).wait_recv()

        @pl.when(b == 0)
        def _():
            merge(cbuf.at[h], st.at[mine + h], b0.at[mine + h], 1, h)

        @pl.when(b == 1)
        def _():
            merge(cbuf.at[h], b0.at[mine + h], st.at[mine + h], 1, h)

        y1(h).start()

    def f2(h):
        y1(h).wait_recv()
        other = bk.at[0, mine + h]

        @pl.when(yodd)
        def _():
            merge(mbuf.at[h], other, cbuf.at[h], 2, h)
            x4(0, h).start()

        @pl.when(jnp.logical_not(yodd))
        def _():
            merge(mbuf.at[h], cbuf.at[h], other, 2, h)

        y2(h).start()

    def f3(h):
        y2(h).wait_recv()
        other = bk.at[1, mine + h]

        @pl.when(yhi)
        def _():
            merge(rbuf.at[h], other, mbuf.at[h], 3, h)
            x4(1, h).start()

        @pl.when(jnp.logical_not(yhi))
        def _():
            merge(rbuf.at[h], mbuf.at[h], other, 3, h)

        @pl.when(jnp.logical_not(zb[0]))
        def _():
            zmsg(0, rbuf.at[h], h).start()

    def f4(h):
        zmsg(0, rbuf.at[h], h).wait_recv()
        x4(2, h).start()
        merge(pbuf.at[h], bk.at[2, mine + h], rbuf.at[h], 4, h)

        @pl.when(jnp.logical_not(zb[1]))
        def _():
            zmsg(1, pbuf.at[h], h).start()

    def f5(h):
        here = bk.at[3, mine + h]
        zmsg(1, here, h).wait_recv()

        @pl.when(jnp.logical_not(zb[0]))
        def _():
            zmsg(1, here, h).start()

        x4(3, h).start()

        @pl.when(z == 3)
        def _():
            merge(qbuf.at[h], here, pbuf.at[h], 8, h)
            zmsg(2, qbuf.at[h], h).start()

    def f7(h):
        here = bk.at[4, mine + h]
        zmsg(2, here, h).wait_recv()

        @pl.when(z < 7)
        def _():
            zmsg(2, here, h).start()

        x4(4, h).start()

    def chip_grad(j, h, k, wait=True):
        if wait:
            x2(j, h).wait_recv()
        e0 = jnp.exp(tb(0, h))
        off = jnp.exp(tb(k, h))
        low = jnp.where(b == 0, off, e0 * off)
        high = jnp.where(b == 0, e0 * off, off)
        return low * g_st[j, mine + h] + high * rg[j, h]

    in_slot = [jnp.where(zb[1], 2, 1), jnp.where(zb[0], 2, 1), 2]
    d_slot = jnp.where(zb[0], jnp.where(zb[1], 2, 1), 0)
    in_cond = [jnp.logical_not(zb[0]), zb[0] != zb[1], jnp.logical_and(z >= 3, z < 7)]

    def e_send(j):
        def go(h):
            if j == 1:
                @pl.when(z != 3)
                def _():
                    x2(4, h).wait_recv()
            else:
                x2(3 + j, h).wait_recv()
            fbuf[j, h] = jnp.exp(tb(4, h)) * ebuf[in_slot[j], h] + chip_grad(3 + j, h, 5, False)
            emsg(j, h).start()
        return go

    def e_wait(j):
        return lambda h: emsg(j, h).wait_recv()

    def a_send(h):
        @pl.when(yhi)
        def _():
            abuf[h] = jnp.exp(tb(3, h)) * ebuf[d_slot, h] + chip_grad(2, h, 6)

        @pl.when(jnp.logical_not(yhi))
        def _():
            abuf[h] = ebuf[d_slot, h]

        amsg(h).start()

    def ya(h):
        amsg(h).wait_recv()
        e23 = jnp.where(yhi, 1.0, jnp.exp(tb(3, h)))
        yv = e23 * ebuf[d_slot, h] + ybuf[0, h]
        ybuf[2, h] = yv

        @pl.when(yodd)
        def _():
            bbuf[h] = jnp.exp(tb(2, h)) * yv + chip_grad(1, h, 7)

        @pl.when(jnp.logical_not(yodd))
        def _():
            bbuf[h] = yv

        bmsg(h).start()

    def yb(h):
        bmsg(h).wait_recv()
        e1 = jnp.where(yodd, 1.0, jnp.exp(tb(2, h)))
        dc = e1 * ybuf[2, h] + ybuf[1, h]

        @pl.when(b == 0)
        def _():
            x2(0, h).wait_recv()
            ds[mine + h] = jnp.exp(tb(1, h)) * dc + rg[0, h]
            xbuf[h] = dc

        @pl.when(b == 1)
        def _():
            ds[mine + h] = dc
            xbuf[h] = jnp.exp(tb(1, h)) * dc + g_st[0, mine + h]

        x5(h).start()

    def intra(h):
        run_h = row(run_sc, h)
        run_col = jnp.transpose(jnp.broadcast_to(run_h, (N, N)))
        q, k, v, g = (x[:, cols(h)] for x in (q_ref, k_ref, v_ref, g_ref))
        qt, gt, kt = qt_sc[h], gt_sc[h], kt_sc[h]
        vt = flip(v)
        s_i = lax.broadcasted_iota(jnp.int32, (N, N), 0)
        t_i = lax.broadcasted_iota(jnp.int32, (N, N), 1)
        causal = s_i <= t_i
        mixing = jnp.bitwise_xor(s_i, t_i)
        fade = jnp.where(causal, jnp.exp(jnp.where(causal, run_h - run_col, 0.0)), 0.0)
        weight = jnp.broadcast_to(gain_ref[0, pl.ds(h, 1), :], (N, N))
        for lev in range(1, LVL_IN):
            weight = jnp.where(mixing >= (1 << (lev - 1)), gain_ref[lev, pl.ds(h, 1), :], weight)
        sc = mm(k, qt)
        gv = mm(v, gt)
        wd = weight * fade
        wt = sc * wd
        xt = gv * wd
        pair = sc * gv * fade
        above = [jnp.sum(pair, axis=0, keepdims=True)]
        for lev in range(1, LVL_IN):
            above.append(jnp.sum(jnp.where(mixing >= (1 << (lev - 1)), pair, 0.0), axis=0, keepdims=True))
        above.append(jnp.zeros((1, N), F32))
        for lev in range(LVL_IN):
            dgain_ref[lev, pl.ds(h, 1), :] = above[lev] - above[lev + 1]
        oacc[h] = jnp.transpose(mm(jnp.concatenate([vt, vt], axis=1), tall(wt)))
        dqt = mm(jnp.concatenate([kt, kt], axis=1), tall(xt))
        dqacc[h] = dqt
        row_sc[pl.ds(h, 1), :] = jnp.sum(dqt * qt.astype(F32), axis=0, keepdims=True)
        dvacc[h] = mm(wide(wt), jnp.concatenate([g, g], axis=0))
        dkacc[h] = mm(wide(xt), jnp.concatenate([q, q], axis=0))

    def level(j, h):
        lift = jnp.exp(row(run_sc, h) + off[j, pl.ds(h, 1), :])
        scale = gain_ref[LVL_IN + j, pl.ds(h, 1), :] * lift
        q = q_ref[:, cols(h)]
        gt = gt_sc[h]
        m_hi, m_lo = split(b0[h] if j == 0 else bk[j - 1, h])
        part_o = mm(jnp.concatenate([q, q], axis=1), jnp.concatenate([m_hi, m_lo], axis=0))
        oacc[h] = oacc[h] + jnp.transpose(jnp.broadcast_to(scale, (N, N))) * part_o
        dt = mm(jnp.concatenate([m_hi, m_lo], axis=1), jnp.concatenate([gt, gt], axis=0))
        dqacc[h] = dqacc[h] + scale * dt
        sums = jnp.sum(dt * qt_sc[h].astype(F32), axis=0, keepdims=True)
        dgain_ref[LVL_IN + j, pl.ds(h, 1), :] = lift * sums
        row_sc[pl.ds(h, 1), :] = row_sc[pl.ds(h, 1), :] + scale * sums

    def level_own(j):
        return lambda h: level(j, mine + h)

    def level_other(j):
        def go(h):
            if j == 0:
                x1b(h).wait_recv()
            else:
                copy(bk.at[j - 1, theirs + h], bk.at[j - 1, theirs + h], ssem.at[7 + j], rx4.at[j - 1, h],
                     part).wait_recv()
            level(j, theirs + h)
        return go

    def tail_terms(h):
        tail = jnp.transpose(jnp.broadcast_to(jnp.exp(row(own, h) - row(run_sc, h)), (N, N)))
        k, v = k_ref[:, cols(h)], v_ref[:, cols(h)]
        d_hi, d_lo = split(ds[h])
        dv = dvacc[h] + tail * mm(jnp.concatenate([k, k], axis=1), jnp.concatenate([d_hi, d_lo], axis=0))
        dk = dkacc[h] + tail * mm(jnp.concatenate([v, v], axis=1), jnp.concatenate([d_hi, d_lo], axis=1), NT)
        dk_ref[:, cols(h)] = dk.astype(BF16)
        dv_ref[:, cols(h)] = dv.astype(BF16)
        t_i = lax.broadcasted_iota(jnp.int32, (N, N), 1)
        col_sc[...] = jnp.where(t_i == h, jnp.sum(v.astype(F32) * dv, axis=1, keepdims=True), col_sc[...])

    def flow(h):
        acc = main_state(h) * ebuf[d_slot, h]
        flow_sc[pl.ds(mine + h, 1), :] = jnp.sum(acc, axis=0, keepdims=True)

        def more(j, k):
            term = jnp.sum(bk[j, mine + h] * ebuf[j - 2, h], axis=0, keepdims=True)
            flow_sc[pl.ds(mine + h, 1), :] = flow_sc[pl.ds(mine + h, 1), :] + jnp.exp(tb(k, h)) * term

        @pl.when(jnp.logical_and(zb[1], jnp.logical_not(zb[0])))
        def _():
            more(3, 4)

        @pl.when(jnp.logical_and(z > 3, z < 7))
        def _():
            more(4, 9)

    def main_state(h):
        upper = jnp.where(z == 3, qbuf[h], pbuf[h])
        return jnp.where(zb[0], upper, rbuf[h])

    def tail_own(h):
        tail_terms(mine + h)

    def tail_other(h):
        copy(ds.at[theirs + h], ds.at[theirs + h], ssem.at[13], rx5.at[h], part).wait_recv()
        tail_terms(theirs + h)

    def grads_early(i):
        h = lax.rem(theirs + i, H)
        make_turned(h)

        for j in (5, 4, 3):
            @pl.when(setbits[j])
            def _(j=j):
                make_grad(j, h)

                @pl.when(i < HH)
                def _():
                    x2(j, i).start()

    def grads_late(i):
        h = lax.rem(theirs + i, H)
        for j in (2, 1, 0):
            @pl.when(b == 1 if j == 0 else setbits[j])
            def _(j=j):
                make_grad(j, h)

                @pl.when(i < HH)
                def _():
                    x2(j, i).start()

    def hop(n):
        return (5 * n + 1) // 2

    def by_z(vals):
        out = jnp.int32(vals[7])
        for i in range(7):
            out = jnp.where(z == i, vals[i], out)
        return out

    far = 1000
    e5_lag = by_z([far, far, far, hop(4), hop(3), hop(2), hop(1), far])
    e4_in = by_z([far, hop(6), hop(5), far, far, HH + hop(2), HH + hop(1), far])
    e4_out = by_z([far, far, hop(5), hop(4), far, far, HH + hop(1), far])
    e3_out = by_z([far, hop(6), far, 0, far, HH + hop(2), far, far])
    d_lag = by_z([hop(7), hop(6), hop(5), hop(4), HH + hop(3), HH + hop(2), 2 * HH + hop(1), 8])
    f7_lag = by_z([far, far, far, far, hop(6), hop(7), hop(8), hop(9)])

    def d_ready(h):
        emsg(0, h).wait_recv()

        @pl.when(z == 2)
        def _():
            ebuf[0, h] = ebuf[0, h] + ebuf[1, h]

    def delta_send(h):
        fbuf[0, h] = chip_grad(3, h, 5) - chip_grad(4, h, 5)
        emsg(0, h).start()

    def early(i, carry):
        grads_early(i)
        return carry

    each(f1)
    row_tables()
    for load in loads[3:]:
        load.wait()
    lax.fori_loop(0, H, early, 0)

    @pl.when(z == 7)
    def _():
        each(e_send(2))
        each(e_send(1))
        each(e_send(0))

    B0 = 2

    def tick(t, carry):
        def stage(fn, lag, cond=None, count=HH):
            h = t - lag
            ok = jnp.logical_and(h >= 0, h < count)
            if cond is not None:
                ok = jnp.logical_and(ok, cond)

            @pl.when(ok)
            def _():
                fn(h)

        @pl.when(t == 2 * zq + 1)
        def _():
            z_tables()

        stage(e_wait(2), B0 + e5_lag)
        stage(e_send(2), B0 + e5_lag, z > 3)
        stage(e_wait(1), B0 + e4_in)
        stage(e_send(1), B0 + e4_out)
        stage(f2, 0)
        stage(f3, hop(2) - hop(1))
        stage(f4, hop(3) - hop(1), zb[0])
        stage(f5, hop(4) - hop(1) + jnp.where(zb[0], hop(5) - hop(4), 0), zb[1])
        stage(f7, f7_lag - hop(1))
        stage(delta_send, B0 + e3_out, z == 3)
        stage(e_send(0), B0 + e3_out, z != 3)
        stage(grads_late, 0, count=H)
        stage(d_ready, B0 + d_lag, in_cond[0])
        stage(a_send, B0 + d_lag)
        stage(flow, B0 + d_lag + 1)
        stage(ya, B0 + d_lag + hop(1))
        stage(yb, B0 + d_lag + hop(2))
        stage(tail_own, B0 + d_lag + hop(2) + 1)
        stage(tail_other, B0 + d_lag + hop(2) + 2)
        stage(lambda i: intra(lax.rem(mine + i, H)), 0, count=H)
        stage(level_own(0), 2, b == 1)
        stage(level_own(1), 3, setbits[1])
        stage(level_own(2), 6, setbits[2])
        stage(level_own(3), 7, setbits[3])
        stage(level_own(4), 12, setbits[4])
        stage(level_own(5), f7_lag - hop(1) + 1, setbits[5])
        stage(level_other(0), 20, b == 1)
        stage(level_other(1), 15, setbits[1])
        stage(level_other(2), 17, setbits[2])
        stage(level_other(3), 13, setbits[3])
        stage(level_other(4), 14, setbits[4])
        stage(level_other(5), f7_lag - hop(1) + 2, setbits[5])
        return carry

    lax.fori_loop(0, B0 + 3 * HH + hop(4), tick, 0)

    da = row_sc[...] - jnp.transpose(col_sc[...])[0:H, :]
    s_i = lax.broadcasted_iota(jnp.int32, (N, N), 0)
    t_i = lax.broadcasted_iota(jnp.int32, (N, N), 1)
    ones = jnp.ones((N, N), F32)

    def dot01(a, m):
        return lax.dot_general(a, m, NN, precision=lax.Precision.HIGHEST, preferred_element_type=F32)

    flux[0] = dot01(da, ones)
    flux[1] = dot01(flow_sc[...], ones)
    for i in range(1, 8):
        rflux(i).start()

    def put(h, carry):
        o_ref[:, cols(h)] = oacc[h].astype(BF16)
        dq_ref[:, cols(h)] = jnp.transpose(dqacc[h]).astype(BF16)
        return carry

    lax.fori_loop(0, H, put, 0)
    after = dot01(da, (s_i >= t_i).astype(F32)) + flux[1]
    for i in range(1, 8):
        rflux(i).wait_recv()
        after = after + rowf[i, 1] + jnp.where(row_from[i] > r, rowf[i, 0], 0.0)
    ddecay_ref[...] = after

    def all_of(src, dst, send, recv):
        return copy(src, dst, send, recv, part)

    half = pl.ds(0, HH)

    def sent(k, buf):
        all_of(buf.at[half], buf.at[half], ssem.at[k], rx1.at[0]).wait_send()

    for j in range(5):
        def late(j=j):
            sent(8 + j, cbuf)
            sent(3 + j, cbuf)
        pl.when(setbits[j + 1])(late)

    @pl.when(b == 0)
    def _():
        sent(1, cbuf)

    @pl.when(b == 1)
    def _():
        sent(2, cbuf)

    sent(0, cbuf)
    for k in (13, 14, 15, 22, 23):
        sent(k, cbuf)
    for j in range(3):
        def zsent(j=j):
            sent(16 + j, cbuf)
        pl.when(in_cond[j])(zsent)
        def esent(j=j):
            sent(19 + j, cbuf)
        pl.when(zb[j])(esent)
    for i in range(1, 8):
        rtot(i).wait_send()
        rflux(i).wait_send()

    @pl.when(zq < 3)
    def _():
        ztot().wait_send()


def fused(q, k, v, g, gain, decay):
    vm = pl.BlockSpec(memory_space=pltpu.VMEM)
    sg = lambda *lead: pltpu.VMEM(lead + (N, N), F32)
    sh = lambda *lead: pltpu.VMEM(lead + (N, N), BF16)
    tv = lambda *lead: pltpu.VMEM(lead + (H, N), F32)
    dma = pltpu.SemaphoreType.DMA
    wide_out = jax.ShapeDtypeStruct((N, H * N), BF16)
    return pl.pallas_call(
        fused_kernel,
        in_specs=[pl.BlockSpec(memory_space=pltpu.MemorySpace.HBM)] * 6,
        out_specs=[vm] * 6,
        out_shape=[wide_out, wide_out, wide_out, wide_out,
                   jax.ShapeDtypeStruct((LVL_IN + XLEV, H, N), F32),
                   jax.ShapeDtypeStruct((H, N), F32)],
        scratch_shapes=[sg(H), sg(XLEV, H), sg(H), sg(XLEV - 1, H), sg(H), sg(H), sg(H), sg(H), sg(H),
                        sh(H), sh(H), sh(H),
                        sg(6, HH), sg(HH), sg(HH), sg(HH), sg(HH), sg(HH),
                        sg(3, HH), sg(3, HH), sg(HH), sg(HH), sg(3, HH), sg(HH),
                        tv(10), tv(8), tv(2), tv(8, 2), tv(XLEV), tv(2), tv(), tv(), tv(), tv(2), tv(), sg(),
                        dma((24,)), dma((HH,)), dma((HH,)), dma((6, HH)), dma((5, HH)), dma((HH,)),
                        dma((HH,)), dma((HH,)), dma((3, HH)), dma((3, HH)), dma((HH,)), dma((HH,))]
                       + [dma((8,))] * 6
                       + [pltpu.VMEM((N, H * N), BF16)] * 4
                       + [tv(LVL_IN + XLEV), tv(), dma((6,))],
        compiler_params=pltpu.CompilerParams(collective_id=0, has_side_effects=True,
                                             vmem_limit_bytes=44 * 1024 * 1024),
        name="fused",
    )(q, k, v, g, gain, decay)


def finish_kernel(*refs):
    ins, outs, sem = refs[:6], refs[6:12], refs[12]
    for i in range(6):
        pltpu.make_async_copy(ins[i], outs[i], sem.at[i]).start()
    for i in range(6):
        pltpu.make_async_copy(ins[i], outs[i], sem.at[i]).wait()


def finish(*arrays):
    return pl.pallas_call(
        finish_kernel,
        in_specs=[pl.BlockSpec(memory_space=pltpu.VMEM)] * 6,
        out_specs=[pl.BlockSpec(memory_space=pl.ANY)] * 6,
        out_shape=[jax.ShapeDtypeStruct(a.shape, a.dtype) for a in arrays],
        scratch_shapes=[pltpu.SemaphoreType.DMA((6,))],
        compiler_params=pltpu.CompilerParams(vmem_limit_bytes=8 * 1024 * 1024),
        name="finish",
    )(*arrays)


def per_device(queries, keys_in, value_input, level_gain, decay_log, out_grad):
    return tuple(finish(*fused(queries, keys_in, value_input, out_grad, level_gain, decay_log)))


def solution(mesh):
    tokens = P(("seq", "ctx"), None)
    gains = P(None, None, ("seq", "ctx"))
    decays = P(None, ("seq", "ctx"))
    return jax.shard_map(
        per_device,
        mesh=mesh,
        in_specs=(tokens, tokens, tokens, gains, decays, tokens),
        out_specs=(tokens, tokens, tokens, tokens, gains, decays),
        check_vma=False,
    )
```

```python
import jax
import jax.numpy as jnp
from jax import lax
from jax.experimental import pallas as pl
from jax.experimental.pallas import tpu as pltpu
from jax.sharding import PartitionSpec as P

MESH = pl.DeviceIdType.MESH
F32 = jnp.float32
BF16 = jnp.bfloat16
H = 16
HH = 8
N = 128
LVL_IN = 8
XLEV = 6

NN = (((1,), (0,)), ((), ()))
NT = (((1,), (1,)), ((), ()))


def mm(a, b, dims=NN):
    return lax.dot_general(a, b, dims, preferred_element_type=F32)


def split(x):
    hi = x.astype(BF16)
    lo = (x - hi.astype(F32)).astype(BF16)
    return hi, lo


def wide(x):
    hi, lo = split(x)
    return jnp.concatenate([hi, lo], axis=1)


def tall(x):
    hi, lo = split(x)
    return jnp.concatenate([hi, lo], axis=0)


def flip(x):
    return jnp.transpose(x.astype(F32)).astype(BF16)


def running_sums(decay):
    r = lax.broadcasted_iota(jnp.int32, (N, N), 0)
    t = lax.broadcasted_iota(jnp.int32, (N, N), 1)
    upper = (r <= t).astype(F32)
    run = lax.dot_general(decay, upper, NN, precision=lax.Precision.HIGHEST, preferred_element_type=F32)
    tot = lax.dot_general(decay, jnp.ones((N, N), F32), NN, precision=lax.Precision.HIGHEST, preferred_element_type=F32)
    return run, tot


def coords():
    c = lax.axis_index("ctx")
    return c, lax.rem(c, 2), lax.rem(c // 2, 4), c // 8


def pick(parts, cond):
    acc = jnp.zeros((H, N), F32)
    for i in range(8):
        acc = acc + jnp.where(cond(i), parts[i], 0.0)
    return acc


def fused_kernel(q_in, k_in, v_in, g_in, gain_in, decay_in,
                 o_ref, dq_ref, dk_ref, dv_ref, dgain_ref, ddecay_ref,
                 st, g_st, b0, bk, ds, oacc, dqacc, dkacc, dvacc, qt_sc, kt_sc, gt_sc,
                 rg, cbuf, mbuf, rbuf, pbuf, qbuf, ebuf, fbuf, abuf, bbuf, ybuf, xbuf,
                 tt, rowt, zt, rowf, off, rsum, own, run_sc, row_sc, flux, flow_sc, col_sc,
                 ssem, rx1, rx1b, rx2, rx4, rx5, ry1, ry2, rz, re, ra, rb,
                 trs, trr, tzs, tzr, frs, frr,
                 q_ref, k_ref, v_ref, g_ref, gain_ref, decay_ref, insem):
    seq = lax.axis_index("seq")
    c, b, y, z = coords()
    r = lax.rem(c, 8)
    mine = b * HH
    theirs = (1 - b) * HH
    part = c + 1 - 2 * b
    yn = c + 2 - 4 * lax.rem(y, 2)
    ym = c + 2 * (3 - 2 * y)
    up = c + 8
    dn = c - 8
    yodd = lax.rem(y, 2) == 1
    yhi = y >= 2
    zb = [lax.rem(z, 2) == 1, lax.rem(z // 2, 2) == 1, z >= 4]
    row_peer = [z * 8 + lax.rem(r + i, 8) for i in range(8)]
    row_from = [lax.rem(r - i + 8, 8) for i in range(8)]

    loads = [pltpu.make_async_copy(src, dst, insem.at[i]) for i, (src, dst) in enumerate((
        (decay_in, decay_ref), (k_in, k_ref), (v_in, v_ref), (q_in, q_ref), (g_in, g_ref), (gain_in, gain_ref)))]
    for load in loads:
        load.start()
    barrier = pltpu.get_barrier_semaphore()
    for i in range(1, 8):
        pl.semaphore_signal(barrier, inc=1, device_id=(seq, row_peer[i]), device_id_type=MESH)

    @pl.when(z < 7)
    def _():
        pl.semaphore_signal(barrier, inc=1, device_id=(seq, up), device_id_type=MESH)

    @pl.when(z > 0)
    def _():
        pl.semaphore_signal(barrier, inc=1, device_id=(seq, dn), device_id_type=MESH)

    loads[0].wait()
    run, tot = running_sums(decay_ref[...])
    run_sc[...] = run
    own[...] = tot
    dgain_ref[...] = jnp.zeros((LVL_IN + XLEV, H, N), F32)
    col_sc[...] = jnp.zeros((N, N), F32)
    flow_sc[...] = jnp.zeros((H, N), F32)

    def cols(h):
        return pl.ds(pl.multiple_of(h * N, N), N)

    def row(ref, h):
        return ref[pl.ds(h, 1), :]

    def make_state(h):
        kt = jnp.transpose(k_ref[:, cols(h)].astype(F32))
        kt_sc[h] = kt.astype(BF16)
        v = v_ref[:, cols(h)]
        st[h] = mm(wide(kt * jnp.exp(row(own, h) - row(run_sc, h))), jnp.concatenate([v, v], axis=0))

    def states_first(h, carry):
        make_state(theirs + h)
        return carry

    loads[1].wait()
    loads[2].wait()
    last_row = z == 7

    @pl.when(jnp.logical_not(last_row))
    def _():
        lax.fori_loop(0, HH, states_first, 0)

    pl.semaphore_wait(barrier, 7 + jnp.minimum(z, 1) + jnp.minimum(7 - z, 1))

    def copy(src, dst, send, recv, who):
        return pltpu.make_async_remote_copy(src_ref=src, dst_ref=dst, send_sem=send, recv_sem=recv,
                                            device_id=(seq, who), device_id_type=MESH)

    def x1(h):
        return copy(st.at[theirs + h], b0.at[theirs + h], ssem.at[0], rx1.at[h], part)

    def x1b(h):
        return copy(st.at[h], b0.at[h], ssem.at[1], rx1b.at[h], part)

    def x2(j, h):
        return copy(g_st.at[j, theirs + h], rg.at[j, h], ssem.at[2 + j], rx2.at[j, h], part)

    def x4(j, h):
        return copy(bk.at[j, mine + h], bk.at[j, mine + h], ssem.at[8 + j], rx4.at[j, h], part)

    def x5(h):
        return copy(xbuf.at[h], ds.at[mine + h], ssem.at[13], rx5.at[h], part)

    def y1(h):
        return copy(cbuf.at[h], bk.at[0, mine + h], ssem.at[14], ry1.at[h], yn)

    def y2(h):
        return copy(mbuf.at[h], bk.at[1, mine + h], ssem.at[15], ry2.at[h], ym)

    def zmsg(j, src, h):
        return copy(src, bk.at[2 + j, mine + h], ssem.at[16 + j], rz.at[j, h], up)

    def emsg(j, h):
        return copy(fbuf.at[j, h], ebuf.at[j, h], ssem.at[19 + j], re.at[j, h], dn)

    def amsg(h):
        return copy(abuf.at[h], ybuf.at[0, h], ssem.at[22], ra.at[h], ym)

    def bmsg(h):
        return copy(bbuf.at[h], ybuf.at[1, h], ssem.at[23], rb.at[h], yn)

    def rtot(i):
        return copy(own, rowt.at[i], trs.at[i], trr.at[i], z * 8 + lax.rem(r + i, 8))

    def ztot():
        return copy(rsum, zt, tzs.at[0], tzr.at[0], up)

    def rflux(i):
        return copy(flux, rowf.at[i], frs.at[i], frr.at[i], row_peer[i])

    setbits = [None, yodd, yhi, zb[0], zb[1], zb[2]]

    def each(fn):
        def body(h, carry):
            fn(h)
            return carry
        lax.fori_loop(0, HH, body, 0)

    rtot(jnp.where(b == 0, 1, 7)).start()

    @pl.when(jnp.logical_not(last_row))
    def _():
        each(lambda h: x1(h).start())

    rtot(jnp.where(b == 0, 7, 1)).start()
    for i in range(2, 7):
        rtot(i).start()

    def make_turned(h):
        qt_sc[h] = flip(q_ref[:, cols(h)])
        gt_sc[h] = flip(g_ref[:, cols(h)])

    def make_grad(j, h):
        g = g_ref[:, cols(h)]
        scale = gain_ref[LVL_IN + j, pl.ds(h, 1), :] * jnp.exp(row(run_sc, h))
        g_st[j, h] = mm(wide(qt_sc[h].astype(F32) * scale), jnp.concatenate([g, g], axis=0))

    def state_mine(h):
        make_state(mine + h)

        @pl.when(b == 0)
        def _():
            x1b(h).start()

    @pl.when(jnp.logical_not(last_row))
    def _():
        each(state_mine)

    for load in loads[3:]:
        load.wait()

    def all_heads(fn):
        def body(i, carry):
            fn(i)
            return carry
        lax.fori_loop(0, H, body, 0)

    def grad_and_send(j):
        def go(i):
            h = lax.rem(theirs + i, H)
            make_grad(j, h)

            @pl.when(i < HH)
            def _():
                x2(j, i).start()
        return go

    def turned_and_top():
        all_heads(make_turned)

        @pl.when(setbits[5])
        def _():
            all_heads(grad_and_send(5))

    @pl.when(last_row)
    def _():
        def partner_head(h):
            make_turned(theirs + h)
            grad_and_send(5)(h)
        each(partner_head)


    @pl.when(z == 7)
    def _():
        def zero(h):
            ebuf[2, h] = jnp.zeros((N, N), F32)
        each(zero)

    pair_slot = jnp.where(b == 0, 7, 1)
    rtot(pair_slot).wait_recv()
    tt[0] = jnp.where(b == 0, own[...], rowt[pair_slot])
    tt[1] = jnp.where(b == 0, rowt[pair_slot], own[...])

    def row_tables():
        rtot(8 - pair_slot).wait_recv()
        for i in range(2, 7):
            rtot(i).wait_recv()
        parts = [own[...]] + [rowt[i] for i in range(1, 8)]
        rows = pick(parts, lambda i: row_from[i] >= 0)
        rsum[1] = rows
        tt[2] = pick(parts, lambda i: row_from[i] // 2 == 2 * (y // 2) + 1)
        tt[3] = pick(parts, lambda i: row_from[i] >= 4)
        tt[4] = rows
        tt[5] = pick(parts, lambda i: row_from[i] < 2 * y)
        tt[6] = pick(parts, lambda i: jnp.logical_and(row_from[i] >= 4, row_from[i] < 2 * y))
        tt[7] = jnp.zeros((H, N), F32)
        off[0] = jnp.zeros((H, N), F32)
        off[1] = jnp.where(b == 1, tt[0], 0.0)
        off[2] = pick(parts, lambda i: jnp.logical_and(row_from[i] >= 4 * (y // 2), row_from[i] < r))
        off[3] = pick(parts, lambda i: row_from[i] < r)

    zq = lax.rem(z, 4)

    def z_tables():
        @pl.when(zq == 0)
        def _():
            zt[...] = jnp.zeros((2, H, N), F32)

        @pl.when(zq > 0)
        def _():
            ztot().wait_recv()

        below, last = zt[0], zt[1]
        tt[8] = tt[4] + last
        tt[9] = tt[4] + below
        off[4] = off[3] + jnp.where(zb[0], last, 0.0)
        off[5] = off[3] + below
        rsum[0] = tt[4] + below

        @pl.when(zq < 3)
        def _():
            ztot().start()

    def tb(k, h):
        return tt[k, pl.ds(mine + h, 1), :]

    def merge(out, low, high, k, h):
        out[...] = jnp.exp(tb(k, h)) * low[...] + high[...]

    def f1(h):
        x1(h).wait_recv()

        @pl.when(b == 0)
        def _():
            merge(cbuf.at[h], st.at[mine + h], b0.at[mine + h], 1, h)

        @pl.when(b == 1)
        def _():
            merge(cbuf.at[h], b0.at[mine + h], st.at[mine + h], 1, h)

        y1(h).start()

    def f2(h):
        y1(h).wait_recv()
        other = bk.at[0, mine + h]

        @pl.when(yodd)
        def _():
            merge(mbuf.at[h], other, cbuf.at[h], 2, h)
            x4(0, h).start()

        @pl.when(jnp.logical_not(yodd))
        def _():
            merge(mbuf.at[h], cbuf.at[h], other, 2, h)

        y2(h).start()

    def f3(h):
        y2(h).wait_recv()
        other = bk.at[1, mine + h]

        @pl.when(yhi)
        def _():
            merge(rbuf.at[h], other, mbuf.at[h], 3, h)
            x4(1, h).start()

        @pl.when(jnp.logical_not(yhi))
        def _():
            merge(rbuf.at[h], mbuf.at[h], other, 3, h)

        @pl.when(jnp.logical_not(zb[0]))
        def _():
            zmsg(0, rbuf.at[h], h).start()

    def f4(h):
        zmsg(0, rbuf.at[h], h).wait_recv()
        x4(2, h).start()
        merge(pbuf.at[h], bk.at[2, mine + h], rbuf.at[h], 4, h)

        @pl.when(jnp.logical_not(zb[1]))
        def _():
            zmsg(1, pbuf.at[h], h).start()

    def f5(h):
        here = bk.at[3, mine + h]
        zmsg(1, here, h).wait_recv()

        @pl.when(jnp.logical_not(zb[0]))
        def _():
            zmsg(1, here, h).start()

        x4(3, h).start()

        @pl.when(z == 3)
        def _():
            merge(qbuf.at[h], here, pbuf.at[h], 8, h)
            zmsg(2, qbuf.at[h], h).start()

    def f7(h):
        here = bk.at[4, mine + h]
        zmsg(2, here, h).wait_recv()

        @pl.when(z < 7)
        def _():
            zmsg(2, here, h).start()

        x4(4, h).start()

    def chip_grad(j, h, k, wait=True):
        if wait:
            x2(j, h).wait_recv()
        e0 = jnp.exp(tb(0, h))
        off = jnp.exp(tb(k, h))
        low = jnp.where(b == 0, off, e0 * off)
        high = jnp.where(b == 0, e0 * off, off)
        return low * g_st[j, mine + h] + high * rg[j, h]

    in_slot = [jnp.where(zb[1], 2, 1), jnp.where(zb[0], 2, 1), 2]
    d_slot = jnp.where(zb[0], jnp.where(zb[1], 2, 1), 0)
    in_cond = [jnp.logical_not(zb[0]), zb[0] != zb[1], jnp.logical_and(z >= 3, z < 7)]

    def e_send(j):
        def go(h):
            if j == 1:
                @pl.when(z != 3)
                def _():
                    x2(4, h).wait_recv()
            else:
                x2(3 + j, h).wait_recv()
            fbuf[j, h] = jnp.exp(tb(4, h)) * ebuf[in_slot[j], h] + chip_grad(3 + j, h, 5, False)
            emsg(j, h).start()
        return go

    def e_wait(j):
        return lambda h: emsg(j, h).wait_recv()

    def a_send(h):
        @pl.when(yhi)
        def _():
            abuf[h] = jnp.exp(tb(3, h)) * ebuf[d_slot, h] + chip_grad(2, h, 6)

        @pl.when(jnp.logical_not(yhi))
        def _():
            abuf[h] = ebuf[d_slot, h]

        amsg(h).start()

    def ya(h):
        amsg(h).wait_recv()
        e23 = jnp.where(yhi, 1.0, jnp.exp(tb(3, h)))
        yv = e23 * ebuf[d_slot, h] + ybuf[0, h]
        ybuf[2, h] = yv

        @pl.when(yodd)
        def _():
            bbuf[h] = jnp.exp(tb(2, h)) * yv + chip_grad(1, h, 7)

        @pl.when(jnp.logical_not(yodd))
        def _():
            bbuf[h] = yv

        bmsg(h).start()

    def yb(h):
        bmsg(h).wait_recv()
        e1 = jnp.where(yodd, 1.0, jnp.exp(tb(2, h)))
        dc = e1 * ybuf[2, h] + ybuf[1, h]

        @pl.when(b == 0)
        def _():
            x2(0, h).wait_recv()
            ds[mine + h] = jnp.exp(tb(1, h)) * dc + rg[0, h]
            xbuf[h] = dc

        @pl.when(b == 1)
        def _():
            ds[mine + h] = dc
            xbuf[h] = jnp.exp(tb(1, h)) * dc + g_st[0, mine + h]

        x5(h).start()

    def intra(h):
        run_h = row(run_sc, h)
        run_col = jnp.transpose(jnp.broadcast_to(run_h, (N, N)))
        q, k, v, g = (x[:, cols(h)] for x in (q_ref, k_ref, v_ref, g_ref))
        qt, gt, kt = qt_sc[h], gt_sc[h], kt_sc[h]
        vt = flip(v)
        s_i = lax.broadcasted_iota(jnp.int32, (N, N), 0)
        t_i = lax.broadcasted_iota(jnp.int32, (N, N), 1)
        causal = s_i <= t_i
        mixing = jnp.bitwise_xor(s_i, t_i)
        fade = jnp.where(causal, jnp.exp(jnp.where(causal, run_h - run_col, 0.0)), 0.0)
        weight = jnp.broadcast_to(gain_ref[0, pl.ds(h, 1), :], (N, N))
        for lev in range(1, LVL_IN):
            weight = jnp.where(mixing >= (1 << (lev - 1)), gain_ref[lev, pl.ds(h, 1), :], weight)
        sc = mm(k, qt)
        gv = mm(v, gt)
        wd = weight * fade
        wt = sc * wd
        xt = gv * wd
        pair = sc * gv * fade
        above = [jnp.sum(pair, axis=0, keepdims=True)]
        for lev in range(1, LVL_IN):
            above.append(jnp.sum(jnp.where(mixing >= (1 << (lev - 1)), pair, 0.0), axis=0, keepdims=True))
        above.append(jnp.zeros((1, N), F32))
        for lev in range(LVL_IN):
            dgain_ref[lev, pl.ds(h, 1), :] = above[lev] - above[lev + 1]
        oacc[h] = jnp.transpose(mm(jnp.concatenate([vt, vt], axis=1), tall(wt)))
        dqt = mm(jnp.concatenate([kt, kt], axis=1), tall(xt))
        dqacc[h] = dqt
        row_sc[pl.ds(h, 1), :] = jnp.sum(dqt * qt.astype(F32), axis=0, keepdims=True)
        dvacc[h] = mm(wide(wt), jnp.concatenate([g, g], axis=0))
        dkacc[h] = mm(wide(xt), jnp.concatenate([q, q], axis=0))

    def level(j, h):
        lift = jnp.exp(row(run_sc, h) + off[j, pl.ds(h, 1), :])
        scale = gain_ref[LVL_IN + j, pl.ds(h, 1), :] * lift
        q = q_ref[:, cols(h)]
        gt = gt_sc[h]
        m_hi, m_lo = split(b0[h] if j == 0 else bk[j - 1, h])
        part_o = mm(jnp.concatenate([q, q], axis=1), jnp.concatenate([m_hi, m_lo], axis=0))
        oacc[h] = oacc[h] + jnp.transpose(jnp.broadcast_to(scale, (N, N))) * part_o
        dt = mm(jnp.concatenate([m_hi, m_lo], axis=1), jnp.concatenate([gt, gt], axis=0))
        dqacc[h] = dqacc[h] + scale * dt
        sums = jnp.sum(dt * qt_sc[h].astype(F32), axis=0, keepdims=True)
        dgain_ref[LVL_IN + j, pl.ds(h, 1), :] = lift * sums
        row_sc[pl.ds(h, 1), :] = row_sc[pl.ds(h, 1), :] + scale * sums

    def level_own(j):
        return lambda h: level(j, mine + h)

    def level_other(j):
        def go(h):
            if j == 0:
                x1b(h).wait_recv()
            else:
                copy(bk.at[j - 1, theirs + h], bk.at[j - 1, theirs + h], ssem.at[7 + j], rx4.at[j - 1, h],
                     part).wait_recv()
            level(j, theirs + h)
        return go

    def tail_terms(h):
        tail = jnp.transpose(jnp.broadcast_to(jnp.exp(row(own, h) - row(run_sc, h)), (N, N)))
        k, v = k_ref[:, cols(h)], v_ref[:, cols(h)]
        d_hi, d_lo = split(ds[h])
        dv = dvacc[h] + tail * mm(jnp.concatenate([k, k], axis=1), jnp.concatenate([d_hi, d_lo], axis=0))
        dk = dkacc[h] + tail * mm(jnp.concatenate([v, v], axis=1), jnp.concatenate([d_hi, d_lo], axis=1), NT)
        dk_ref[:, cols(h)] = dk.astype(BF16)
        dv_ref[:, cols(h)] = dv.astype(BF16)
        t_i = lax.broadcasted_iota(jnp.int32, (N, N), 1)
        col_sc[...] = jnp.where(t_i == h, jnp.sum(v.astype(F32) * dv, axis=1, keepdims=True), col_sc[...])

    def flow(h):
        acc = main_state(h) * ebuf[d_slot, h]
        flow_sc[pl.ds(mine + h, 1), :] = jnp.sum(acc, axis=0, keepdims=True)

        def more(j, k):
            term = jnp.sum(bk[j, mine + h] * ebuf[j - 2, h], axis=0, keepdims=True)
            flow_sc[pl.ds(mine + h, 1), :] = flow_sc[pl.ds(mine + h, 1), :] + jnp.exp(tb(k, h)) * term

        @pl.when(jnp.logical_and(zb[1], jnp.logical_not(zb[0])))
        def _():
            more(3, 4)

        @pl.when(jnp.logical_and(z > 3, z < 7))
        def _():
            more(4, 9)

    def main_state(h):
        upper = jnp.where(z == 3, qbuf[h], pbuf[h])
        return jnp.where(zb[0], upper, rbuf[h])

    def tail_own(h):
        tail_terms(mine + h)

    def tail_other(h):
        copy(ds.at[theirs + h], ds.at[theirs + h], ssem.at[13], rx5.at[h], part).wait_recv()
        tail_terms(theirs + h)

    def grads_late(i):
        h = lax.rem(theirs + i, H)
        for j in (2, 1, 0):
            @pl.when(b == 1 if j == 0 else setbits[j])
            def _(j=j):
                make_grad(j, h)

                @pl.when(i < HH)
                def _():
                    x2(j, i).start()

    def hop(n):
        return (5 * n + 1) // 2

    def by_z(vals):
        out = jnp.int32(vals[7])
        for i in range(7):
            out = jnp.where(z == i, vals[i], out)
        return out

    far = 1000
    e5_lag = by_z([far, far, far, hop(4), hop(3), hop(2), hop(1), far])
    e4_in = by_z([far, hop(6), hop(5), far, far, HH + hop(2), HH + hop(1), far])
    e4_out = by_z([far, far, hop(5), hop(4), far, far, HH + hop(1), far])
    e3_out = by_z([far, hop(6), far, 0, far, HH + hop(2), far, far])
    d_lag = by_z([hop(7), hop(6), hop(5), hop(4), HH + hop(3), HH + hop(2), 2 * HH + hop(1), 8])
    f7_lag = by_z([far, far, far, far, hop(6), hop(7), hop(8), hop(9)])

    def d_ready(h):
        emsg(0, h).wait_recv()

        @pl.when(z == 2)
        def _():
            ebuf[0, h] = ebuf[0, h] + ebuf[1, h]

    def delta_send(h):
        fbuf[0, h] = chip_grad(3, h, 5) - chip_grad(4, h, 5)
        emsg(0, h).start()

    @pl.when(jnp.logical_not(last_row))
    def _():
        each(f1)

    row_tables()

    @pl.when(last_row)
    def _():
        def own_head(h):
            make_turned(mine + h)
            make_grad(5, mine + h)
            e_send(2)(h)
        each(own_head)
        lax.fori_loop(0, HH, states_first, 0)
        each(lambda h: x1(h).start())
        each(state_mine)
        each(f1)

    @pl.when(jnp.logical_not(last_row))
    def _():
        turned_and_top()

    for j in (4, 3):
        @pl.when(setbits[j])
        def _(j=j):
            all_heads(grad_and_send(j))

        @pl.when(last_row)
        def _(j=j):
            each(e_send(j - 3))

    B0 = 0
    F0 = 0

    def tick(t, carry):
        def stage(fn, lag, cond=None, count=HH):
            h = t - lag
            ok = jnp.logical_and(h >= 0, h < count)
            if cond is not None:
                ok = jnp.logical_and(ok, cond)

            @pl.when(ok)
            def _():
                fn(h)

        @pl.when(t == 2 * zq + 1)
        def _():
            z_tables()

        stage(e_wait(2), B0 + e5_lag)
        stage(e_send(2), B0 + e5_lag, z > 3)
        stage(e_wait(1), B0 + e4_in)
        stage(e_send(1), B0 + e4_out)
        stage(f2, F0)
        stage(f3, F0 + hop(2) - hop(1))
        stage(f4, F0 + hop(3) - hop(1), zb[0])
        stage(f5, F0 + hop(4) - hop(1) + jnp.where(zb[0], hop(5) - hop(4), 0), zb[1])
        stage(f7, f7_lag - hop(1))
        stage(delta_send, B0 + e3_out, z == 3)
        stage(e_send(0), B0 + e3_out, z != 3)
        stage(grads_late, 0, count=H)
        stage(d_ready, B0 + d_lag, in_cond[0])
        stage(a_send, B0 + d_lag)
        stage(flow, B0 + d_lag + 4)
        stage(ya, B0 + d_lag + hop(1))
        stage(yb, B0 + d_lag + hop(2))
        stage(tail_own, B0 + d_lag + hop(2) + 1)
        stage(tail_other, B0 + d_lag + hop(2) + 2)
        stage(lambda i: intra(lax.rem(mine + i, H)), 0, count=H)
        stage(level_own(0), 2, b == 1)
        stage(level_own(1), 3, setbits[1])
        stage(level_own(2), 6, setbits[2])
        stage(level_own(3), 7, setbits[3])
        stage(level_own(4), 12, setbits[4])
        stage(level_own(5), f7_lag - hop(1) + 1, setbits[5])
        stage(level_other(0), 20, b == 1)
        stage(level_other(1), 15, setbits[1])
        stage(level_other(2), 17, setbits[2])
        stage(level_other(3), 13, setbits[3])
        stage(level_other(4), 14, setbits[4])
        stage(level_other(5), f7_lag - hop(1) + 2, setbits[5])
        return carry

    lax.fori_loop(0, B0 + 3 * HH + hop(4), tick, 0)

    da = row_sc[...] - jnp.transpose(col_sc[...])[0:H, :]
    s_i = lax.broadcasted_iota(jnp.int32, (N, N), 0)
    t_i = lax.broadcasted_iota(jnp.int32, (N, N), 1)
    ones = jnp.ones((N, N), F32)

    def dot01(a, m):
        return lax.dot_general(a, m, NN, precision=lax.Precision.HIGHEST, preferred_element_type=F32)

    flux[0] = dot01(da, ones)
    flux[1] = dot01(flow_sc[...], ones)
    for i in range(1, 8):
        rflux(i).start()

    def put(h, carry):
        o_ref[:, cols(h)] = oacc[h].astype(BF16)
        dq_ref[:, cols(h)] = jnp.transpose(dqacc[h]).astype(BF16)
        return carry

    lax.fori_loop(0, H, put, 0)
    after = dot01(da, (s_i >= t_i).astype(F32)) + flux[1]
    for i in range(1, 8):
        rflux(i).wait_recv()
        after = after + rowf[i, 1] + jnp.where(row_from[i] > r, rowf[i, 0], 0.0)
    ddecay_ref[...] = after

    def all_of(src, dst, send, recv):
        return copy(src, dst, send, recv, part)

    half = pl.ds(0, HH)

    def sent(k, buf):
        all_of(buf.at[half], buf.at[half], ssem.at[k], rx1.at[0]).wait_send()

    for j in range(5):
        def late(j=j):
            sent(8 + j, cbuf)
            sent(3 + j, cbuf)
        pl.when(setbits[j + 1])(late)

    @pl.when(b == 0)
    def _():
        sent(1, cbuf)

    @pl.when(b == 1)
    def _():
        sent(2, cbuf)

    sent(0, cbuf)
    for k in (13, 14, 15, 22, 23):
        sent(k, cbuf)
    for j in range(3):
        def zsent(j=j):
            sent(16 + j, cbuf)
        pl.when(in_cond[j])(zsent)
        def esent(j=j):
            sent(19 + j, cbuf)
        pl.when(zb[j])(esent)
    for i in range(1, 8):
        rtot(i).wait_send()
        rflux(i).wait_send()

    @pl.when(zq < 3)
    def _():
        ztot().wait_send()


def fused(q, k, v, g, gain, decay):
    vm = pl.BlockSpec(memory_space=pltpu.VMEM)
    sg = lambda *lead: pltpu.VMEM(lead + (N, N), F32)
    sh = lambda *lead: pltpu.VMEM(lead + (N, N), BF16)
    tv = lambda *lead: pltpu.VMEM(lead + (H, N), F32)
    dma = pltpu.SemaphoreType.DMA
    wide_out = jax.ShapeDtypeStruct((N, H * N), BF16)
    return pl.pallas_call(
        fused_kernel,
        in_specs=[pl.BlockSpec(memory_space=pltpu.MemorySpace.HBM)] * 6,
        out_specs=[vm] * 6,
        out_shape=[wide_out, wide_out, wide_out, wide_out,
                   jax.ShapeDtypeStruct((LVL_IN + XLEV, H, N), F32),
                   jax.ShapeDtypeStruct((H, N), F32)],
        scratch_shapes=[sg(H), sg(XLEV, H), sg(H), sg(XLEV - 1, H), sg(H), sg(H), sg(H), sg(H), sg(H),
                        sh(H), sh(H), sh(H),
                        sg(6, HH), sg(HH), sg(HH), sg(HH), sg(HH), sg(HH),
                        sg(3, HH), sg(3, HH), sg(HH), sg(HH), sg(3, HH), sg(HH),
                        tv(10), tv(8), tv(2), tv(8, 2), tv(XLEV), tv(2), tv(), tv(), tv(), tv(2), tv(), sg(),
                        dma((24,)), dma((HH,)), dma((HH,)), dma((6, HH)), dma((5, HH)), dma((HH,)),
                        dma((HH,)), dma((HH,)), dma((3, HH)), dma((3, HH)), dma((HH,)), dma((HH,))]
                       + [dma((8,))] * 6
                       + [pltpu.VMEM((N, H * N), BF16)] * 4
                       + [tv(LVL_IN + XLEV), tv(), dma((6,))],
        compiler_params=pltpu.CompilerParams(collective_id=0, has_side_effects=True,
                                             vmem_limit_bytes=44 * 1024 * 1024),
        name="fused",
    )(*(pltpu.with_memory_space_constraint(a, pltpu.MemorySpace.HBM) for a in (q, k, v, g, gain, decay)))


def finish_kernel(*refs):
    ins, outs, sem = refs[:6], refs[6:12], refs[12]
    for i in range(6):
        pltpu.make_async_copy(ins[i], outs[i], sem.at[i]).start()
    for i in range(6):
        pltpu.make_async_copy(ins[i], outs[i], sem.at[i]).wait()


def finish(*arrays):
    return pl.pallas_call(
        finish_kernel,
        in_specs=[pl.BlockSpec(memory_space=pltpu.VMEM)] * 6,
        out_specs=[pl.BlockSpec(memory_space=pl.ANY)] * 6,
        out_shape=[jax.ShapeDtypeStruct(a.shape, a.dtype) for a in arrays],
        scratch_shapes=[pltpu.SemaphoreType.DMA((6,))],
        compiler_params=pltpu.CompilerParams(vmem_limit_bytes=8 * 1024 * 1024),
        name="finish",
    )(*arrays)


def per_device(queries, keys_in, value_input, level_gain, decay_log, out_grad):
    return tuple(finish(*fused(queries, keys_in, value_input, out_grad, level_gain, decay_log)))


def solution(mesh):
    tokens = P(("seq", "ctx"), None)
    gains = P(None, None, ("seq", "ctx"))
    decays = P(None, ("seq", "ctx"))
    return jax.shard_map(
        per_device,
        mesh=mesh,
        in_specs=(tokens, tokens, tokens, gains, decays, tokens),
        out_specs=(tokens, tokens, tokens, tokens, gains, decays),
        check_vma=False,
    )
```

```python
import jax
import jax.numpy as jnp
from jax import lax
from jax.experimental import pallas as pl
from jax.experimental.pallas import tpu as pltpu
from jax.sharding import PartitionSpec as P

MESH = pl.DeviceIdType.MESH
F32 = jnp.float32
BF16 = jnp.bfloat16
H = 16
HH = 8
N = 128
LVL_IN = 8
XLEV = 6

NN = (((1,), (0,)), ((), ()))
NT = (((1,), (1,)), ((), ()))


def mm(a, b, dims=NN):
    return lax.dot_general(a, b, dims, preferred_element_type=F32)


def split(x):
    hi = x.astype(BF16)
    lo = (x - hi.astype(F32)).astype(BF16)
    return hi, lo


def wide(x):
    hi, lo = split(x)
    return jnp.concatenate([hi, lo], axis=1)


def tall(x):
    hi, lo = split(x)
    return jnp.concatenate([hi, lo], axis=0)


def flip(x):
    return jnp.transpose(x.astype(F32)).astype(BF16)


def running_sums(decay):
    r = lax.broadcasted_iota(jnp.int32, (N, N), 0)
    t = lax.broadcasted_iota(jnp.int32, (N, N), 1)
    upper = (r <= t).astype(F32)
    run = lax.dot_general(decay, upper, NN, precision=lax.Precision.HIGHEST, preferred_element_type=F32)
    tot = lax.dot_general(decay, jnp.ones((N, N), F32), NN, precision=lax.Precision.HIGHEST, preferred_element_type=F32)
    return run, tot


def coords():
    c = lax.axis_index("ctx")
    return c, lax.rem(c, 2), lax.rem(c // 2, 4), c // 8


def pick(parts, cond):
    acc = jnp.zeros((H, N), F32)
    for i in range(8):
        acc = acc + jnp.where(cond(i), parts[i], 0.0)
    return acc


def fused_kernel(q_in, k_in, v_in, g_in, gain_in, decay_in,
                 o_ref, dq_ref, dk_ref, dv_ref, dgain_ref, ddecay_ref,
                 st, g_st, b0, bk, ds, oacc, dqacc, dkacc, dvacc, qt_sc, kt_sc, gt_sc,
                 rg, cbuf, mbuf, rbuf, pbuf, qbuf, ebuf, fbuf, abuf, bbuf, ybuf, xbuf,
                 tt, rowt, zt, rowf, off, rsum, own, run_sc, row_sc, flux, flow_sc, col_sc,
                 ssem, rx1, rx1b, rx2, rx4, rx5, ry1, ry2, rz, re, ra, rb,
                 trs, trr, tzs, tzr, frs, frr,
                 q_ref, k_ref, v_ref, g_ref, gain_ref, decay_ref, insem):
    seq = lax.axis_index("seq")
    c, b, y, z = coords()
    r = lax.rem(c, 8)
    mine = b * HH
    theirs = (1 - b) * HH
    part = c + 1 - 2 * b
    yn = c + 2 - 4 * lax.rem(y, 2)
    ym = c + 2 * (3 - 2 * y)
    up = c + 8
    dn = c - 8
    yodd = lax.rem(y, 2) == 1
    yhi = y >= 2
    zb = [lax.rem(z, 2) == 1, lax.rem(z // 2, 2) == 1, z >= 4]
    row_peer = [z * 8 + lax.rem(r + i, 8) for i in range(8)]
    row_from = [lax.rem(r - i + 8, 8) for i in range(8)]

    loads = [pltpu.make_async_copy(src, dst, insem.at[i]) for i, (src, dst) in enumerate((
        (decay_in, decay_ref), (k_in, k_ref), (v_in, v_ref), (q_in, q_ref), (g_in, g_ref), (gain_in, gain_ref)))]
    for load in loads:
        load.start()
    barrier = pltpu.get_barrier_semaphore()
    for i in range(1, 8):
        pl.semaphore_signal(barrier, inc=1, device_id=(seq, row_peer[i]), device_id_type=MESH)

    @pl.when(z < 7)
    def _():
        pl.semaphore_signal(barrier, inc=1, device_id=(seq, up), device_id_type=MESH)

    @pl.when(z > 0)
    def _():
        pl.semaphore_signal(barrier, inc=1, device_id=(seq, dn), device_id_type=MESH)

    loads[0].wait()
    run, tot = running_sums(decay_ref[...])
    run_sc[...] = run
    own[...] = tot
    dgain_ref[...] = jnp.zeros((LVL_IN + XLEV, H, N), F32)
    col_sc[...] = jnp.zeros((N, N), F32)
    flow_sc[...] = jnp.zeros((H, N), F32)

    def cols(h):
        return pl.ds(pl.multiple_of(h * N, N), N)

    def row(ref, h):
        return ref[pl.ds(h, 1), :]

    def make_state(h):
        kt = jnp.transpose(k_ref[:, cols(h)].astype(F32))
        kt_sc[h] = kt.astype(BF16)
        v = v_ref[:, cols(h)]
        st[h] = mm(wide(kt * jnp.exp(row(own, h) - row(run_sc, h))), jnp.concatenate([v, v], axis=0))

    def states_first(h, carry):
        make_state(theirs + h)
        return carry

    loads[1].wait()
    loads[2].wait()
    last_row = z == 7

    @pl.when(jnp.logical_not(last_row))
    def _():
        lax.fori_loop(0, HH, states_first, 0)

    pl.semaphore_wait(barrier, 7 + jnp.minimum(z, 1) + jnp.minimum(7 - z, 1))

    def copy(src, dst, send, recv, who):
        return pltpu.make_async_remote_copy(src_ref=src, dst_ref=dst, send_sem=send, recv_sem=recv,
                                            device_id=(seq, who), device_id_type=MESH)

    def x1(h):
        return copy(st.at[theirs + h], b0.at[theirs + h], ssem.at[0], rx1.at[h], part)

    def x1b(h):
        return copy(st.at[h], b0.at[h], ssem.at[1], rx1b.at[h], part)

    def x2(j, h):
        return copy(g_st.at[j, theirs + h], rg.at[j, h], ssem.at[2 + j], rx2.at[j, h], part)

    def x4(j, h):
        return copy(bk.at[j, mine + h], bk.at[j, mine + h], ssem.at[8 + j], rx4.at[j, h], part)

    def x5(h):
        return copy(xbuf.at[h], ds.at[mine + h], ssem.at[13], rx5.at[h], part)

    def y1(h):
        return copy(cbuf.at[h], bk.at[0, mine + h], ssem.at[14], ry1.at[h], yn)

    def y2(h):
        return copy(mbuf.at[h], bk.at[1, mine + h], ssem.at[15], ry2.at[h], ym)

    def zmsg(j, src, h):
        return copy(src, bk.at[2 + j, mine + h], ssem.at[16 + j], rz.at[j, h], up)

    def emsg(j, h):
        return copy(fbuf.at[j, h], ebuf.at[j, h], ssem.at[19 + j], re.at[j, h], dn)

    def amsg(h):
        return copy(abuf.at[h], ybuf.at[0, h], ssem.at[22], ra.at[h], ym)

    def bmsg(h):
        return copy(bbuf.at[h], ybuf.at[1, h], ssem.at[23], rb.at[h], yn)

    def rtot(i):
        return copy(own, rowt.at[i], trs.at[i], trr.at[i], z * 8 + lax.rem(r + i, 8))

    def ztot():
        return copy(rsum, zt, tzs.at[0], tzr.at[0], up)

    def rflux(i):
        return copy(flux, rowf.at[i], frs.at[i], frr.at[i], row_peer[i])

    setbits = [None, yodd, yhi, zb[0], zb[1], zb[2]]

    def each(fn):
        def body(h, carry):
            fn(h)
            return carry
        lax.fori_loop(0, HH, body, 0)

    rtot(jnp.where(b == 0, 1, 7)).start()

    @pl.when(jnp.logical_not(last_row))
    def _():
        each(lambda h: x1(h).start())

    rtot(jnp.where(b == 0, 7, 1)).start()
    for i in range(2, 7):
        rtot(i).start()

    def make_turned(h):
        qt_sc[h] = flip(q_ref[:, cols(h)])
        gt_sc[h] = flip(g_ref[:, cols(h)])

    def make_grad(j, h):
        g = g_ref[:, cols(h)]
        scale = gain_ref[LVL_IN + j, pl.ds(h, 1), :] * jnp.exp(row(run_sc, h))
        g_st[j, h] = mm(wide(qt_sc[h].astype(F32) * scale), jnp.concatenate([g, g], axis=0))

    def state_mine(h):
        make_state(mine + h)

        @pl.when(b == 0)
        def _():
            x1b(h).start()

    @pl.when(jnp.logical_not(last_row))
    def _():
        each(state_mine)

    for load in loads[3:]:
        load.wait()

    def all_heads(fn):
        def body(i, carry):
            fn(i)
            return carry
        lax.fori_loop(0, H, body, 0)

    def grad_and_send(j):
        def go(i):
            h = lax.rem(theirs + i, H)
            make_grad(j, h)

            @pl.when(i < HH)
            def _():
                x2(j, i).start()
        return go

    def turned_and_top():
        all_heads(make_turned)

        @pl.when(setbits[5])
        def _():
            all_heads(grad_and_send(5))

    @pl.when(last_row)
    def _():
        def partner_head(h):
            make_turned(theirs + h)
            grad_and_send(5)(h)
        each(partner_head)


    @pl.when(z == 7)
    def _():
        def zero(h):
            ebuf[2, h] = jnp.zeros((N, N), F32)
        each(zero)

    pair_slot = jnp.where(b == 0, 7, 1)
    rtot(pair_slot).wait_recv()
    tt[0] = jnp.where(b == 0, own[...], rowt[pair_slot])
    tt[1] = jnp.where(b == 0, rowt[pair_slot], own[...])

    def row_tables():
        rtot(8 - pair_slot).wait_recv()
        for i in range(2, 7):
            rtot(i).wait_recv()
        parts = [own[...]] + [rowt[i] for i in range(1, 8)]
        rows = pick(parts, lambda i: row_from[i] >= 0)
        rsum[1] = rows
        tt[2] = pick(parts, lambda i: row_from[i] // 2 == 2 * (y // 2) + 1)
        tt[3] = pick(parts, lambda i: row_from[i] >= 4)
        tt[4] = rows
        tt[5] = pick(parts, lambda i: row_from[i] < 2 * y)
        tt[6] = pick(parts, lambda i: jnp.logical_and(row_from[i] >= 4, row_from[i] < 2 * y))
        tt[7] = jnp.zeros((H, N), F32)
        off[0] = jnp.zeros((H, N), F32)
        off[1] = jnp.where(b == 1, tt[0], 0.0)
        off[2] = pick(parts, lambda i: jnp.logical_and(row_from[i] >= 4 * (y // 2), row_from[i] < r))
        off[3] = pick(parts, lambda i: row_from[i] < r)

    zq = lax.rem(z, 4)

    def z_tables():
        @pl.when(zq == 0)
        def _():
            zt[...] = jnp.zeros((2, H, N), F32)

        @pl.when(zq > 0)
        def _():
            ztot().wait_recv()

        below, last = zt[0], zt[1]
        tt[8] = tt[4] + last
        tt[9] = tt[4] + below
        off[4] = off[3] + jnp.where(zb[0], last, 0.0)
        off[5] = off[3] + below
        rsum[0] = tt[4] + below

        @pl.when(zq < 3)
        def _():
            ztot().start()

    def tb(k, h):
        return tt[k, pl.ds(mine + h, 1), :]

    def merge(out, low, high, k, h):
        out[...] = jnp.exp(tb(k, h)) * low[...] + high[...]

    def f1(h):
        x1(h).wait_recv()

        @pl.when(b == 0)
        def _():
            merge(cbuf.at[h], st.at[mine + h], b0.at[mine + h], 1, h)

        @pl.when(b == 1)
        def _():
            merge(cbuf.at[h], b0.at[mine + h], st.at[mine + h], 1, h)

        y1(h).start()

    def f2(h):
        y1(h).wait_recv()
        other = bk.at[0, mine + h]

        @pl.when(yodd)
        def _():
            merge(mbuf.at[h], other, cbuf.at[h], 2, h)
            x4(0, h).start()

        @pl.when(jnp.logical_not(yodd))
        def _():
            merge(mbuf.at[h], cbuf.at[h], other, 2, h)

        y2(h).start()

    def f3(h):
        y2(h).wait_recv()
        other = bk.at[1, mine + h]

        @pl.when(yhi)
        def _():
            merge(rbuf.at[h], other, mbuf.at[h], 3, h)
            x4(1, h).start()

        @pl.when(jnp.logical_not(yhi))
        def _():
            merge(rbuf.at[h], mbuf.at[h], other, 3, h)

        @pl.when(jnp.logical_not(zb[0]))
        def _():
            zmsg(0, rbuf.at[h], h).start()

    def f4(h):
        zmsg(0, rbuf.at[h], h).wait_recv()
        x4(2, h).start()
        merge(pbuf.at[h], bk.at[2, mine + h], rbuf.at[h], 4, h)

        @pl.when(jnp.logical_not(zb[1]))
        def _():
            zmsg(1, pbuf.at[h], h).start()

    def f5(h):
        here = bk.at[3, mine + h]
        zmsg(1, here, h).wait_recv()

        @pl.when(jnp.logical_not(zb[0]))
        def _():
            zmsg(1, here, h).start()

        x4(3, h).start()

        @pl.when(z == 3)
        def _():
            merge(qbuf.at[h], here, pbuf.at[h], 8, h)
            zmsg(2, qbuf.at[h], h).start()

    def f7(h):
        here = bk.at[4, mine + h]
        zmsg(2, here, h).wait_recv()

        @pl.when(z < 7)
        def _():
            zmsg(2, here, h).start()

        x4(4, h).start()

    def chip_grad(j, h, k, wait=True):
        if wait:
            x2(j, h).wait_recv()
        e0 = jnp.exp(tb(0, h))
        off = jnp.exp(tb(k, h))
        low = jnp.where(b == 0, off, e0 * off)
        high = jnp.where(b == 0, e0 * off, off)
        return low * g_st[j, mine + h] + high * rg[j, h]

    in_slot = [jnp.where(zb[1], 2, 1), jnp.where(zb[0], 2, 1), 2]
    d_slot = jnp.where(zb[0], jnp.where(zb[1], 2, 1), 0)
    in_cond = [jnp.logical_not(zb[0]), zb[0] != zb[1], jnp.logical_and(z >= 3, z < 7)]

    def e_send(j):
        def go(h):
            if j == 1:
                @pl.when(z != 3)
                def _():
                    x2(4, h).wait_recv()
            else:
                x2(3 + j, h).wait_recv()
            fbuf[j, h] = jnp.exp(tb(4, h)) * ebuf[in_slot[j], h] + chip_grad(3 + j, h, 5, False)
            emsg(j, h).start()
        return go

    def e_wait(j):
        return lambda h: emsg(j, h).wait_recv()

    def a_send(h):
        @pl.when(yhi)
        def _():
            abuf[h] = jnp.exp(tb(3, h)) * ebuf[d_slot, h] + chip_grad(2, h, 6)

        @pl.when(jnp.logical_not(yhi))
        def _():
            abuf[h] = ebuf[d_slot, h]

        amsg(h).start()

    def ya(h):
        amsg(h).wait_recv()
        e23 = jnp.where(yhi, 1.0, jnp.exp(tb(3, h)))
        yv = e23 * ebuf[d_slot, h] + ybuf[0, h]
        ybuf[2, h] = yv

        @pl.when(yodd)
        def _():
            bbuf[h] = jnp.exp(tb(2, h)) * yv + chip_grad(1, h, 7)

        @pl.when(jnp.logical_not(yodd))
        def _():
            bbuf[h] = yv

        bmsg(h).start()

    def yb(h):
        bmsg(h).wait_recv()
        e1 = jnp.where(yodd, 1.0, jnp.exp(tb(2, h)))
        dc = e1 * ybuf[2, h] + ybuf[1, h]

        @pl.when(b == 0)
        def _():
            x2(0, h).wait_recv()
            ds[mine + h] = jnp.exp(tb(1, h)) * dc + rg[0, h]
            xbuf[h] = dc

        @pl.when(b == 1)
        def _():
            ds[mine + h] = dc
            xbuf[h] = jnp.exp(tb(1, h)) * dc + g_st[0, mine + h]

        x5(h).start()

    def intra(h):
        run_h = row(run_sc, h)
        run_col = jnp.transpose(jnp.broadcast_to(run_h, (N, N)))
        q, k, v, g = (x[:, cols(h)] for x in (q_ref, k_ref, v_ref, g_ref))
        qt, gt, kt = qt_sc[h], gt_sc[h], kt_sc[h]
        vt = flip(v)
        s_i = lax.broadcasted_iota(jnp.int32, (N, N), 0)
        t_i = lax.broadcasted_iota(jnp.int32, (N, N), 1)
        causal = s_i <= t_i
        mixing = jnp.bitwise_xor(s_i, t_i)
        fade = jnp.where(causal, jnp.exp(jnp.where(causal, run_h - run_col, 0.0)), 0.0)
        weight = jnp.broadcast_to(gain_ref[0, pl.ds(h, 1), :], (N, N))
        for lev in range(1, LVL_IN):
            weight = jnp.where(mixing >= (1 << (lev - 1)), gain_ref[lev, pl.ds(h, 1), :], weight)
        sc = mm(k, qt)
        gv = mm(v, gt)
        wd = weight * fade
        wt = sc * wd
        xt = gv * wd
        pair = sc * gv * fade
        above = [jnp.sum(pair, axis=0, keepdims=True)]
        for lev in range(1, LVL_IN):
            above.append(jnp.sum(jnp.where(mixing >= (1 << (lev - 1)), pair, 0.0), axis=0, keepdims=True))
        above.append(jnp.zeros((1, N), F32))
        for lev in range(LVL_IN):
            dgain_ref[lev, pl.ds(h, 1), :] = above[lev] - above[lev + 1]
        oacc[h] = jnp.transpose(mm(jnp.concatenate([vt, vt], axis=1), tall(wt)))
        dqt = mm(jnp.concatenate([kt, kt], axis=1), tall(xt))
        dqacc[h] = dqt
        row_sc[pl.ds(h, 1), :] = jnp.sum(dqt * qt.astype(F32), axis=0, keepdims=True)
        dvacc[h] = mm(wide(wt), jnp.concatenate([g, g], axis=0))
        dkacc[h] = mm(wide(xt), jnp.concatenate([q, q], axis=0))

    def level(j, h):
        lift = jnp.exp(row(run_sc, h) + off[j, pl.ds(h, 1), :])
        scale = gain_ref[LVL_IN + j, pl.ds(h, 1), :] * lift
        q = q_ref[:, cols(h)]
        gt = gt_sc[h]
        m_hi, m_lo = split(b0[h] if j == 0 else bk[j - 1, h])
        part_o = mm(jnp.concatenate([q, q], axis=1), jnp.concatenate([m_hi, m_lo], axis=0))
        oacc[h] = oacc[h] + jnp.transpose(jnp.broadcast_to(scale, (N, N))) * part_o
        dt = mm(jnp.concatenate([m_hi, m_lo], axis=1), jnp.concatenate([gt, gt], axis=0))
        dqacc[h] = dqacc[h] + scale * dt
        sums = jnp.sum(dt * qt_sc[h].astype(F32), axis=0, keepdims=True)
        dgain_ref[LVL_IN + j, pl.ds(h, 1), :] = lift * sums
        row_sc[pl.ds(h, 1), :] = row_sc[pl.ds(h, 1), :] + scale * sums

    def level_own(j):
        return lambda h: level(j, mine + h)

    def level_other(j):
        def go(h):
            if j == 0:
                x1b(h).wait_recv()
            else:
                copy(bk.at[j - 1, theirs + h], bk.at[j - 1, theirs + h], ssem.at[7 + j], rx4.at[j - 1, h],
                     part).wait_recv()
            level(j, theirs + h)
        return go

    def tail_terms(h):
        tail = jnp.transpose(jnp.broadcast_to(jnp.exp(row(own, h) - row(run_sc, h)), (N, N)))
        k, v = k_ref[:, cols(h)], v_ref[:, cols(h)]
        d_hi, d_lo = split(ds[h])
        dv = dvacc[h] + tail * mm(jnp.concatenate([k, k], axis=1), jnp.concatenate([d_hi, d_lo], axis=0))
        dk = dkacc[h] + tail * mm(jnp.concatenate([v, v], axis=1), jnp.concatenate([d_hi, d_lo], axis=1), NT)
        dk_ref[:, cols(h)] = dk.astype(BF16)
        dv_ref[:, cols(h)] = dv.astype(BF16)
        t_i = lax.broadcasted_iota(jnp.int32, (N, N), 1)
        col_sc[...] = jnp.where(t_i == h, jnp.sum(v.astype(F32) * dv, axis=1, keepdims=True), col_sc[...])

    def flow(h):
        acc = main_state(h) * ebuf[d_slot, h]
        flow_sc[pl.ds(mine + h, 1), :] = jnp.sum(acc, axis=0, keepdims=True)

        def more(j, k):
            term = jnp.sum(bk[j, mine + h] * ebuf[j - 2, h], axis=0, keepdims=True)
            flow_sc[pl.ds(mine + h, 1), :] = flow_sc[pl.ds(mine + h, 1), :] + jnp.exp(tb(k, h)) * term

        @pl.when(jnp.logical_and(zb[1], jnp.logical_not(zb[0])))
        def _():
            more(3, 4)

        @pl.when(jnp.logical_and(z > 3, z < 7))
        def _():
            more(4, 9)

    def main_state(h):
        upper = jnp.where(z == 3, qbuf[h], pbuf[h])
        return jnp.where(zb[0], upper, rbuf[h])

    def tail_own(h):
        tail_terms(mine + h)

    def tail_other(h):
        copy(ds.at[theirs + h], ds.at[theirs + h], ssem.at[13], rx5.at[h], part).wait_recv()
        tail_terms(theirs + h)

    def grads_late(i):
        h = lax.rem(theirs + i, H)
        for j in (2, 1, 0):
            @pl.when(b == 1 if j == 0 else setbits[j])
            def _(j=j):
                make_grad(j, h)

                @pl.when(i < HH)
                def _():
                    x2(j, i).start()

    def hop(n):
        return (5 * n + 1) // 2

    def by_z(vals):
        out = jnp.int32(vals[7])
        for i in range(7):
            out = jnp.where(z == i, vals[i], out)
        return out

    far = 1000
    e5_lag = by_z([far, far, far, hop(4), hop(3), hop(2), hop(1), far])
    e4_in = by_z([far, hop(6), hop(5), far, far, HH + hop(2), HH + hop(1), far])
    e4_out = by_z([far, far, hop(5), hop(4), far, far, HH + hop(1), far])
    e3_out = by_z([far, hop(6), far, 0, far, HH + hop(2), far, far])
    d_lag = by_z([hop(7), hop(6), hop(5), hop(4), HH + hop(3), HH + hop(2), 2 * HH + hop(1), 8])
    f7_lag = by_z([far, far, far, far, hop(6), hop(7), hop(8), hop(9)])

    def d_ready(h):
        emsg(0, h).wait_recv()

        @pl.when(z == 2)
        def _():
            ebuf[0, h] = ebuf[0, h] + ebuf[1, h]

    def delta_send(h):
        fbuf[0, h] = chip_grad(3, h, 5) - chip_grad(4, h, 5)
        emsg(0, h).start()

    @pl.when(jnp.logical_not(last_row))
    def _():
        each(f1)

    row_tables()

    @pl.when(last_row)
    def _():
        def own_head(h):
            make_turned(mine + h)
            make_grad(5, mine + h)
            e_send(2)(h)
        each(own_head)
        lax.fori_loop(0, HH, states_first, 0)
        each(lambda h: x1(h).start())
        each(state_mine)
        each(f1)

    @pl.when(jnp.logical_not(last_row))
    def _():
        turned_and_top()

    for j in (4, 3):
        @pl.when(setbits[j])
        def _(j=j):
            all_heads(grad_and_send(j))

        @pl.when(last_row)
        def _(j=j):
            each(e_send(j - 3))

    B0 = 0
    F0 = 0

    def tick(t, carry):
        def stage(fn, lag, cond=None, count=HH):
            h = t - lag
            ok = jnp.logical_and(h >= 0, h < count)
            if cond is not None:
                ok = jnp.logical_and(ok, cond)

            @pl.when(ok)
            def _():
                fn(h)

        @pl.when(t == 2 * zq + 1)
        def _():
            z_tables()

        stage(e_wait(2), B0 + e5_lag)
        stage(e_send(2), B0 + e5_lag, z > 3)
        stage(e_wait(1), B0 + e4_in)
        stage(e_send(1), B0 + e4_out)
        stage(f2, F0)
        stage(f3, F0 + hop(2) - hop(1))
        stage(f4, F0 + hop(3) - hop(1), zb[0])
        stage(f5, F0 + hop(4) - hop(1) + jnp.where(zb[0], hop(5) - hop(4), 0), zb[1])
        stage(f7, f7_lag - hop(1))
        stage(delta_send, B0 + e3_out, z == 3)
        stage(e_send(0), B0 + e3_out, z != 3)
        stage(grads_late, 0, count=H)
        stage(d_ready, B0 + d_lag, in_cond[0])
        stage(a_send, B0 + d_lag)
        stage(flow, B0 + d_lag + 4)
        stage(ya, B0 + d_lag + hop(1))
        stage(yb, B0 + d_lag + hop(2))
        stage(tail_own, B0 + d_lag + hop(2) + 1)
        stage(tail_other, B0 + d_lag + hop(2) + 2)
        stage(lambda i: intra(lax.rem(mine + i, H)), 0, count=H)
        stage(level_own(0), 2, b == 1)
        stage(level_own(1), 3, setbits[1])
        stage(level_own(2), 6, setbits[2])
        stage(level_own(3), 7, setbits[3])
        stage(level_own(4), 12, setbits[4])
        stage(level_own(5), f7_lag - hop(1) + 1, setbits[5])
        stage(level_other(0), 20, b == 1)
        stage(level_other(1), 19, setbits[1])
        stage(level_other(2), 21, setbits[2])
        stage(level_other(3), 18, setbits[3])
        stage(level_other(4), 16, setbits[4])
        stage(level_other(5), f7_lag - hop(1) + 2, setbits[5])
        return carry

    lax.fori_loop(0, B0 + 3 * HH + hop(4), tick, 0)

    da = row_sc[...] - jnp.transpose(col_sc[...])[0:H, :]
    s_i = lax.broadcasted_iota(jnp.int32, (N, N), 0)
    t_i = lax.broadcasted_iota(jnp.int32, (N, N), 1)
    ones = jnp.ones((N, N), F32)

    def dot01(a, m):
        return lax.dot_general(a, m, NN, precision=lax.Precision.HIGHEST, preferred_element_type=F32)

    flux[0] = da
    flux[1] = flow_sc[...]
    for i in range(1, 8):
        rflux(i).start()

    def put(h, carry):
        o_ref[:, cols(h)] = oacc[h].astype(BF16)
        dq_ref[:, cols(h)] = jnp.transpose(dqacc[h]).astype(BF16)
        return carry

    lax.fori_loop(0, H, put, 0)
    inside = dot01(da, (s_i >= t_i).astype(F32))
    after = flux[1]
    for i in range(1, 8):
        rflux(i).wait_recv()
        after = after + rowf[i, 1] + jnp.where(row_from[i] > r, rowf[i, 0], 0.0)
    ddecay_ref[...] = inside + dot01(after, ones)

    def all_of(src, dst, send, recv):
        return copy(src, dst, send, recv, part)

    half = pl.ds(0, HH)

    def sent(k, buf):
        all_of(buf.at[half], buf.at[half], ssem.at[k], rx1.at[0]).wait_send()

    for j in range(5):
        def late(j=j):
            sent(8 + j, cbuf)
            sent(3 + j, cbuf)
        pl.when(setbits[j + 1])(late)

    @pl.when(b == 0)
    def _():
        sent(1, cbuf)

    @pl.when(b == 1)
    def _():
        sent(2, cbuf)

    sent(0, cbuf)
    for k in (13, 14, 15, 22, 23):
        sent(k, cbuf)
    for j in range(3):
        def zsent(j=j):
            sent(16 + j, cbuf)
        pl.when(in_cond[j])(zsent)
        def esent(j=j):
            sent(19 + j, cbuf)
        pl.when(zb[j])(esent)
    for i in range(1, 8):
        rtot(i).wait_send()
        rflux(i).wait_send()

    @pl.when(zq < 3)
    def _():
        ztot().wait_send()


def fused(q, k, v, g, gain, decay):
    vm = pl.BlockSpec(memory_space=pltpu.VMEM)
    sg = lambda *lead: pltpu.VMEM(lead + (N, N), F32)
    sh = lambda *lead: pltpu.VMEM(lead + (N, N), BF16)
    tv = lambda *lead: pltpu.VMEM(lead + (H, N), F32)
    dma = pltpu.SemaphoreType.DMA
    wide_out = jax.ShapeDtypeStruct((N, H * N), BF16)
    return pl.pallas_call(
        fused_kernel,
        in_specs=[pl.BlockSpec(memory_space=pltpu.MemorySpace.HBM)] * 6,
        out_specs=[vm] * 6,
        out_shape=[wide_out, wide_out, wide_out, wide_out,
                   jax.ShapeDtypeStruct((LVL_IN + XLEV, H, N), F32),
                   jax.ShapeDtypeStruct((H, N), F32)],
        scratch_shapes=[sg(H), sg(XLEV, H), sg(H), sg(XLEV - 1, H), sg(H), sg(H), sg(H), sg(H), sg(H),
                        sh(H), sh(H), sh(H),
                        sg(6, HH), sg(HH), sg(HH), sg(HH), sg(HH), sg(HH),
                        sg(3, HH), sg(3, HH), sg(HH), sg(HH), sg(3, HH), sg(HH),
                        tv(10), tv(8), tv(2), tv(8, 2), tv(XLEV), tv(2), tv(), tv(), tv(), tv(2), tv(), sg(),
                        dma((24,)), dma((HH,)), dma((HH,)), dma((6, HH)), dma((5, HH)), dma((HH,)),
                        dma((HH,)), dma((HH,)), dma((3, HH)), dma((3, HH)), dma((HH,)), dma((HH,))]
                       + [dma((8,))] * 6
                       + [pltpu.VMEM((N, H * N), BF16)] * 4
                       + [tv(LVL_IN + XLEV), tv(), dma((6,))],
        compiler_params=pltpu.CompilerParams(collective_id=0, has_side_effects=True,
                                             vmem_limit_bytes=44 * 1024 * 1024),
        name="fused",
    )(*(pltpu.with_memory_space_constraint(a, pltpu.MemorySpace.HBM) for a in (q, k, v, g, gain, decay)))


def finish_kernel(*refs):
    ins, outs, sem = refs[:6], refs[6:12], refs[12]
    for i in range(6):
        pltpu.make_async_copy(ins[i], outs[i], sem.at[i]).start()
    for i in range(6):
        pltpu.make_async_copy(ins[i], outs[i], sem.at[i]).wait()


def finish(*arrays):
    return pl.pallas_call(
        finish_kernel,
        in_specs=[pl.BlockSpec(memory_space=pltpu.VMEM)] * 6,
        out_specs=[pl.BlockSpec(memory_space=pl.ANY)] * 6,
        out_shape=[jax.ShapeDtypeStruct(a.shape, a.dtype) for a in arrays],
        scratch_shapes=[pltpu.SemaphoreType.DMA((6,))],
        compiler_params=pltpu.CompilerParams(vmem_limit_bytes=8 * 1024 * 1024),
        name="finish",
    )(*arrays)


def per_device(queries, keys_in, value_input, level_gain, decay_log, out_grad):
    return tuple(finish(*fused(queries, keys_in, value_input, out_grad, level_gain, decay_log)))


def solution(mesh):
    tokens = P(("seq", "ctx"), None)
    gains = P(None, None, ("seq", "ctx"))
    decays = P(None, ("seq", "ctx"))
    return jax.shard_map(
        per_device,
        mesh=mesh,
        in_specs=(tokens, tokens, tokens, gains, decays, tokens),
        out_specs=(tokens, tokens, tokens, tokens, gains, decays),
        check_vma=False,
    )
```
